32 devices in a mesh: inline: 8 (over z, y), xline: 4 (over x, core).
Axes of the slice: x: 2, y: 2, z: 4, core: 2. Of those that a mesh axis runs over, the one named last changes fastest.
Arguments:
- samples: float32 [2, 8, 4096], P(None, 'inline', 'xline'), may hold values from -6 to 6
Outputs:
- values: float32 [2, 8192], P(None, ('inline', 'xline'))
The draws below stay inside these ranges and needn't reach their ends.
All inputs are finite; a program needn't handle non-finite values.
Results may differ from the reference program's by a relative error of at most 0.0003.
Values sent between devices are 32-bit elements; how exact they have to be, the bound alone decides.
A program may use at most 64 MiB of HBM per device.

```python
import math
import jax
import jax.numpy as jnp
from jax import lax

GI = 1
GC = 4
NF = 256
COLS = 256
NI = 8
NCF = 4096
N_INLINE = 8
N_XLINE = 4


def level_of(rng, dims, cuts, low, largest):
    loudness, own = 1.0, jax.random.fold_in(rng, 6)
    for dim, blocks in cuts:
        draws = jnp.exp(jax.random.uniform(jax.random.fold_in(own, dim), (blocks,), jnp.float32, low / len(cuts), largest / len(cuts)))
        loudness = loudness * jnp.repeat(draws, dims[dim] // blocks).reshape([-1 if axis == dim else 1 for axis in range(len(dims))])
    return loudness


def scatter_about(own_key, dims, scale, most, shards=(), held_as=jnp.bfloat16):
    values = jax.random.normal(own_key, dims, jnp.float32) * scale
    if len(shards) > 0:
        values = level_of(own_key, dims, shards, -0.22, 0.18) * values
    return jnp.clip(values, min=-most, max=most).astype(held_as)


def setup_inputs(seed: int = 0) -> dict:
    keys = jax.random.split(jax.random.key(seed), 2)
    samples = scatter_about(keys[0], (2, NI, NCF), 1.0, 6.0, ((1, 8), (2, 4)), jnp.float32)
    return {"samples": samples}


KAPPA = 40.0
HIGH = lax.Precision.HIGHEST

def cheb_nodes():
    node_order = jnp.arange(5, dtype=jnp.float32)
    return 0.5 * jnp.cos(node_order * (math.pi / 4.0))

def lagrange(points):
    node_list = cheb_nodes()
    basis_rows = []
    for node_index in range(5):
        factor = jnp.ones_like(points)
        for other_node in range(5):
            if other_node != node_index:
                factor = factor * (points - node_list[other_node]) / (node_list[node_index] - node_list[other_node])
        basis_rows.append(factor)
    return jnp.stack(basis_rows)

def box_points(inline_low, inline_width, xline_low, xline_width):
    shifted = cheb_nodes() + 0.5
    grid_shape = (5, 5, 5)
    along_inline = jnp.broadcast_to((inline_low + inline_width * shifted)[:, None, None], grid_shape).reshape(125)
    along_xline = jnp.broadcast_to((xline_low + xline_width * shifted)[None, :, None], grid_shape).reshape(125)
    frequency = jnp.broadcast_to(shifted[None, None, :], grid_shape).reshape(125)
    return (along_inline, along_xline, frequency)

def traveltime(points, centers):
    offset_inline, offset_xline, frequency = points
    anchor = 0.5 + centers[0][None, :]
    radicand = anchor * anchor + centers[1][None, :] * (offset_inline * offset_inline)[:, None]
    radicand = radicand + centers[2][None, :] * (offset_xline * offset_xline)[:, None]
    return KAPPA * (0.5 + frequency)[:, None] * jnp.sqrt(radicand)

def finish(summed, parent_span, centers):
    phase_angle = traveltime(box_points(parent_span[0], parent_span[1], parent_span[2], parent_span[3]), centers)
    cosine = jnp.cos(phase_angle)
    sine_vals = jnp.sin(phase_angle)
    return jnp.stack([summed[0] * cosine + summed[1] * sine_vals, summed[1] * cosine - summed[0] * sine_vals])

def child_term(weights, child_side, axis_pick, parent_span, children):
    inline_low, inline_width, xline_low, xline_width = parent_span
    if axis_pick == 0:
        phase_angle = traveltime(box_points(inline_low + 0.5 * inline_width * child_side, 0.5 * inline_width, xline_low, xline_width), children)
    else:
        phase_angle = traveltime(box_points(inline_low, inline_width, xline_low + 0.5 * xline_width * child_side, 0.5 * xline_width), children)
    cosine = jnp.cos(phase_angle)
    sine_vals = jnp.sin(phase_angle)
    real_in = jnp.concatenate([weights[0], weights[0]], axis=1)
    imag_in = jnp.concatenate([weights[1], weights[1]], axis=1)
    stacked = jnp.stack([cosine * real_in - sine_vals * imag_in, sine_vals * real_in + cosine * imag_in])
    stacked = stacked.reshape(2, 5, 5, 5, -1)
    matrix = lagrange((child_side - 0.5) * 0.5 + 0.5 * cheb_nodes())
    if axis_pick == 0:
        mixed = jnp.einsum('ab,rbcdn->racdn', matrix, stacked, precision=HIGH)
    else:
        mixed = jnp.einsum('ab,rcbdn->rcadn', matrix, stacked, precision=HIGH)
    return mixed.reshape(2, 125, -1)

def parent_box(inline_pos, xline_pos, inline_count, xline_count, merged, axis_pick):
    inline_bits = merged[0] + (1 if axis_pick == 0 else 0)
    xline_bits = merged[1] + (1 if axis_pick == 1 else 0)
    inline_low = (inline_pos >> inline_bits << inline_bits).astype(jnp.float32) / inline_count
    xline_low = (xline_pos >> xline_bits << xline_bits).astype(jnp.float32) / xline_count
    return (inline_low, 2.0 ** inline_bits / inline_count, xline_low, 2.0 ** xline_bits / xline_count)

def roster(inline_count, xline_count):
    inline_bits = inline_count.bit_length() - 1
    xline_bits = xline_count.bit_length() - 1
    level_plan = []
    for level_num in range(max(inline_bits, xline_bits)):
        if level_num < inline_bits:
            level_plan.append((0, level_num))
        if level_num < xline_bits:
            level_plan.append((1, level_num))
    return level_plan

def split_counts(column_count):
    tree_depth = (column_count - 1).bit_length()
    return (tree_depth, [len([depth_step for depth_step in range(tree_depth) if depth_step % 3 == axis_num]) for axis_num in range(3)])

def initial_centers(column_count):
    tree_depth = (column_count - 1).bit_length()
    column = jnp.arange(column_count, dtype=jnp.int32)
    coords = []
    for axis_num in range(3):
        splits = [depth_step for depth_step in range(tree_depth) if depth_step % 3 == axis_num]
        coord = jnp.full((column_count,), 0.5 * 0.5 ** len(splits), jnp.float32)
        for split_rank, depth_step in enumerate(splits):
            digit = column >> tree_depth - 1 - depth_step & 1
            coord = coord + digit.astype(jnp.float32) * 0.5 ** (split_rank + 1)
        coords.append(coord)
    return jnp.stack(coords)

def split_targets(centers, split_dim, span_width):
    offsets = [0.0, 0.0, 0.0]
    offsets[split_dim] = 0.25 * span_width
    shift_col = jnp.array(offsets, dtype=jnp.float32)[:, None]
    return jnp.concatenate([centers - shift_col, centers + shift_col], axis=1)

def leaf_weights(flat_samples, inline_pos, xline_pos, inline_count, xline_count, centers, count_inline, count_xline, freq_count):
    z_inline = (jnp.arange(count_inline, dtype=jnp.float32) + 0.5) / count_inline - 0.5
    z_xline = (jnp.arange(count_xline, dtype=jnp.float32) + 0.5) / count_xline - 0.5
    z_freq = (jnp.arange(freq_count, dtype=jnp.float32) + 0.5) / freq_count - 0.5
    basis_rest = jnp.einsum('bc,df->bdcf', lagrange(z_xline), lagrange(z_freq), precision=HIGH).reshape(25, -1)
    inline_basis = lagrange(z_inline).T
    inline_low = inline_pos.astype(jnp.float32) / inline_count
    xline_low = xline_pos.astype(jnp.float32) / xline_count
    grid_shape = (count_xline, freq_count)
    sample_xline = jnp.broadcast_to((xline_low + (z_xline + 0.5) / xline_count)[:, None], grid_shape).reshape(-1)
    sample_freq = jnp.broadcast_to((z_freq + 0.5)[None, :], grid_shape).reshape(-1)
    row_samples = flat_samples.reshape(2, count_inline, -1).transpose(1, 0, 2)
    row_inline = inline_low + (z_inline + 0.5) / inline_count
    column_count = centers.shape[1]

    def add_row(total, items):
        row_pair, inline_coord, row_basis = items
        coord_vec = jnp.zeros_like(sample_freq) + inline_coord
        phase_angle = traveltime((coord_vec, sample_xline, sample_freq), centers)
        cosine = jnp.cos(phase_angle)
        sine_vals = jnp.sin(phase_angle)
        real_in = row_pair[0][:, None]
        imag_in = row_pair[1][:, None]
        real_part = jnp.dot(basis_rest, cosine * real_in - sine_vals * imag_in, precision=HIGH)
        imag_part = jnp.dot(basis_rest, sine_vals * real_in + cosine * imag_in, precision=HIGH)
        pair = jnp.stack([real_part, imag_part])
        spread = row_basis[None, :, None, None] * pair[:, None, :, :]
        return (total + spread.reshape(2, 125, column_count), None)
    start_total = jnp.zeros((2, 125, column_count), dtype=jnp.float32)
    summed, unused = lax.scan(add_row, start_total, (row_samples, row_inline, inline_basis))
    leaf_span = (inline_low, 1.0 / inline_count, xline_low, 1.0 / xline_count)
    return finish(summed, leaf_span, centers)

def reference(samples):
    inline_count = N_INLINE
    xline_count = N_XLINE
    devices = inline_count * xline_count
    flat_samples = samples.reshape(2, inline_count, GI, xline_count, GC * NF)
    flat_samples = flat_samples.transpose(1, 3, 0, 2, 4).reshape(devices, 2, GI * GC * NF)
    device_ids = jnp.arange(devices, dtype=jnp.int32)
    inline_index = device_ids // xline_count
    xline_index = device_ids % xline_count
    start_centers = initial_centers(COLS)

    def leaf_one(items):
        return leaf_weights(items[0], items[1], items[2], inline_count, xline_count, start_centers, GI, GC, NF)
    weights = lax.map(leaf_one, (flat_samples, inline_index, xline_index))
    centers = jnp.broadcast_to(start_centers[None], (devices, 3, COLS))
    tree_depth, counts = split_counts(COLS)
    half_cols = COLS // 2
    merged = [0, 0]
    level_plan = roster(inline_count, xline_count)
    for position, (axis_pick, bit_place) in enumerate(level_plan):
        split_dim = tree_depth % 3
        span_width = 0.5 ** counts[split_dim]
        is_last = position == len(level_plan) - 1
        shift_bits = bit_place + (xline_count.bit_length() - 1 if axis_pick == 0 else 0)
        partner = device_ids ^ 1 << shift_bits
        axis_index = inline_index if axis_pick == 0 else xline_index
        own_bits = axis_index >> bit_place & 1
        partner_weights = jnp.take(weights, partner, axis=0)
        merged_now = list(merged)

        def level_one(own_weights, far_weights, own_centers, own_bit, inline_pos, xline_pos):
            keep_start = (own_bit * half_cols).astype(jnp.int32)
            parent_span = parent_box(inline_pos, xline_pos, inline_count, xline_count, merged_now, axis_pick)
            children = split_targets(lax.dynamic_slice_in_dim(own_centers, keep_start, half_cols, 1), split_dim, span_width)
            own_child = own_bit.astype(jnp.float32)
            own_term = child_term(lax.dynamic_slice_in_dim(own_weights, keep_start, half_cols, 2), own_child, axis_pick, parent_span, children)
            far_term = child_term(lax.dynamic_slice_in_dim(far_weights, keep_start, half_cols, 2), 1.0 - own_child, axis_pick, parent_span, children)
            summed = own_term + far_term
            if is_last:
                return (lax.optimization_barrier(jnp.sum(summed, axis=1)), children)
            return (finish(summed, parent_span, children), children)
        weights, centers = jax.vmap(level_one)(weights, partner_weights, centers, own_bits, inline_index, xline_index)
        merged[axis_pick] += 1
        counts[split_dim] += 1
        tree_depth += 1
    sample_norm = 1.0 / math.sqrt(GI * GC * NF * devices)
    return weights.transpose(1, 0, 2).reshape(2, devices * COLS) * sample_norm
```

```python
import functools
import math

import jax
import jax.numpy as jnp
import numpy as np
from jax import lax
from jax.experimental import pallas as pl
from jax.experimental.pallas import tpu as pltpu
from jax.sharding import PartitionSpec as P

NF = 256
COLS = 256
KAPPA = 40.0
SPLIT = 8
GATHERED = 2
SCATTERED = 3
MESH = pl.DeviceIdType.MESH

NODES = np.array([0.5, 0.5 * math.sqrt(0.5), 0.0, -0.5 * math.sqrt(0.5), -0.5])


def lagrange(points):
    points = np.asarray(points, np.float64)
    rows = []
    for k in range(5):
        factor = np.ones_like(points)
        for j in range(5):
            if j != k:
                factor = factor * (points - NODES[j]) / (NODES[k] - NODES[j])
        rows.append(factor)
    table = np.stack(rows)
    return np.where(np.abs(table) < 1e-13, 0.0, table)


MIX = [lagrange((t - 0.5) / 2 + NODES / 2) for t in range(2)]


def roster(inline_count, xline_count):
    inline_bits = inline_count.bit_length() - 1
    xline_bits = xline_count.bit_length() - 1
    plan = []
    for level in range(max(inline_bits, xline_bits)):
        if level < inline_bits:
            plan.append((0, level))
        if level < xline_bits:
            plan.append((1, level))
    return plan


def split_counts():
    depth = (COLS - 1).bit_length()
    return depth, [len([j for j in range(depth) if j % 3 == axis]) for axis in range(3)]


def initial_centers(column):
    depth, _ = split_counts()
    coords = []
    for axis in range(3):
        splits = [j for j in range(depth) if j % 3 == axis]
        coord = jnp.full(column.shape, 0.5 * 0.5 ** len(splits), jnp.float32)
        for rank, j in enumerate(splits):
            digit = (column >> (depth - 1 - j)) & 1
            coord = coord + digit.astype(jnp.float32) * 0.5 ** (rank + 1)
        coords.append(coord)
    return coords


def poly(square, terms):
    total = jnp.full(square.shape, terms[-1], jnp.float32)
    for term in reversed(terms[:-1]):
        total = total * square + term
    return total


def series(limit):
    both = []
    for odd in (1, 0):
        terms = []
        while not terms or limit ** (2 * len(terms) + odd) / math.factorial(2 * len(terms) + odd) > 1e-7:
            terms.append((-1.0) ** len(terms) / math.factorial(2 * len(terms) + odd))
        both.append(terms)
    return both


def root_of(square):
    return square * lax.rsqrt(square)


def parts_of(value):
    high = value.astype(jnp.bfloat16)
    return high, (value - high.astype(jnp.float32)).astype(jnp.bfloat16)


def product(left, right):
    return jnp.dot(left, right, preferred_element_type=jnp.float32)


def small_sincos(angle, limit):
    sine, cosine = series(limit)
    square = angle * angle
    return angle * poly(square, sine), poly(square, cosine)


def turn_sincos(turns):
    half = (turns - jnp.round(turns)) * math.pi
    s, c = small_sincos(half, math.pi / 2)
    return 2.0 * s * c, 1.0 - 2.0 * s * s


def rotors(before, after, reach):
    gap = root_of(after) - root_of(before)
    cs, cc = small_sincos(gap * (0.5 * KAPPA), 0.5 * KAPPA * reach)
    bs, bc = small_sincos(gap * (NODES[1] * KAPPA), NODES[1] * KAPPA * reach)
    twice = cs + cs
    a_s, a_c = twice * cc, 1.0 - twice * cs
    p, q, u, v = a_c * bc, a_s * bs, a_s * bc, a_c * bs
    return [
        (a_c * cc - a_s * cs, a_s * cc + a_c * cs),
        (p - q, u + v),
        (a_c, a_s),
        (p + q, u - v),
        (cc, cs),
    ]


def side_points(low, width):
    return [low + width * (z + 0.5) for z in NODES]


def radicands(centers, xi, xc):
    anchor = 0.5 + centers[0]
    first = [anchor * anchor + centers[1] * (x * x) for x in xi]
    second = [centers[2] * (x * x) for x in xc]
    return lambda i, j: first[i] + second[j]


def shifted(centers, axis, amount):
    return [c + amount if k == axis else c for k, c in enumerate(centers)]


def leaf_sums(samples_ref, arrive, store, inline_pos, xline_pos, inline_count, xline_count):
    cx = samples_ref.shape[2] // NF
    fine = NF // SPLIT
    column = lax.broadcasted_iota(jnp.int32, (1, COLS), 1)
    centers = initial_centers(column)
    row = lax.broadcasted_iota(jnp.int32, (fine + SPLIT, COLS), 0).astype(jnp.float32)
    weight = jnp.where(row < fine, 0.5 + (row + 0.5) / NF, (row - fine) * (fine / NF))
    lane = lax.broadcasted_iota(jnp.int32, (SPLIT, NF), 1)
    block = lax.broadcasted_iota(jnp.int32, (SPLIT, NF), 0)
    mask = lane // fine == block
    pick = (
        lax.broadcasted_iota(jnp.int32, (NF, fine), 0) % fine
        == lax.broadcasted_iota(jnp.int32, (NF, fine), 1)
    ).astype(jnp.bfloat16)
    spot = lax.broadcasted_iota(jnp.int32, (SPLIT, fine), 0) * fine
    spot = spot + lax.broadcasted_iota(jnp.int32, (SPLIT, fine), 1)
    z = (spot.astype(jnp.float32) + 0.5) / NF - 0.5
    basis = []
    for k in range(5):
        factor = None
        for j in range(5):
            if j != k:
                term = (z - NODES[j]) * (1.0 / (NODES[k] - NODES[j]))
                factor = term if factor is None else factor * term
        basis.append(factor)
    x0 = (inline_pos + 0.5) / inline_count
    tables = []
    for c in range(cx):
        x1 = (xline_pos + (c + 0.5) / cx) / xline_count
        anchor = 0.5 + centers[0]
        root = root_of(anchor * anchor + centers[1] * (x0 * x0) + centers[2] * (x1 * x1))
        tables.append(turn_sincos(weight * (root * (KAPPA / (2 * math.pi)))))
    arrive()
    pieces = []
    for c in range(cx):
        for part in range(2):
            line = samples_ref[part, :, c * NF : (c + 1) * NF]
            pieces.append(jnp.where(mask, line, 0.0))
    high, low = parts_of(jnp.concatenate(pieces, axis=0))
    spread = product(high, pick) + product(low, pick)
    for c in range(cx):
        sine, cosine = tables[c]
        span = 5 * SPLIT
        left = [
            spread[(2 * c + part) * SPLIT : (2 * c + part + 1) * SPLIT] * table
            for part in range(2)
            for table in basis
        ]
        lh, ll = parts_of(jnp.concatenate(left, axis=0))
        sh, sl = parts_of(sine[:fine])
        ch, cl = parts_of(cosine[:fine])
        by_cos = product(lh, ch) + (product(lh, cl) + product(ll, ch))
        by_sin = product(lh, sh) + (product(lh, sl) + product(ll, sh))
        re = by_cos[:span] - by_sin[span:]
        im = by_sin[:span] + by_cos[span:]
        hs, hc = sine[fine:], cosine[fine:]
        rows = [[], []]
        for k in range(5):
            r, i = re[k * SPLIT : (k + 1) * SPLIT], im[k * SPLIT : (k + 1) * SPLIT]
            rows[0].append(jnp.sum(r * hc - i * hs, axis=0, keepdims=True))
            rows[1].append(jnp.sum(i * hc + r * hs, axis=0, keepdims=True))
        for part in range(2):
            store((part * cx + c) * 5, jnp.concatenate(rows[part], axis=0))


def wait_all(ref, sem):
    pltpu.make_async_copy(ref, ref, sem).wait()


def leaf_rows(cx):
    return -(-10 * cx // 8) * 8


def kernel(
    counts,
    scattered,
    samples_hbm,
    out_ref,
    samples_ref,
    fetch_sem,
    state,
    first_spin,
    spin,
    leaf_out,
    leaf_in,
    part_out,
    part_in,
    gather_send,
    gather_recv,
    scatter_send,
    scatter_recv,
    swap_out=None,
    swap_in=None,
    swap_send=None,
    swap_recv=None,
):
    fetch = pltpu.make_async_copy(samples_hbm, samples_ref, fetch_sem)
    fetch.start()
    cx = samples_ref.shape[2] // NF
    pitch = leaf_rows(cx)
    index = (lax.axis_index("inline"), lax.axis_index("xline"))
    plan = roster(*counts)
    middle = plan[GATHERED : len(plan) - scattered]
    final = plan[len(plan) - scattered :]
    bits = [(index[axis] >> place) & 1 for axis, place in plan]
    size = [c * 1.0 for c in counts]

    def other(flips):
        target = list(index)
        for axis, place in flips:
            target[axis] = target[axis] ^ (1 << place)
        return tuple(target)

    def subsets(levels):
        return [
            [level for k, level in enumerate(levels) if pattern >> k & 1]
            for pattern in range(1, 1 << len(levels))
        ]

    near = subsets(plan[:GATHERED])
    far = [[plan[1]] + flips for flips in [[]] + subsets(final)][::-1]
    calls = near + [f for f in far if f not in near] + [[level] for level in middle]
    partners = [other(f) for f in calls]
    barrier = pltpu.get_barrier_semaphore()
    for partner in partners:
        pl.semaphore_signal(barrier, inc=1, device_id=partner, device_id_type=MESH)

    half = COLS // 2
    own_slot = bits[0] * 2 + bits[1]
    own_row = own_slot * pitch

    def keep(row, value):
        for side in range(2):
            leaf_out[side * pitch + row : side * pitch + row + 5, :] = value[
                :, side * half : (side + 1) * half
            ]

    position = [i.astype(jnp.float32) for i in index]
    leaf_sums(samples_ref, fetch.wait, keep, position[0], position[1], size[0], size[1])
    mine = pl.multiple_of(bits[0] * pitch, 8)
    leaf_in[pl.ds(pl.multiple_of(own_row, 8), pitch), :] = leaf_out[pl.ds(mine, pitch), :]

    pl.semaphore_wait(barrier, len(partners))
    for flips in near:
        wanted = bits[0] ^ (1 if plan[0] in flips else 0)
        copy = pltpu.make_async_remote_copy(
            src_ref=leaf_out.at[pl.ds(pl.multiple_of(wanted * pitch, 8), pitch), :],
            dst_ref=leaf_in.at[pl.ds(pl.multiple_of(own_row, 8), pitch), :],
            send_sem=gather_send,
            recv_sem=gather_recv,
            device_id=other(flips),
            device_id_type=MESH,
        )
        copy.start()

    sub = lax.broadcasted_iota(jnp.int32, (8, half), 0)
    flag = [((sub >> k) & 1) == 1 for k in range(3)]
    sign = [jnp.where(f, 1.0, -1.0) for f in flag]
    depth, splits = split_counts()
    merged = [0, 0]

    def advance():
        nonlocal depth
        axis = depth % 3
        quarter = 0.25 * 0.5 ** splits[axis]
        splits[axis] += 1
        depth += 1
        return axis, quarter

    def box(axis):
        width = 2.0 ** merged[axis] / size[axis]
        low = ((index[axis] >> merged[axis]) << merged[axis]).astype(jnp.float32) / size[axis]
        return low, width

    def parent_low(axis):
        up = merged[axis] + 1
        return ((index[axis] >> up) << up).astype(jnp.float32) / size[axis]

    def prepare(slot, centers, children, xi, xc, reach):
        old, new = radicands(centers, xi, xc), radicands(children, xi, xc)
        for i in range(5):
            for j in range(5):
                for k, (c, s) in enumerate(rotors(old(i, j), new(i, j), reach)):
                    row = (i * 5 + j) * 5 + k
                    spin[slot, 0, row], spin[slot, 1, row] = c, s

    def turn(slot):
        for row in range(125):
            re, im = state[0, row], state[1, row]
            c, s = spin[slot, 0, row], spin[slot, 1, row]
            state[0, row] = re * c - im * s
            state[1, row] = re * s + im * c

    def mix(axis, choose, finish):
        used = [
            [(b, choose(a, b)) for b in range(5) if MIX[0][a, b] != 0.0 or MIX[1][a, b] != 0.0]
            for a in range(5)
        ]
        for part in range(2):
            for o in range(5):
                for k in range(5):
                    place = [
                        ((a * 5 + o) if axis == 0 else (o * 5 + a)) * 5 + k for a in range(5)
                    ]
                    values = [state[part, r] for r in place]
                    for a in range(5):
                        total = None
                        for b, coefficient in used[a]:
                            term = values[b] * coefficient
                            total = term if total is None else total + term
                        state[part, place[a]] = finish(total)

    column = lax.broadcasted_iota(jnp.int32, (8, half), 1) + bits[0] * half
    centers = initial_centers(column)

    axis, quarter = advance()
    children = shifted(centers, axis, (1.0 - 2.0 * bits[1].astype(jnp.float32)) * quarter)
    low0, width0 = parent_low(0), 1.0 / size[0]
    low1, width1 = parent_low(1), 1.0 / size[1]
    xc = side_points(low1 + jnp.where(flag[2], width1, 0.0), width1)
    for t in range(2):
        x = [low0 + width0 * (t + 0.5)]
        old, new = radicands(centers, x, xc), radicands(children, x, xc)
        for j in range(5):
            for k, (c, s) in enumerate(rotors(old(0, j), new(0, j), quarter)):
                row = (j * 2 + t) * 5 + k
                first_spin[0, row], first_spin[1, row] = c, s
    merged[0] += 1
    centers = children

    def pair_geometry(level_axis, centers):
        axis, quarter = advance()
        children = shifted(centers, axis, sign[1] * quarter)
        spans = []
        for k in range(2):
            low, width = box(k)
            if k == level_axis:
                low = parent_low(k) + jnp.where(flag[2], width, 0.0)
            spans.append(side_points(low, width))
        merged[level_axis] += 1
        return (centers, children, spans[0], spans[1], quarter), axis

    geometry, axis = pair_geometry(plan[1][0], centers)
    prepare(0, *geometry)
    later = []
    for k, level in enumerate(middle):
        side = 2.0 * bits[GATHERED + k].astype(jnp.float32) - 1.0
        centers = shifted(geometry[0], axis, side * geometry[4])
        geometry, axis = pair_geometry(level[0], centers)
        later.append(geometry)
    spot = [1, 2, 0]
    centers = geometry[1]
    for k, level in enumerate(final):
        axis, quarter = advance()
        low0, width0 = box(0)
        low1, width1 = box(1)
        xi, xc = side_points(low0, width0), side_points(low1, width1)
        if k < scattered - 1:
            children = shifted(centers, axis, sign[spot[k + 1]] * quarter)
            prepare(1 + k, centers, children, xi, xc, quarter)
            centers = children
        else:
            for side in range(2):
                children = shifted(centers, axis, (2.0 * side - 1.0) * quarter)
                prepare(1 + k + side, centers, children, xi, xc, quarter)
        merged[level[0]] += 1

    wait_all(leaf_in.at[pl.ds(0, len(near) * pitch), :], gather_recv)
    across = lagrange((np.arange(cx) + 0.5) / cx - 0.5)
    for k in range(5):
        sums = [[], []]
        for t in range(2):
            for part in range(2):
                values = []
                for c in range(cx):
                    row = (part * cx + c) * 5 + k
                    lines = [
                        jnp.broadcast_to(leaf_in[pl.ds((2 * t + q) * pitch + row, 1), :], (8, half))
                        for q in range(2)
                    ]
                    values.append(jnp.where(flag[2], lines[1], lines[0]))
                for j in range(5):
                    total = values[0] * across[j, 0]
                    for c in range(1, cx):
                        total = total + values[c] * across[j, c]
                    sums[part].append(total)
        for j in range(5):
            turned = []
            for t in range(2):
                re, im = sums[0][t * 5 + j], sums[1][t * 5 + j]
                row = (j * 2 + t) * 5 + k
                c, s = first_spin[0, row], first_spin[1, row]
                turned.append((re * c - im * s, re * s + im * c))
            for i in range(5):
                for part in range(2):
                    state[part, (i * 5 + j) * 5 + k] = (
                        turned[0][part] * MIX[0][i, 2] + turned[1][part] * MIX[1][i, 2]
                    )

    def joined(level_axis):
        turn(0)
        mix(
            level_axis,
            lambda a, b: jnp.where(flag[2], MIX[1][a, b], MIX[0][a, b]).astype(jnp.float32),
            lambda x: x + pltpu.roll(x, 4, 0),
        )

    joined(plan[1][0])

    for k, level in enumerate(middle):
        bit = bits[GATHERED + k]

        def pack(r, carry):
            mine = pl.ds(bit * 2, 1)
            theirs = pl.ds((1 - bit) * 2, 1)
            for part in range(2):
                line = pl.ds(part * 125 + r, 1)
                swap_out[k, line, :] = state[part, r, theirs, :]
                swap_in[2 * k + 1, line, :] = state[part, r, mine, :]
            return carry

        lax.fori_loop(0, 125, pack, 0)
        copy = pltpu.make_async_remote_copy(
            src_ref=swap_out.at[k],
            dst_ref=swap_in.at[2 * k],
            send_sem=swap_send.at[k],
            recv_sem=swap_recv.at[k],
            device_id=other([level]),
            device_id_type=MESH,
        )
        copy.start()
        prepare(0, *later[k])
        copy.wait()
        own_high = (sub >> 2) == bit

        def unpack(r, carry):
            for part in range(2):
                line = pl.ds(part * 125 + r, 1)
                near_line = jnp.broadcast_to(swap_in[2 * k + 1, line, :], (8, half))
                far_line = jnp.broadcast_to(swap_in[2 * k, line, :], (8, half))
                state[part, r] = jnp.where(own_high, near_line, far_line)
            return carry

        lax.fori_loop(0, 125, unpack, 0)
        joined(level[0])

    for k, level in enumerate(final[:-1]):
        turn(1 + k)
        side = bits[len(plan) - scattered + k].astype(jnp.float32)
        mix(
            level[0],
            lambda a, b: (1.0 - side) * MIX[0][a, b] + side * MIX[1][a, b],
            lambda x: x,
        )

    sums = [[None, None], [None, None]]
    for row in range(125):
        re, im = state[0, row], state[1, row]
        for side in range(2):
            c, s = spin[scattered + side, 0, row], spin[scattered + side, 1, row]
            for part, term in enumerate((re * c - im * s, re * s + im * c)):
                held = sums[part][side]
                sums[part][side] = term if held is None else held + term
    for part in range(2):
        for side in range(2):
            part_out[pl.ds(part * 2 + side, 8, stride=8), :] = sums[part][side]

    def place_of(flips):
        total = 0
        for k, level in enumerate(final):
            bit = bits[len(plan) - scattered + k] ^ (1 if level in flips else 0)
            total = total + bit * (1 << spot[k])
        return pl.multiple_of(total * 8, 8)

    for k, flips in enumerate(far):
        copy = pltpu.make_async_remote_copy(
            src_ref=part_out.at[pl.ds(place_of(flips), 8), :],
            dst_ref=part_in.at[k],
            send_sem=scatter_send,
            recv_sem=scatter_recv,
            device_id=other(flips),
            device_id_type=MESH,
        )
        copy.start()
    wait_all(leaf_in.at[pl.ds(0, len(near) * pitch), :], gather_send)
    wait_all(part_in, scatter_recv)
    total = part_in[0]
    for k in range(1, len(far)):
        total = total + part_in[k]
    wait_all(part_in, scatter_send)
    for part in range(2):
        for side in range(2):
            line = part * 2 + side
            out_ref[part : part + 1, side * half : (side + 1) * half] = total[line : line + 1, :]


def shards(samples):
    counts = (lax.axis_size("inline"), lax.axis_size("xline"))
    plan = roster(*counts)
    scattered = SCATTERED
    middle = len(plan) - GATHERED - scattered
    if middle < 0 or samples.shape[1] != 1 or plan[:2] != [(0, 0), (1, 0)]:
        raise ValueError("unsupported mesh")
    half = COLS // 2
    pitch = leaf_rows(samples.shape[2] // NF)
    swaps = [
        pltpu.VMEM((middle, 256, half), jnp.float32),
        pltpu.VMEM((2 * middle, 256, half), jnp.float32),
        pltpu.SemaphoreType.DMA((middle,)),
        pltpu.SemaphoreType.DMA((middle,)),
    ]
    norm = 1.0 / math.sqrt(samples.shape[1] * samples.shape[2] * counts[0] * counts[1])
    values = pl.pallas_call(
        functools.partial(kernel, counts, scattered),
        out_shape=jax.ShapeDtypeStruct((2, COLS), jnp.float32),
        in_specs=[pl.BlockSpec(memory_space=pltpu.HBM)],
        out_specs=pl.BlockSpec(memory_space=pltpu.VMEM),
        scratch_shapes=[
            pltpu.VMEM(samples.shape, jnp.float32),
            pltpu.SemaphoreType.DMA,
            pltpu.VMEM((2, 125, 8, half), jnp.float32),
            pltpu.VMEM((2, 50, 8, half), jnp.float32),
            pltpu.VMEM((scattered + 2, 2, 125, 8, half), jnp.float32),
            pltpu.VMEM((2 * pitch, half), jnp.float32),
            pltpu.VMEM((4 * pitch, half), jnp.float32),
            pltpu.VMEM((64, half), jnp.float32),
            pltpu.VMEM((1 << scattered, 8, half), jnp.float32),
            *[pltpu.SemaphoreType.DMA] * 4,
            *(swaps if middle else []),
        ],
        compiler_params=pltpu.CompilerParams(
            collective_id=0, has_side_effects=True, vmem_limit_bytes=20 << 20
        ),
    )(pltpu.with_memory_space_constraint(samples, pltpu.HBM))
    return values * norm


def solution(mesh):
    return jax.shard_map(
        shards,
        mesh=mesh,
        in_specs=(P(None, "inline", "xline"),),
        out_specs=P(None, ("inline", "xline")),
        check_vma=False,
    )
```

```python
import functools
import math

import jax
import jax.numpy as jnp
import numpy as np
from jax import lax
from jax.experimental import pallas as pl
from jax.experimental.pallas import tpu as pltpu
from jax.sharding import PartitionSpec as P

NF = 256
COLS = 256
KAPPA = 40.0
SPLIT = 8
GATHERED = 2
SCATTERED = 3
MESH = pl.DeviceIdType.MESH
PAIRS = [(0, 4), (1, 3), (2, 2)]

NODES = np.array([0.5, 0.5 * math.sqrt(0.5), 0.0, -0.5 * math.sqrt(0.5), -0.5])


def lagrange(points):
    points = np.asarray(points, np.float64)
    rows = []
    for k in range(5):
        factor = np.ones_like(points)
        for j in range(5):
            if j != k:
                factor = factor * (points - NODES[j]) / (NODES[k] - NODES[j])
        rows.append(factor)
    table = np.stack(rows)
    return np.where(np.abs(table) < 1e-13, 0.0, table)


MIX = [lagrange((t - 0.5) / 2 + NODES / 2) for t in range(2)]


def roster(inline_count, xline_count):
    inline_bits = inline_count.bit_length() - 1
    xline_bits = xline_count.bit_length() - 1
    plan = []
    for level in range(max(inline_bits, xline_bits)):
        if level < inline_bits:
            plan.append((0, level))
        if level < xline_bits:
            plan.append((1, level))
    return plan


def split_counts():
    depth = (COLS - 1).bit_length()
    return depth, [len([j for j in range(depth) if j % 3 == axis]) for axis in range(3)]


def initial_centers(column):
    depth, _ = split_counts()
    coords = []
    for axis in range(3):
        splits = [j for j in range(depth) if j % 3 == axis]
        coord = jnp.full(column.shape, 0.5 * 0.5 ** len(splits), jnp.float32)
        for rank, j in enumerate(splits):
            digit = (column >> (depth - 1 - j)) & 1
            coord = coord + digit.astype(jnp.float32) * 0.5 ** (rank + 1)
        coords.append(coord)
    return coords


def poly(square, terms):
    total = jnp.full(square.shape, terms[-1], jnp.float32)
    for term in reversed(terms[:-1]):
        total = total * square + term
    return total


def series(limit):
    both = []
    for odd in (1, 0):
        terms = []
        while not terms or limit ** (2 * len(terms) + odd) / math.factorial(2 * len(terms) + odd) > 1e-7:
            terms.append((-1.0) ** len(terms) / math.factorial(2 * len(terms) + odd))
        both.append(terms)
    return both


def root_of(square):
    return square * lax.rsqrt(square)


def parts_of(value):
    high = value.astype(jnp.bfloat16)
    return high, (value - high.astype(jnp.float32)).astype(jnp.bfloat16)


def product(left, right):
    return jnp.dot(left, right, preferred_element_type=jnp.float32)


def small_sincos(angle, limit):
    sine, cosine = series(limit)
    square = angle * angle
    return angle * poly(square, sine), poly(square, cosine)


def turn_sincos(turns):
    half = (turns - jnp.round(turns)) * math.pi
    s, c = small_sincos(half, math.pi / 2)
    return 2.0 * s * c, 1.0 - 2.0 * s * s


def base_rotors(before, after, reach):
    gap = root_of(after) - root_of(before)
    cs, cc = small_sincos(gap * (0.5 * KAPPA), 0.5 * KAPPA * reach)
    bs, bc = small_sincos(gap * (NODES[1] * KAPPA), NODES[1] * KAPPA * reach)
    twice = cs + cs
    return (cc, cs), (bc, bs), (1.0 - twice * cs, twice * cc)


def rotors(before, after, reach):
    (cc, cs), (bc, bs), (a_c, a_s) = base_rotors(before, after, reach)
    p, q, u, v = a_c * bc, a_s * bs, a_s * bc, a_c * bs
    return [
        (a_c * cc - a_s * cs, a_s * cc + a_c * cs),
        (p - q, u + v),
        (a_c, a_s),
        (p + q, u - v),
        (cc, cs),
    ]


def pair_rotors(before, after, reach, sign):
    (cc, cs), (bc, bs), (a_c, a_s) = base_rotors(before, after, reach)
    cs, bs = cs * sign, bs * sign
    return [
        (a_c * cc - a_s * cs, a_s * cc + a_c * cs),
        (a_c * bc - a_s * bs, a_s * bc + a_c * bs),
        (a_c, a_s),
    ]


def side_points(low, width):
    return [low + width * (z + 0.5) for z in NODES]


def radicands(centers, xi, xc):
    anchor = 0.5 + centers[0]
    first = [anchor * anchor + centers[1] * (x * x) for x in xi]
    second = [centers[2] * (x * x) for x in xc]
    return lambda i, j: first[i] + second[j]


def shifted(centers, axis, amount):
    return [c + amount if k == axis else c for k, c in enumerate(centers)]


def leaf_sums(samples_ref, arrive, store, inline_pos, xline_pos, inline_count, xline_count):
    cx = samples_ref.shape[2] // NF
    fine = NF // SPLIT
    column = lax.broadcasted_iota(jnp.int32, (1, COLS), 1)
    centers = initial_centers(column)
    row = lax.broadcasted_iota(jnp.int32, (fine + SPLIT, COLS), 0).astype(jnp.float32)
    weight = jnp.where(row < fine, 0.5 + (row + 0.5) / NF, (row - fine) * (fine / NF))
    lane = lax.broadcasted_iota(jnp.int32, (SPLIT, NF), 1)
    block = lax.broadcasted_iota(jnp.int32, (SPLIT, NF), 0)
    mask = lane // fine == block
    pick = (
        lax.broadcasted_iota(jnp.int32, (NF, fine), 0) % fine
        == lax.broadcasted_iota(jnp.int32, (NF, fine), 1)
    ).astype(jnp.bfloat16)
    spot = lax.broadcasted_iota(jnp.int32, (SPLIT, fine), 0) * fine
    spot = spot + lax.broadcasted_iota(jnp.int32, (SPLIT, fine), 1)
    z = (spot.astype(jnp.float32) + 0.5) / NF - 0.5
    basis = []
    for k in range(5):
        factor = None
        for j in range(5):
            if j != k:
                term = (z - NODES[j]) * (1.0 / (NODES[k] - NODES[j]))
                factor = term if factor is None else factor * term
        basis.append(factor)
    x0 = (inline_pos + 0.5) / inline_count
    tables = []
    for c in range(cx):
        x1 = (xline_pos + (c + 0.5) / cx) / xline_count
        anchor = 0.5 + centers[0]
        root = root_of(anchor * anchor + centers[1] * (x0 * x0) + centers[2] * (x1 * x1))
        tables.append(turn_sincos(weight * (root * (KAPPA / (2 * math.pi)))))
    arrive()
    pieces = []
    for c in range(cx):
        for part in range(2):
            line = samples_ref[part, :, c * NF : (c + 1) * NF]
            pieces.append(jnp.where(mask, line, 0.0))
    high, low = parts_of(jnp.concatenate(pieces, axis=0))
    spread = product(high, pick) + product(low, pick)
    for c in range(cx):
        sine, cosine = tables[c]
        span = 5 * SPLIT
        left = [
            spread[(2 * c + part) * SPLIT : (2 * c + part + 1) * SPLIT] * table
            for part in range(2)
            for table in basis
        ]
        lh, ll = parts_of(jnp.concatenate(left, axis=0))
        sh, sl = parts_of(sine[:fine])
        ch, cl = parts_of(cosine[:fine])
        by_cos = product(lh, ch) + (product(lh, cl) + product(ll, ch))
        by_sin = product(lh, sh) + (product(lh, sl) + product(ll, sh))
        re = by_cos[:span] - by_sin[span:]
        im = by_sin[:span] + by_cos[span:]
        hs, hc = sine[fine:], cosine[fine:]
        rows = [[], []]
        for k in range(5):
            r, i = re[k * SPLIT : (k + 1) * SPLIT], im[k * SPLIT : (k + 1) * SPLIT]
            rows[0].append(jnp.sum(r * hc - i * hs, axis=0, keepdims=True))
            rows[1].append(jnp.sum(i * hc + r * hs, axis=0, keepdims=True))
        for part in range(2):
            store((part * cx + c) * 5, jnp.concatenate(rows[part], axis=0))


def wait_all(ref, sem):
    pltpu.make_async_copy(ref, ref, sem).wait()


def leaf_rows(cx):
    return -(-10 * cx // 8) * 8


def kernel(
    counts,
    scattered,
    samples_hbm,
    out_ref,
    samples_ref,
    fetch_sem,
    state,
    first_spin,
    spin,
    leaf_out,
    leaf_in,
    part_out,
    part_in,
    gather_send,
    gather_recv,
    scatter_send,
    scatter_recv,
    swap_out=None,
    swap_in=None,
    swap_send=None,
    swap_recv=None,
):
    fetch = pltpu.make_async_copy(samples_hbm, samples_ref, fetch_sem)
    fetch.start()
    cx = samples_ref.shape[2] // NF
    pitch = leaf_rows(cx)
    index = (lax.axis_index("inline"), lax.axis_index("xline"))
    plan = roster(*counts)
    middle = plan[GATHERED : len(plan) - scattered]
    final = plan[len(plan) - scattered :]
    bits = [(index[axis] >> place) & 1 for axis, place in plan]
    size = [c * 1.0 for c in counts]

    def other(flips):
        target = list(index)
        for axis, place in flips:
            target[axis] = target[axis] ^ (1 << place)
        return tuple(target)

    def subsets(levels):
        return [
            [level for k, level in enumerate(levels) if pattern >> k & 1]
            for pattern in range(1, 1 << len(levels))
        ]

    near = subsets(plan[:GATHERED])
    far = [[plan[1]] + flips for flips in [[]] + subsets(final)][::-1]
    calls = near + [f for f in far if f not in near] + [[level] for level in middle]
    partners = [other(f) for f in calls]
    barrier = pltpu.get_barrier_semaphore()
    for partner in partners:
        pl.semaphore_signal(barrier, inc=1, device_id=partner, device_id_type=MESH)

    half = COLS // 2
    own_slot = bits[0] * 2 + bits[1]
    own_row = own_slot * pitch

    def keep(row, value):
        for side in range(2):
            leaf_out[side * pitch + row : side * pitch + row + 5, :] = value[
                :, side * half : (side + 1) * half
            ]

    position = [i.astype(jnp.float32) for i in index]
    leaf_sums(samples_ref, fetch.wait, keep, position[0], position[1], size[0], size[1])
    mine = pl.multiple_of(bits[0] * pitch, 8)
    leaf_in[pl.ds(pl.multiple_of(own_row, 8), pitch), :] = leaf_out[pl.ds(mine, pitch), :]

    pl.semaphore_wait(barrier, len(partners))
    for flips in near:
        wanted = bits[0] ^ (1 if plan[0] in flips else 0)
        copy = pltpu.make_async_remote_copy(
            src_ref=leaf_out.at[pl.ds(pl.multiple_of(wanted * pitch, 8), pitch), :],
            dst_ref=leaf_in.at[pl.ds(pl.multiple_of(own_row, 8), pitch), :],
            send_sem=gather_send,
            recv_sem=gather_recv,
            device_id=other(flips),
            device_id_type=MESH,
        )
        copy.start()

    sub = lax.broadcasted_iota(jnp.int32, (8, half), 0)
    flag = [((sub >> k) & 1) == 1 for k in range(3)]
    sign = [jnp.where(f, 1.0, -1.0) for f in flag]
    depth, splits = split_counts()
    merged = [0, 0]

    def advance():
        nonlocal depth
        axis = depth % 3
        quarter = 0.25 * 0.5 ** splits[axis]
        splits[axis] += 1
        depth += 1
        return axis, quarter

    def box(axis):
        width = 2.0 ** merged[axis] / size[axis]
        low = ((index[axis] >> merged[axis]) << merged[axis]).astype(jnp.float32) / size[axis]
        return low, width

    def parent_low(axis):
        up = merged[axis] + 1
        return ((index[axis] >> up) << up).astype(jnp.float32) / size[axis]

    def prepare(slot, centers, children, xi, xc, reach):
        old, new = radicands(centers, xi, xc), radicands(children, xi, xc)
        for i in range(5):
            for j in range(5):
                for k, (c, s) in enumerate(rotors(old(i, j), new(i, j), reach)):
                    row = (i * 5 + j) * 5 + k
                    spin[slot, 0, row], spin[slot, 1, row] = c, s

    def prepare_pairs(centers, children, xi, xc, reach):
        old, new = radicands(centers, xi, xc), radicands(children, xi, xc)
        for i in range(5):
            for j in range(5):
                for k, (c, s) in enumerate(pair_rotors(old(i, j), new(i, j), reach, -sign[0])):
                    row = (i * 5 + j) * 3 + k
                    spin[0, 0, row], spin[0, 1, row] = c, s

    def place(axis, o, k):
        return [((a * 5 + o) if axis == 0 else (o * 5 + a)) * 5 + k for a in range(5)]

    def fold(slot, axis, choose, held):
        for o in range(5):
            for k in range(5):
                rows = place(axis, o, k)
                after = [[spin[slot, part, r] for r in rows] for part in range(2)]
                for b in range(5):
                    both = []
                    for part in range(2):
                        total = None
                        for a in range(5):
                            if MIX[0][a, b] != 0.0 or MIX[1][a, b] != 0.0:
                                term = after[part][a] * choose(a, b)
                                total = term if total is None else total + term
                        both.append(total)
                    re, im = both
                    c, s = spin[held, 0, rows[b]], spin[held, 1, rows[b]]
                    spin[slot, 0, rows[b]] = re * c - im * s
                    spin[slot, 1, rows[b]] = re * s + im * c

    def turn(slot):
        for row in range(125):
            re, im = state[0, row], state[1, row]
            c, s = spin[slot, 0, row], spin[slot, 1, row]
            state[0, row] = re * c - im * s
            state[1, row] = re * s + im * c

    def mix(axis, choose, finish):
        used = [
            [(b, choose(a, b)) for b in range(5) if MIX[0][a, b] != 0.0 or MIX[1][a, b] != 0.0]
            for a in range(5)
        ]
        for part in range(2):
            for o in range(5):
                for k in range(5):
                    rows = place(axis, o, k)
                    values = [state[part, r] for r in rows]
                    for a in range(5):
                        total = None
                        for b, coefficient in used[a]:
                            term = values[b] * coefficient
                            total = term if total is None else total + term
                        state[part, rows[a]] = finish(total)

    column = lax.broadcasted_iota(jnp.int32, (8, half), 1) + bits[0] * half
    centers = initial_centers(column)

    axis, quarter = advance()
    children = shifted(centers, axis, (1.0 - 2.0 * bits[1].astype(jnp.float32)) * quarter)
    low0, width0 = parent_low(0), 1.0 / size[0]
    low1, width1 = parent_low(1), 1.0 / size[1]
    xc = side_points(low1 + jnp.where(flag[2], width1, 0.0), width1)
    for t in range(2):
        x = [low0 + width0 * (t + 0.5)]
        old, new = radicands(centers, x, xc), radicands(children, x, xc)
        for j in range(5):
            for k, (c, s) in enumerate(pair_rotors(old(0, j), new(0, j), quarter, -sign[0])):
                row = (j * 2 + t) * 3 + k
                first_spin[0, row], first_spin[1, row] = c, s
    merged[0] += 1
    centers = children

    def pair_geometry(level_axis, centers):
        axis, quarter = advance()
        children = shifted(centers, axis, sign[1] * quarter)
        spans = []
        for k in range(2):
            low, width = box(k)
            if k == level_axis:
                low = parent_low(k) + jnp.where(flag[2], width, 0.0)
            spans.append(side_points(low, width))
        merged[level_axis] += 1
        return (centers, children, spans[0], spans[1], quarter), axis

    geometry, axis = pair_geometry(plan[1][0], centers)
    prepare_pairs(*geometry)
    later = []
    for k, level in enumerate(middle):
        side = 2.0 * bits[GATHERED + k].astype(jnp.float32) - 1.0
        centers = shifted(geometry[0], axis, side * geometry[4])
        geometry, axis = pair_geometry(level[0], centers)
        later.append(geometry)
    spot = [1, 2, 0]
    centers = geometry[1]
    for k, level in enumerate(final):
        axis, quarter = advance()
        low0, width0 = box(0)
        low1, width1 = box(1)
        xi, xc = side_points(low0, width0), side_points(low1, width1)
        if k < scattered - 1:
            children = shifted(centers, axis, sign[spot[k + 1]] * quarter)
            prepare(1 + k, centers, children, xi, xc, quarter)
            centers = children
        else:
            for side in range(2):
                children = shifted(centers, axis, (2.0 * side - 1.0) * quarter)
                prepare(1 + k + side, centers, children, xi, xc, quarter)
        merged[level[0]] += 1
    for k in reversed(range(scattered - 1)):
        side = bits[len(plan) - scattered + k].astype(jnp.float32)
        for last in range(2):
            fold(
                scattered + last,
                final[k][0],
                lambda a, b: (1.0 - side) * MIX[0][a, b] + side * MIX[1][a, b],
                1 + k,
            )

    wait_all(leaf_in.at[pl.ds(0, len(near) * pitch), :], gather_recv)
    across = lagrange((np.arange(cx) + 0.5) / cx - 0.5)
    sums = [[None, None], [None, None]]

    def gather_sums(row, re, im):
        for last in range(2):
            c, s = spin[scattered + last, 0, row], spin[scattered + last, 1, row]
            for part, term in enumerate((re * c - im * s, re * s + im * c)):
                held = sums[part][last]
                sums[part][last] = term if held is None else held + term

    def keep_state(row, re, im):
        state[0, row], state[1, row] = re, im

    emit = keep_state if middle else gather_sums
    used = [
        [
            (b, jnp.where(flag[2], MIX[1][a, b], MIX[0][a, b]).astype(jnp.float32))
            for b in range(5)
            if MIX[0][a, b] != 0.0 or MIX[1][a, b] != 0.0
        ]
        for a in range(5)
    ]
    even = [0.5 * (MIX[0][i, 2] + MIX[1][i, 2]) for i in range(3)]
    odd = [0.5 * (MIX[0][i, 2] - MIX[1][i, 2]) for i in range(3)]

    def second_level(pair, i, before):
        lo, hi = PAIRS[pair]
        turned = []
        for j in range(5):
            re, im = before[0][j], before[1][j]
            row = (i * 5 + j) * 3 + pair
            c, s = spin[0, 0, row], spin[0, 1, row]
            turned.append((re * c - im * s, re * s + im * c))
        for a in range(5):
            both = []
            for part in range(2):
                total = None
                for b, coefficient in used[a]:
                    term = turned[b][part] * coefficient
                    total = term if total is None else total + term
                both.append(total + pltpu.roll(total, 4, 0))
            row = (i * 5 + a) * 5
            if lo == hi:
                emit(row + lo, *both)
            else:
                emit(row + lo, *[jnp.where(flag[0], pltpu.roll(x, 1, 0), x) for x in both])
                emit(row + hi, *[jnp.where(flag[0], x, pltpu.roll(x, 7, 0)) for x in both])

    for pair, (lo, hi) in enumerate(PAIRS):
        turned = []
        for t in range(2):
            across_sums = []
            for part in range(2):
                values = []
                for c in range(cx):
                    row = 2 * t * pitch + (part * cx + c) * 5
                    lines = []
                    for q in range(2):
                        first, second = [
                            jnp.broadcast_to(leaf_in[pl.ds(q * pitch + row + k, 1), :], (8, half))
                            for k in (lo, hi)
                        ]
                        lines.append(first if lo == hi else jnp.where(flag[0], second, first))
                    values.append(jnp.where(flag[2], lines[1], lines[0]))
                totals = []
                for j in range(5):
                    total = values[0] * across[j, 0]
                    for c in range(1, cx):
                        total = total + values[c] * across[j, c]
                    totals.append(total)
                across_sums.append(totals)
            both = []
            for j in range(5):
                re, im = across_sums[0][j], across_sums[1][j]
                row = (j * 2 + t) * 3 + pair
                c, s = first_spin[0, row], first_spin[1, row]
                both.append((re * c - im * s, re * s + im * c))
            turned.append(both)
        plus = [[turned[0][j][p] + turned[1][j][p] for j in range(5)] for p in range(2)]
        minus = [[turned[0][j][p] - turned[1][j][p] for j in range(5)] for p in range(2)]
        for i in range(2):
            es = [[x * even[i] for x in line] for line in plus]
            os = [[x * odd[i] for x in line] for line in minus]
            second_level(pair, i, [[e + o for e, o in zip(*ls)] for ls in zip(es, os)])
            second_level(pair, 4 - i, [[e - o for e, o in zip(*ls)] for ls in zip(es, os)])
        second_level(pair, 2, [[x * even[2] for x in line] for line in plus])

    def joined(level_axis):
        turn(0)
        mix(
            level_axis,
            lambda a, b: jnp.where(flag[2], MIX[1][a, b], MIX[0][a, b]).astype(jnp.float32),
            lambda x: x + pltpu.roll(x, 4, 0),
        )

    for k, level in enumerate(middle):
        bit = bits[GATHERED + k]

        def pack(r, carry):
            mine = pl.ds(bit * 2, 1)
            theirs = pl.ds((1 - bit) * 2, 1)
            for part in range(2):
                line = pl.ds(part * 125 + r, 1)
                swap_out[k, line, :] = state[part, r, theirs, :]
                swap_in[2 * k + 1, line, :] = state[part, r, mine, :]
            return carry

        lax.fori_loop(0, 125, pack, 0)
        copy = pltpu.make_async_remote_copy(
            src_ref=swap_out.at[k],
            dst_ref=swap_in.at[2 * k],
            send_sem=swap_send.at[k],
            recv_sem=swap_recv.at[k],
            device_id=other([level]),
            device_id_type=MESH,
        )
        copy.start()
        prepare(0, *later[k])
        copy.wait()
        own_high = (sub >> 2) == bit

        def unpack(r, carry):
            for part in range(2):
                line = pl.ds(part * 125 + r, 1)
                near_line = jnp.broadcast_to(swap_in[2 * k + 1, line, :], (8, half))
                far_line = jnp.broadcast_to(swap_in[2 * k, line, :], (8, half))
                state[part, r] = jnp.where(own_high, near_line, far_line)
            return carry

        lax.fori_loop(0, 125, unpack, 0)
        joined(level[0])

    if middle:
        for row in range(125):
            gather_sums(row, state[0, row], state[1, row])
    for part in range(2):
        for side in range(2):
            part_out[pl.ds(part * 2 + side, 8, stride=8), :] = sums[part][side]

    def place_of(flips):
        total = 0
        for k, level in enumerate(final):
            bit = bits[len(plan) - scattered + k] ^ (1 if level in flips else 0)
            total = total + bit * (1 << spot[k])
        return pl.multiple_of(total * 8, 8)

    for k, flips in enumerate(far):
        copy = pltpu.make_async_remote_copy(
            src_ref=part_out.at[pl.ds(place_of(flips), 8), :],
            dst_ref=part_in.at[k],
            send_sem=scatter_send,
            recv_sem=scatter_recv,
            device_id=other(flips),
            device_id_type=MESH,
        )
        copy.start()
    wait_all(leaf_in.at[pl.ds(0, len(near) * pitch), :], gather_send)
    wait_all(part_in, scatter_recv)
    total = part_in[0]
    for k in range(1, len(far)):
        total = total + part_in[k]
    wait_all(part_in, scatter_send)
    for part in range(2):
        for side in range(2):
            line = part * 2 + side
            out_ref[part : part + 1, side * half : (side + 1) * half] = total[line : line + 1, :]


def shards(samples):
    counts = (lax.axis_size("inline"), lax.axis_size("xline"))
    plan = roster(*counts)
    scattered = SCATTERED
    middle = len(plan) - GATHERED - scattered
    if middle < 0 or samples.shape[1] != 1 or plan[:2] != [(0, 0), (1, 0)]:
        raise ValueError("unsupported mesh")
    half = COLS // 2
    pitch = leaf_rows(samples.shape[2] // NF)
    swaps = [
        pltpu.VMEM((middle, 256, half), jnp.float32),
        pltpu.VMEM((2 * middle, 256, half), jnp.float32),
        pltpu.SemaphoreType.DMA((middle,)),
        pltpu.SemaphoreType.DMA((middle,)),
    ]
    norm = 1.0 / math.sqrt(samples.shape[1] * samples.shape[2] * counts[0] * counts[1])
    values = pl.pallas_call(
        functools.partial(kernel, counts, scattered),
        out_shape=jax.ShapeDtypeStruct((2, COLS), jnp.float32),
        in_specs=[pl.BlockSpec(memory_space=pltpu.HBM)],
        out_specs=pl.BlockSpec(memory_space=pltpu.VMEM),
        scratch_shapes=[
            pltpu.VMEM(samples.shape, jnp.float32),
            pltpu.SemaphoreType.DMA,
            pltpu.VMEM((2, 125, 8, half), jnp.float32),
            pltpu.VMEM((2, 30, 8, half), jnp.float32),
            pltpu.VMEM((scattered + 2, 2, 125, 8, half), jnp.float32),
            pltpu.VMEM((2 * pitch, half), jnp.float32),
            pltpu.VMEM((4 * pitch, half), jnp.float32),
            pltpu.VMEM((64, half), jnp.float32),
            pltpu.VMEM((1 << scattered, 8, half), jnp.float32),
            *[pltpu.SemaphoreType.DMA] * 4,
            *(swaps if middle else []),
        ],
        compiler_params=pltpu.CompilerParams(
            collective_id=0, has_side_effects=True, vmem_limit_bytes=20 << 20
        ),
    )(pltpu.with_memory_space_constraint(samples, pltpu.HBM))
    return values * norm


def solution(mesh):
    return jax.shard_map(
        shards,
        mesh=mesh,
        in_specs=(P(None, "inline", "xline"),),
        out_specs=P(None, ("inline", "xline")),
        check_vma=False,
    )
```

```python
import functools
import math

import jax
import jax.numpy as jnp
import numpy as np
from jax import lax
from jax.experimental import pallas as pl
from jax.experimental.pallas import tpu as pltpu
from jax.sharding import PartitionSpec as P

NF = 256
COLS = 256
KAPPA = 40.0
LANES = 128
GATHERED = 2
SCATTERED = 3
MESH = pl.DeviceIdType.MESH
PAIRS = [(0, 4), (1, 3), (2, 2)]

NODES = np.array([0.5, 0.5 * math.sqrt(0.5), 0.0, -0.5 * math.sqrt(0.5), -0.5])


def lagrange(points):
    points = np.asarray(points, np.float64)
    rows = []
    for k in range(5):
        factor = np.ones_like(points)
        for j in range(5):
            if j != k:
                factor = factor * (points - NODES[j]) / (NODES[k] - NODES[j])
        rows.append(factor)
    table = np.stack(rows)
    return np.where(np.abs(table) < 1e-13, 0.0, table)


MIX = [lagrange((t - 0.5) / 2 + NODES / 2) for t in range(2)]


def roster(inline_count, xline_count):
    inline_bits = inline_count.bit_length() - 1
    xline_bits = xline_count.bit_length() - 1
    plan = []
    for level in range(max(inline_bits, xline_bits)):
        if level < inline_bits:
            plan.append((0, level))
        if level < xline_bits:
            plan.append((1, level))
    return plan


def split_counts():
    depth = (COLS - 1).bit_length()
    return depth, [len([j for j in range(depth) if j % 3 == axis]) for axis in range(3)]


def initial_centers(column):
    depth, _ = split_counts()
    coords = []
    for axis in range(3):
        splits = [j for j in range(depth) if j % 3 == axis]
        coord = jnp.full(column.shape, 0.5 * 0.5 ** len(splits), jnp.float32)
        for rank, j in enumerate(splits):
            digit = (column >> (depth - 1 - j)) & 1
            coord = coord + digit.astype(jnp.float32) * 0.5 ** (rank + 1)
        coords.append(coord)
    return coords


def poly(square, terms):
    total = jnp.full(square.shape, terms[-1], jnp.float32)
    for term in reversed(terms[:-1]):
        total = total * square + term
    return total


def series(limit):
    both = []
    for odd in (1, 0):
        terms = []
        while not terms or limit ** (2 * len(terms) + odd) / math.factorial(2 * len(terms) + odd) > 1e-7:
            terms.append((-1.0) ** len(terms) / math.factorial(2 * len(terms) + odd))
        both.append(terms)
    return both


def root_of(square):
    return square * lax.rsqrt(square)


def parts_of(value):
    high = value.astype(jnp.bfloat16)
    return high, (value - high.astype(jnp.float32)).astype(jnp.bfloat16)


def product(left, right):
    return jnp.dot(left, right, preferred_element_type=jnp.float32)


def small_sincos(angle, limit):
    sine, cosine = series(limit)
    square = angle * angle
    return angle * poly(square, sine), poly(square, cosine)


def turn_sincos(turns):
    half = (turns - jnp.round(turns)) * math.pi
    s, c = small_sincos(half, math.pi / 2)
    return 2.0 * s * c, 1.0 - 2.0 * s * s


def base_rotors(before, after, reach):
    gap = root_of(after) - root_of(before)
    cs, cc = small_sincos(gap * (0.5 * KAPPA), 0.5 * KAPPA * reach)
    bs, bc = small_sincos(gap * (NODES[1] * KAPPA), NODES[1] * KAPPA * reach)
    twice = cs + cs
    return (cc, cs), (bc, bs), (1.0 - twice * cs, twice * cc)


def rotors(before, after, reach):
    (cc, cs), (bc, bs), (a_c, a_s) = base_rotors(before, after, reach)
    p, q, u, v = a_c * bc, a_s * bs, a_s * bc, a_c * bs
    return [
        (a_c * cc - a_s * cs, a_s * cc + a_c * cs),
        (p - q, u + v),
        (a_c, a_s),
        (p + q, u - v),
        (cc, cs),
    ]


def pair_rotors(before, after, reach, sign):
    (cc, cs), (bc, bs), (a_c, a_s) = base_rotors(before, after, reach)
    cs, bs = cs * sign, bs * sign
    return [
        (a_c * cc - a_s * cs, a_s * cc + a_c * cs),
        (a_c * bc - a_s * bs, a_s * bc + a_c * bs),
        (a_c, a_s),
    ]


def side_points(low, width):
    return [low + width * (z + 0.5) for z in NODES]


def radicands(centers, xi, xc):
    anchor = 0.5 + centers[0]
    first = [anchor * anchor + centers[1] * (x * x) for x in xi]
    second = [centers[2] * (x * x) for x in xc]
    return lambda i, j: first[i] + second[j]


def shifted(centers, axis, amount):
    return [c + amount if k == axis else c for k, c in enumerate(centers)]


def leaf_sums(samples_ref, arrive, store, inline_pos, xline_pos, inline_count, xline_count):
    rows = samples_ref.shape[1]
    halves = NF // LANES
    cx = rows // halves
    fine = LANES // cx
    turn = KAPPA / (2 * math.pi)
    centers = initial_centers(lax.broadcasted_iota(jnp.int32, (1, COLS), 1))
    anchor = 0.5 + centers[0]
    x0 = (inline_pos + 0.5) / inline_count
    roots = []
    for c in range(cx):
        x1 = (xline_pos + (c + 0.5) / cx) / xline_count
        root = root_of(anchor * anchor + centers[1] * (x0 * x0) + centers[2] * (x1 * x1))
        roots.append(root * turn)
    step = lax.broadcasted_iota(jnp.int32, (fine, COLS), 0).astype(jnp.float32) * (1.0 / NF)
    near = [turn_sincos(step * root) for root in roots]
    near = [jnp.concatenate([table[part] for table in near], axis=0) for part in range(2)]
    row = lax.broadcasted_iota(jnp.int32, (rows, COLS), 0)
    root = jnp.broadcast_to(roots[0], (rows, COLS))
    for c in range(1, cx):
        root = jnp.where(row // halves == c, roots[c], root)
    far = []
    for d in range(cx):
        start = row % halves * LANES + (row // halves + cx - d) % cx * fine
        far.append(turn_sincos(root * (0.5 + (start.astype(jnp.float32) + 0.5) / NF)))
    row = lax.broadcasted_iota(jnp.int32, (rows, LANES), 0)
    lane = lax.broadcasted_iota(jnp.int32, (rows, LANES), 1)
    mask = lane // fine == row // halves
    basis = []
    for d in range(cx):
        spot = row % halves * LANES + (row // halves + cx - d) % cx * fine + lane % fine
        z = (spot.astype(jnp.float32) + 0.5) / NF - 0.5
        line = []
        for k in range(5):
            factor = None
            for j in range(5):
                if j != k:
                    term = (z - NODES[j]) * (1.0 / (NODES[k] - NODES[j]))
                    factor = term if factor is None else factor * term
            line.append(jnp.where(mask, factor, 0.0))
        basis.append(line)
    odd = row % 2 == 1
    width = COLS // 2
    tables = []
    for side in range(2):
        lanes = slice(side * width, (side + 1) * width)
        high, low = parts_of(jnp.concatenate([near[1][:, lanes], near[0][:, lanes]], axis=1))
        tables.append((jnp.concatenate([high, high], axis=0), low))
    arrive()
    moved = [
        [samples_ref[part] if d == 0 else pltpu.roll(samples_ref[part], d * fine, 1) for d in range(cx)]
        for part in range(2)
    ]
    left = [moved[part][d] * basis[d][k] for k in range(5) for part in range(2) for d in range(cx)]
    high, low = parts_of(jnp.concatenate(left, axis=0))
    both = jnp.concatenate([high, low], axis=1)
    for side in range(2):
        lanes = slice(side * width, (side + 1) * width)
        made = product(both, tables[side][0]) + product(high, tables[side][1])
        for k in range(5):
            sums = [None, None]
            for d in range(cx):
                start = (k * 2 * cx + d) * rows
                re = made[start : start + rows]
                im = made[start + cx * rows : start + (cx + 1) * rows]
                r, i = re[:, :width] - im[:, width:], re[:, width:] + im[:, :width]
                hs, hc = far[d][0][:, lanes], far[d][1][:, lanes]
                for part, term in enumerate((r * hc - i * hs, i * hc + r * hs)):
                    sums[part] = term if sums[part] is None else sums[part] + term
            re, im = sums
            pair = jnp.where(odd, im + pltpu.roll(im, 1, 0), re + pltpu.roll(re, rows - 1, 0))
            store(side, k * rows, pair)


def wait_all(ref, sem):
    pltpu.make_async_copy(ref, ref, sem).wait()


def kernel(
    counts,
    scattered,
    samples_hbm,
    out_ref,
    samples_ref,
    fetch_sem,
    state,
    first_spin,
    spin,
    leaf_out,
    leaf_in,
    part_out,
    part_in,
    gather_send,
    gather_recv,
    scatter_send,
    scatter_recv,
    swap_out=None,
    swap_in=None,
    swap_send=None,
    swap_recv=None,
):
    fetch = pltpu.make_async_copy(samples_hbm, samples_ref, fetch_sem)
    fetch.start()
    rows = samples_ref.shape[1]
    cx = rows * LANES // NF
    pitch = 5 * rows
    index = (lax.axis_index("inline"), lax.axis_index("xline"))
    plan = roster(*counts)
    middle = plan[GATHERED : len(plan) - scattered]
    final = plan[len(plan) - scattered :]
    bits = [(index[axis] >> place) & 1 for axis, place in plan]
    size = [c * 1.0 for c in counts]

    def other(flips):
        target = list(index)
        for axis, place in flips:
            target[axis] = target[axis] ^ (1 << place)
        return tuple(target)

    def subsets(levels):
        return [
            [level for k, level in enumerate(levels) if pattern >> k & 1]
            for pattern in range(1, 1 << len(levels))
        ]

    near = sorted(subsets(plan[:GATHERED]), key=lambda flips: plan[0] not in flips)
    far = [[plan[1]] + flips for flips in [[]] + subsets(final)][::-1]
    calls = near + [f for f in far if f not in near] + [[level] for level in middle]
    partners = [other(f) for f in calls]
    barrier = pltpu.get_barrier_semaphore()
    for partner in partners:
        pl.semaphore_signal(barrier, inc=1, device_id=partner, device_id_type=MESH)

    half = COLS // 2
    own_slot = bits[0] * 2 + bits[1]
    own_row = own_slot * pitch

    def keep(side, row, value):
        leaf_out[side * pitch + row : side * pitch + row + rows, :] = value

    position = [i.astype(jnp.float32) for i in index]
    leaf_sums(samples_ref, fetch.wait, keep, position[0], position[1], size[0], size[1])
    mine = pl.multiple_of(bits[0] * pitch, 8)
    leaf_in[pl.ds(pl.multiple_of(own_row, 8), pitch), :] = leaf_out[pl.ds(mine, pitch), :]

    pl.semaphore_wait(barrier, len(partners))
    for flips in near:
        wanted = bits[0] ^ (1 if plan[0] in flips else 0)
        copy = pltpu.make_async_remote_copy(
            src_ref=leaf_out.at[pl.ds(pl.multiple_of(wanted * pitch, 8), pitch), :],
            dst_ref=leaf_in.at[pl.ds(pl.multiple_of(own_row, 8), pitch), :],
            send_sem=gather_send,
            recv_sem=gather_recv,
            device_id=other(flips),
            device_id_type=MESH,
        )
        copy.start()

    sub = lax.broadcasted_iota(jnp.int32, (8, half), 0)
    flag = [((sub >> k) & 1) == 1 for k in range(3)]
    sign = [jnp.where(f, 1.0, -1.0) for f in flag]
    depth, splits = split_counts()
    merged = [0, 0]

    def advance():
        nonlocal depth
        axis = depth % 3
        quarter = 0.25 * 0.5 ** splits[axis]
        splits[axis] += 1
        depth += 1
        return axis, quarter

    def box(axis):
        width = 2.0 ** merged[axis] / size[axis]
        low = ((index[axis] >> merged[axis]) << merged[axis]).astype(jnp.float32) / size[axis]
        return low, width

    def parent_low(axis):
        up = merged[axis] + 1
        return ((index[axis] >> up) << up).astype(jnp.float32) / size[axis]

    def prepare(slot, centers, children, xi, xc, reach):
        old, new = radicands(centers, xi, xc), radicands(children, xi, xc)
        for i in range(5):
            for j in range(5):
                for k, (c, s) in enumerate(rotors(old(i, j), new(i, j), reach)):
                    row = (i * 5 + j) * 5 + k
                    spin[slot, 0, row], spin[slot, 1, row] = c, s

    def prepare_pairs(centers, children, xi, xc, reach):
        old, new = radicands(centers, xi, xc), radicands(children, xi, xc)
        for i in range(5):
            for j in range(5):
                for k, (c, s) in enumerate(pair_rotors(old(i, j), new(i, j), reach, -sign[0])):
                    row = (i * 5 + j) * 3 + k
                    spin[0, 0, row], spin[0, 1, row] = c, s

    def place(axis, o, k):
        return [((a * 5 + o) if axis == 0 else (o * 5 + a)) * 5 + k for a in range(5)]

    def fold(slot, axis, choose, held):
        for o in range(5):
            for k in range(5):
                rows = place(axis, o, k)
                after = [[spin[slot, part, r] for r in rows] for part in range(2)]
                for b in range(5):
                    both = []
                    for part in range(2):
                        total = None
                        for a in range(5):
                            if MIX[0][a, b] != 0.0 or MIX[1][a, b] != 0.0:
                                term = after[part][a] * choose(a, b)
                                total = term if total is None else total + term
                        both.append(total)
                    re, im = both
                    c, s = spin[held, 0, rows[b]], spin[held, 1, rows[b]]
                    spin[slot, 0, rows[b]] = re * c - im * s
                    spin[slot, 1, rows[b]] = re * s + im * c

    def turn(slot):
        for row in range(125):
            re, im = state[0, row], state[1, row]
            c, s = spin[slot, 0, row], spin[slot, 1, row]
            state[0, row] = re * c - im * s
            state[1, row] = re * s + im * c

    def mix(axis, choose, finish):
        used = [
            [(b, choose(a, b)) for b in range(5) if MIX[0][a, b] != 0.0 or MIX[1][a, b] != 0.0]
            for a in range(5)
        ]
        for part in range(2):
            for o in range(5):
                for k in range(5):
                    rows = place(axis, o, k)
                    values = [state[part, r] for r in rows]
                    for a in range(5):
                        total = None
                        for b, coefficient in used[a]:
                            term = values[b] * coefficient
                            total = term if total is None else total + term
                        state[part, rows[a]] = finish(total)

    column = lax.broadcasted_iota(jnp.int32, (8, half), 1) + bits[0] * half
    centers = initial_centers(column)

    axis, quarter = advance()
    children = shifted(centers, axis, (1.0 - 2.0 * bits[1].astype(jnp.float32)) * quarter)
    low0, width0 = parent_low(0), 1.0 / size[0]
    low1, width1 = parent_low(1), 1.0 / size[1]
    xc = side_points(low1 + jnp.where(flag[2], width1, 0.0), width1)
    for t in range(2):
        x = [low0 + width0 * (t + 0.5)]
        old, new = radicands(centers, x, xc), radicands(children, x, xc)
        for j in range(5):
            for k, (c, s) in enumerate(pair_rotors(old(0, j), new(0, j), quarter, -sign[0])):
                row = (j * 2 + t) * 3 + k
                first_spin[0, row], first_spin[1, row] = c, s
    merged[0] += 1
    centers = children

    def pair_geometry(level_axis, centers):
        axis, quarter = advance()
        children = shifted(centers, axis, sign[1] * quarter)
        spans = []
        for k in range(2):
            low, width = box(k)
            if k == level_axis:
                low = parent_low(k) + jnp.where(flag[2], width, 0.0)
            spans.append(side_points(low, width))
        merged[level_axis] += 1
        return (centers, children, spans[0], spans[1], quarter), axis

    geometry, axis = pair_geometry(plan[1][0], centers)
    prepare_pairs(*geometry)
    later = []
    for k, level in enumerate(middle):
        side = 2.0 * bits[GATHERED + k].astype(jnp.float32) - 1.0
        centers = shifted(geometry[0], axis, side * geometry[4])
        geometry, axis = pair_geometry(level[0], centers)
        later.append(geometry)
    spot = [1, 2, 0]
    centers = geometry[1]
    for k, level in enumerate(final):
        axis, quarter = advance()
        low0, width0 = box(0)
        low1, width1 = box(1)
        xi, xc = side_points(low0, width0), side_points(low1, width1)
        if k < scattered - 1:
            children = shifted(centers, axis, sign[spot[k + 1]] * quarter)
            prepare(1 + k, centers, children, xi, xc, quarter)
            centers = children
        else:
            for side in range(2):
                children = shifted(centers, axis, (2.0 * side - 1.0) * quarter)
                prepare(1 + k + side, centers, children, xi, xc, quarter)
        merged[level[0]] += 1
    for k in reversed(range(scattered - 1)):
        side = bits[len(plan) - scattered + k].astype(jnp.float32)
        for last in range(2):
            fold(
                scattered + last,
                final[k][0],
                lambda a, b: (1.0 - side) * MIX[0][a, b] + side * MIX[1][a, b],
                1 + k,
            )

    wait_all(leaf_in.at[pl.ds(0, len(near) * pitch), :], gather_recv)
    across = lagrange((np.arange(cx) + 0.5) / cx - 0.5)
    sums = [[None, None], [None, None]]

    def gather_sums(row, re, im):
        for last in range(2):
            c, s = spin[scattered + last, 0, row], spin[scattered + last, 1, row]
            for part, term in enumerate((re * c - im * s, re * s + im * c)):
                held = sums[part][last]
                sums[part][last] = term if held is None else held + term

    def keep_state(row, re, im):
        state[0, row], state[1, row] = re, im

    emit = keep_state if middle else gather_sums
    used = [
        [
            (b, jnp.where(flag[2], MIX[1][a, b], MIX[0][a, b]).astype(jnp.float32))
            for b in range(5)
            if MIX[0][a, b] != 0.0 or MIX[1][a, b] != 0.0
        ]
        for a in range(5)
    ]
    even = [0.5 * (MIX[0][i, 2] + MIX[1][i, 2]) for i in range(3)]
    odd = [0.5 * (MIX[0][i, 2] - MIX[1][i, 2]) for i in range(3)]

    def second_level(pair, i, before):
        lo, hi = PAIRS[pair]
        turned = []
        for j in range(5):
            re, im = before[0][j], before[1][j]
            row = (i * 5 + j) * 3 + pair
            c, s = spin[0, 0, row], spin[0, 1, row]
            turned.append((re * c - im * s, re * s + im * c))
        for a in range(5):
            both = []
            for part in range(2):
                total = None
                for b, coefficient in used[a]:
                    term = turned[b][part] * coefficient
                    total = term if total is None else total + term
                both.append(total + pltpu.roll(total, 4, 0))
            row = (i * 5 + a) * 5
            if lo == hi:
                emit(row + lo, *both)
            else:
                emit(row + lo, *[jnp.where(flag[0], pltpu.roll(x, 1, 0), x) for x in both])
                emit(row + hi, *[jnp.where(flag[0], x, pltpu.roll(x, 7, 0)) for x in both])

    for pair, (lo, hi) in enumerate(PAIRS):
        turned = []
        for t in range(2):
            across_sums = []
            for part in range(2):
                values = []
                for c in range(cx):
                    row = 2 * t * pitch + 2 * c + part
                    lines = []
                    for q in range(2):
                        first, second = [
                            jnp.broadcast_to(leaf_in[pl.ds(q * pitch + row + k * rows, 1), :], (8, half))
                            for k in (lo, hi)
                        ]
                        lines.append(first if lo == hi else jnp.where(flag[0], second, first))
                    values.append(jnp.where(flag[2], lines[1], lines[0]))
                totals = []
                for j in range(5):
                    total = values[0] * across[j, 0]
                    for c in range(1, cx):
                        total = total + values[c] * across[j, c]
                    totals.append(total)
                across_sums.append(totals)
            both = []
            for j in range(5):
                re, im = across_sums[0][j], across_sums[1][j]
                row = (j * 2 + t) * 3 + pair
                c, s = first_spin[0, row], first_spin[1, row]
                both.append((re * c - im * s, re * s + im * c))
            turned.append(both)
        plus = [[turned[0][j][p] + turned[1][j][p] for j in range(5)] for p in range(2)]
        minus = [[turned[0][j][p] - turned[1][j][p] for j in range(5)] for p in range(2)]
        for i in range(2):
            es = [[x * even[i] for x in line] for line in plus]
            os = [[x * odd[i] for x in line] for line in minus]
            second_level(pair, i, [[e + o for e, o in zip(*ls)] for ls in zip(es, os)])
            second_level(pair, 4 - i, [[e - o for e, o in zip(*ls)] for ls in zip(es, os)])
        second_level(pair, 2, [[x * even[2] for x in line] for line in plus])

    def joined(level_axis):
        turn(0)
        mix(
            level_axis,
            lambda a, b: jnp.where(flag[2], MIX[1][a, b], MIX[0][a, b]).astype(jnp.float32),
            lambda x: x + pltpu.roll(x, 4, 0),
        )

    for k, level in enumerate(middle):
        bit = bits[GATHERED + k]

        def pack(r, carry):
            mine = pl.ds(bit * 2, 1)
            theirs = pl.ds((1 - bit) * 2, 1)
            for part in range(2):
                line = pl.ds(part * 125 + r, 1)
                swap_out[k, line, :] = state[part, r, theirs, :]
                swap_in[2 * k + 1, line, :] = state[part, r, mine, :]
            return carry

        lax.fori_loop(0, 125, pack, 0)
        copy = pltpu.make_async_remote_copy(
            src_ref=swap_out.at[k],
            dst_ref=swap_in.at[2 * k],
            send_sem=swap_send.at[k],
            recv_sem=swap_recv.at[k],
            device_id=other([level]),
            device_id_type=MESH,
        )
        copy.start()
        prepare(0, *later[k])
        copy.wait()
        own_high = (sub >> 2) == bit

        def unpack(r, carry):
            for part in range(2):
                line = pl.ds(part * 125 + r, 1)
                near_line = jnp.broadcast_to(swap_in[2 * k + 1, line, :], (8, half))
                far_line = jnp.broadcast_to(swap_in[2 * k, line, :], (8, half))
                state[part, r] = jnp.where(own_high, near_line, far_line)
            return carry

        lax.fori_loop(0, 125, unpack, 0)
        joined(level[0])

    if middle:
        for row in range(125):
            gather_sums(row, state[0, row], state[1, row])
    for part in range(2):
        for side in range(2):
            part_out[pl.ds(part * 2 + side, 8, stride=8), :] = sums[part][side]

    def place_of(flips):
        total = 0
        for k, level in enumerate(final):
            bit = bits[len(plan) - scattered + k] ^ (1 if level in flips else 0)
            total = total + bit * (1 << spot[k])
        return pl.multiple_of(total * 8, 8)

    for k, flips in enumerate(far):
        copy = pltpu.make_async_remote_copy(
            src_ref=part_out.at[pl.ds(place_of(flips), 8), :],
            dst_ref=part_in.at[k],
            send_sem=scatter_send,
            recv_sem=scatter_recv,
            device_id=other(flips),
            device_id_type=MESH,
        )
        copy.start()
    wait_all(leaf_in.at[pl.ds(0, len(near) * pitch), :], gather_send)
    wait_all(part_in, scatter_recv)
    total = part_in[0]
    for k in range(1, len(far)):
        total = total + part_in[k]
    wait_all(part_in, scatter_send)
    for part in range(2):
        for side in range(2):
            line = part * 2 + side
            out_ref[part : part + 1, side * half : (side + 1) * half] = total[line : line + 1, :]


def shards(samples):
    counts = (lax.axis_size("inline"), lax.axis_size("xline"))
    plan = roster(*counts)
    scattered = SCATTERED
    middle = len(plan) - GATHERED - scattered
    size = samples.shape[2]
    fits = samples.shape[1] == 1 and size == 8 * LANES and NF == 2 * LANES
    if middle < 0 or not fits or plan[:2] != [(0, 0), (1, 0)]:
        raise ValueError("unsupported mesh")
    half = COLS // 2
    samples = samples.reshape(2, size // LANES, LANES)
    pitch = 5 * samples.shape[1]
    swaps = [
        pltpu.VMEM((middle, 256, half), jnp.float32),
        pltpu.VMEM((2 * middle, 256, half), jnp.float32),
        pltpu.SemaphoreType.DMA((middle,)),
        pltpu.SemaphoreType.DMA((middle,)),
    ]
    norm = 1.0 / math.sqrt(size * counts[0] * counts[1])
    values = pl.pallas_call(
        functools.partial(kernel, counts, scattered),
        out_shape=jax.ShapeDtypeStruct((2, COLS), jnp.float32),
        in_specs=[pl.BlockSpec(memory_space=pltpu.HBM)],
        out_specs=pl.BlockSpec(memory_space=pltpu.VMEM),
        scratch_shapes=[
            pltpu.VMEM(samples.shape, jnp.float32),
            pltpu.SemaphoreType.DMA,
            pltpu.VMEM((2, 125, 8, half), jnp.float32),
            pltpu.VMEM((2, 30, 8, half), jnp.float32),
            pltpu.VMEM((scattered + 2, 2, 125, 8, half), jnp.float32),
            pltpu.VMEM((2 * pitch, half), jnp.float32),
            pltpu.VMEM((4 * pitch, half), jnp.float32),
            pltpu.VMEM((64, half), jnp.float32),
            pltpu.VMEM((1 << scattered, 8, half), jnp.float32),
            *[pltpu.SemaphoreType.DMA] * 4,
            *(swaps if middle else []),
        ],
        compiler_params=pltpu.CompilerParams(
            collective_id=0, has_side_effects=True, vmem_limit_bytes=20 << 20
        ),
    )(pltpu.with_memory_space_constraint(samples, pltpu.HBM))
    return values * norm


def solution(mesh):
    return jax.shard_map(
        shards,
        mesh=mesh,
        in_specs=(P(None, "inline", "xline"),),
        out_specs=P(None, ("inline", "xline")),
        check_vma=False,
    )
```

```python
import functools
import math

import jax
import jax.numpy as jnp
import numpy as np
from jax import lax
from jax.experimental import pallas as pl
from jax.experimental.pallas import tpu as pltpu
from jax.sharding import PartitionSpec as P

NF = 256
COLS = 256
KAPPA = 40.0
LANES = 128
GATHERED = 2
SCATTERED = 3
MESH = pl.DeviceIdType.MESH
PAIRS = [(0, 4), (1, 3), (2, 2)]
ORDER = [0, 4, 1, 3, 2]

NODES = np.array([0.5, 0.5 * math.sqrt(0.5), 0.0, -0.5 * math.sqrt(0.5), -0.5])


def lagrange(points):
    points = np.asarray(points, np.float64)
    rows = []
    for k in range(5):
        factor = np.ones_like(points)
        for j in range(5):
            if j != k:
                factor = factor * (points - NODES[j]) / (NODES[k] - NODES[j])
        rows.append(factor)
    table = np.stack(rows)
    return np.where(np.abs(table) < 1e-13, 0.0, table)


MIX = [lagrange((t - 0.5) / 2 + NODES / 2) for t in range(2)]


def roster(inline_count, xline_count):
    inline_bits = inline_count.bit_length() - 1
    xline_bits = xline_count.bit_length() - 1
    plan = []
    for level in range(max(inline_bits, xline_bits)):
        if level < inline_bits:
            plan.append((0, level))
        if level < xline_bits:
            plan.append((1, level))
    return plan


def split_counts():
    depth = (COLS - 1).bit_length()
    return depth, [len([j for j in range(depth) if j % 3 == axis]) for axis in range(3)]


def initial_centers(column):
    depth, _ = split_counts()
    coords = []
    for axis in range(3):
        splits = [j for j in range(depth) if j % 3 == axis]
        coord = jnp.full(column.shape, 0.5 * 0.5 ** len(splits), jnp.float32)
        for rank, j in enumerate(splits):
            digit = (column >> (depth - 1 - j)) & 1
            coord = coord + digit.astype(jnp.float32) * 0.5 ** (rank + 1)
        coords.append(coord)
    return coords


def poly(square, terms):
    total = jnp.full(square.shape, terms[-1], jnp.float32)
    for term in reversed(terms[:-1]):
        total = total * square + term
    return total


def series(limit):
    both = []
    for odd in (1, 0):
        terms = []
        while not terms or limit ** (2 * len(terms) + odd) / math.factorial(2 * len(terms) + odd) > 1e-7:
            terms.append((-1.0) ** len(terms) / math.factorial(2 * len(terms) + odd))
        both.append(terms)
    return both


def root_of(square):
    return square * lax.rsqrt(square)


def parts_of(value):
    high = value.astype(jnp.bfloat16)
    return high, (value - high.astype(jnp.float32)).astype(jnp.bfloat16)


def product(left, right):
    return jnp.dot(left, right, preferred_element_type=jnp.float32)


def small_sincos(angle, limit):
    sine, cosine = series(limit)
    square = angle * angle
    return angle * poly(square, sine), poly(square, cosine)


def turn_sincos(turns):
    half = (turns - jnp.round(turns)) * math.pi
    s, c = small_sincos(half, math.pi / 2)
    return 2.0 * s * c, 1.0 - 2.0 * s * s


def base_rotors(before, after, reach):
    gap = root_of(after) - root_of(before)
    cs, cc = small_sincos(gap * (0.5 * KAPPA), 0.5 * KAPPA * reach)
    bs, bc = small_sincos(gap * (NODES[1] * KAPPA), NODES[1] * KAPPA * reach)
    twice = cs + cs
    return (cc, cs), (bc, bs), (1.0 - twice * cs, twice * cc)


def rotors(before, after, reach):
    (cc, cs), (bc, bs), (a_c, a_s) = base_rotors(before, after, reach)
    p, q, u, v = a_c * bc, a_s * bs, a_s * bc, a_c * bs
    return [
        (a_c * cc - a_s * cs, a_s * cc + a_c * cs),
        (p - q, u + v),
        (a_c, a_s),
        (p + q, u - v),
        (cc, cs),
    ]


def pair_rotors(before, after, reach, sign):
    (cc, cs), (bc, bs), (a_c, a_s) = base_rotors(before, after, reach)
    cs, bs = cs * sign, bs * sign
    return [
        (a_c * cc - a_s * cs, a_s * cc + a_c * cs),
        (a_c * bc - a_s * bs, a_s * bc + a_c * bs),
        (a_c, a_s),
    ]


def side_points(low, width, turned=1.0):
    return [low + width * (z * turned + 0.5) for z in NODES]


def radicands(centers, xi, xc):
    anchor = 0.5 + centers[0]
    first = [anchor * anchor + centers[1] * (x * x) for x in xi]
    second = [centers[2] * (x * x) for x in xc]
    return lambda i, j: first[i] + second[j]


def shifted(centers, axis, amount):
    return [c + amount if k == axis else c for k, c in enumerate(centers)]


def leaf_sums(samples_ref, arrive, store, done, column, inline_pos, xline_pos, inline_count, xline_count):
    rows = samples_ref.shape[1]
    halves = NF // LANES
    cx = rows // halves
    fine = LANES // cx
    turn = KAPPA / (2 * math.pi)
    centers = initial_centers(column)
    anchor = 0.5 + centers[0]
    x0 = (inline_pos + 0.5) / inline_count
    roots = []
    for c in range(cx):
        x1 = (xline_pos + (c + 0.5) / cx) / xline_count
        root = root_of(anchor * anchor + centers[1] * (x0 * x0) + centers[2] * (x1 * x1))
        roots.append(root * turn)
    step = lax.broadcasted_iota(jnp.int32, (fine, COLS), 0).astype(jnp.float32) * (1.0 / NF)
    near = [turn_sincos(step * root) for root in roots]
    near = [jnp.concatenate([table[part] for table in near], axis=0) for part in range(2)]
    row = lax.broadcasted_iota(jnp.int32, (rows, COLS), 0)
    root = jnp.broadcast_to(roots[0], (rows, COLS))
    for c in range(1, cx):
        root = jnp.where(row // halves == c, roots[c], root)
    far = []
    for d in range(cx):
        start = row % halves * LANES + (row // halves + cx - d) % cx * fine
        far.append(turn_sincos(root * (0.5 + (start.astype(jnp.float32) + 0.5) / NF)))
    row = lax.broadcasted_iota(jnp.int32, (rows, LANES), 0)
    lane = lax.broadcasted_iota(jnp.int32, (rows, LANES), 1)
    mask = lane // fine == row // halves
    basis = []
    for d in range(cx):
        spot = row % halves * LANES + (row // halves + cx - d) % cx * fine + lane % fine
        z = (spot.astype(jnp.float32) + 0.5) / NF - 0.5
        line = []
        for k in range(5):
            factor = None
            for j in range(5):
                if j != k:
                    term = (z - NODES[j]) * (1.0 / (NODES[k] - NODES[j]))
                    factor = term if factor is None else factor * term
            line.append(jnp.where(mask, factor, 0.0))
        basis.append(line)
    odd = row % 2 == 1
    width = COLS // 2
    tables = []
    for side in range(2):
        lanes = slice(side * width, (side + 1) * width)
        high, low = parts_of(jnp.concatenate([near[1][:, lanes], near[0][:, lanes]], axis=1))
        tables.append((jnp.concatenate([high, high], axis=0), low))
    arrive()
    moved = [
        [samples_ref[part] if d == 0 else pltpu.roll(samples_ref[part], d * fine, 1) for d in range(cx)]
        for part in range(2)
    ]
    left = [moved[part][d] * basis[d][k] for k in ORDER for part in range(2) for d in range(cx)]
    high, low = parts_of(jnp.concatenate(left, axis=0))
    both = jnp.concatenate([high, low], axis=1)
    cut = 4 * cx * rows
    for side in range(2):
        lanes = slice(side * width, (side + 1) * width)
        made = [
            product(both[part], tables[side][0]) + product(high[part], tables[side][1])
            for part in (slice(0, cut), slice(cut, None))
        ]
        for spot in range(5):
            sums = [None, None]
            for d in range(cx):
                start = (spot * 2 * cx + d) * rows
                half = made[start >= cut]
                start = start - cut if start >= cut else start
                re = half[start : start + rows]
                im = half[start + cx * rows : start + (cx + 1) * rows]
                r, i = re[:, :width] - im[:, width:], re[:, width:] + im[:, :width]
                hs, hc = far[d][0][:, lanes], far[d][1][:, lanes]
                for part, term in enumerate((r * hc - i * hs, i * hc + r * hs)):
                    sums[part] = term if sums[part] is None else sums[part] + term
            re, im = sums
            pair = jnp.where(odd, im + pltpu.roll(im, 1, 0), re + pltpu.roll(re, rows - 1, 0))
            store(side, spot, pair)
        done(side)


def wait_all(ref, sem):
    pltpu.make_async_copy(ref, ref, sem).wait()


def kernel(
    counts,
    scattered,
    samples_hbm,
    out_ref,
    samples_ref,
    fetch_sem,
    state,
    first_spin,
    spin,
    mixed,
    leaf_out,
    leaf_in,
    part_out,
    part_in,
    gather_send,
    gather_recv_0,
    gather_recv_1,
    gather_recv_2,
    scatter_send,
    scatter_recv,
    swap_out=None,
    swap_in=None,
    swap_send=None,
    swap_recv=None,
):
    gather_recv = (gather_recv_0, gather_recv_1, gather_recv_2)
    fetch = pltpu.make_async_copy(samples_hbm, samples_ref, fetch_sem)
    fetch.start()
    rows = samples_ref.shape[1]
    cx = rows * LANES // NF
    pitch = 5 * rows
    index = (lax.axis_index("inline"), lax.axis_index("xline"))
    plan = roster(*counts)
    middle = plan[GATHERED : len(plan) - scattered]
    final = plan[len(plan) - scattered :]
    bits = [(index[axis] >> place) & 1 for axis, place in plan]
    size = [c * 1.0 for c in counts]

    def other(flips):
        target = list(index)
        for axis, place in flips:
            target[axis] = target[axis] ^ (1 << place)
        return tuple(target)

    def subsets(levels):
        return [
            [level for k, level in enumerate(levels) if pattern >> k & 1]
            for pattern in range(1, 1 << len(levels))
        ]

    near = sorted(subsets(plan[:GATHERED]), key=lambda flips: plan[0] not in flips)
    far = [[plan[1]] + flips for flips in [[]] + subsets(final)][::-1]
    calls = near + [f for f in far if f not in near] + [[level] for level in middle]
    partners = [other(f) for f in calls]
    barrier = pltpu.get_barrier_semaphore()
    for partner in partners:
        pl.semaphore_signal(barrier, inc=1, device_id=partner, device_id_type=MESH)

    half = COLS // 2
    own_slot = bits[0] * 2 + bits[1]
    own_row = own_slot * pitch

    def keep(side, spot, value):
        row = side * pitch + spot * rows
        leaf_out[row : row + rows, :] = value

    def send(side):
        if side == 0:
            pl.semaphore_wait(barrier, len(partners))
        for (start, length), sem in zip(pieces, gather_recv):
            for flips in near:
                if (plan[0] in flips) == (side == 0):
                    pltpu.make_async_remote_copy(
                        src_ref=leaf_out.at[pl.ds(side * pitch + start, length), :],
                        dst_ref=leaf_in.at[pl.ds(pl.multiple_of(own_row + start, 8), length), :],
                        send_sem=gather_send,
                        recv_sem=sem,
                        device_id=other(flips),
                        device_id_type=MESH,
                    ).start()

    pieces = [(0, 2 * rows), (2 * rows, 2 * rows), (4 * rows, rows)]
    lane = lax.broadcasted_iota(jnp.int32, (1, COLS), 1)
    column = lane % half + half * jnp.where(lane < half, 1 - bits[0], bits[0])
    position = [i.astype(jnp.float32) for i in index]
    leaf_sums(samples_ref, fetch.wait, keep, send, column, position[0], position[1], size[0], size[1])
    leaf_in[pl.ds(pl.multiple_of(own_row, 8), pitch), :] = leaf_out[pl.ds(pitch, pitch), :]

    sub = lax.broadcasted_iota(jnp.int32, (8, half), 0)
    flag = [((sub >> k) & 1) == 1 for k in range(3)]
    sign = [jnp.where(f, 1.0, -1.0) for f in flag]
    depth, splits = split_counts()
    merged = [0, 0]

    def advance():
        nonlocal depth
        axis = depth % 3
        quarter = 0.25 * 0.5 ** splits[axis]
        splits[axis] += 1
        depth += 1
        return axis, quarter

    def box(axis):
        width = 2.0 ** merged[axis] / size[axis]
        low = ((index[axis] >> merged[axis]) << merged[axis]).astype(jnp.float32) / size[axis]
        return low, width

    def parent_low(axis):
        up = merged[axis] + 1
        return ((index[axis] >> up) << up).astype(jnp.float32) / size[axis]

    def prepare(slot, centers, children, xi, xc, reach):
        old, new = radicands(centers, xi, xc), radicands(children, xi, xc)
        for i in range(5):
            for j in range(5):
                for k, (c, s) in enumerate(rotors(old(i, j), new(i, j), reach)):
                    row = (i * 5 + j) * 5 + k
                    spin[slot, 0, row], spin[slot, 1, row] = c, s

    def prepare_pairs(centers, children, xi, xc, reach):
        old, new = radicands(centers, xi, xc), radicands(children, xi, xc)
        for i in range(5):
            for j in range(5):
                for k, (c, s) in enumerate(pair_rotors(old(i, j), new(i, j), reach, -sign[0])):
                    row = (i * 5 + j) * 3 + k
                    spin[0, 0, row], spin[0, 1, row] = c, s

    def place(axis, o, k):
        return [((a * 5 + o) if axis == 0 else (o * 5 + a)) * 5 + k for a in range(5)]

    def fold(slot, axis, held, finish):
        for o in range(5):
            for k in range(5):
                rows = place(axis, o, k)
                after = [[spin[slot, part, r] for r in rows] for part in range(2)]
                for b in range(5):
                    both = []
                    for part in range(2):
                        total = None
                        for a in range(5):
                            if MIX[1][a, b] != 0.0:
                                term = after[part][a]
                                if MIX[1][a, b] != 1.0:
                                    term = term * MIX[1][a, b]
                                total = term if total is None else total + term
                        both.append(total)
                    re, im = both
                    c, s = spin[held, 0, rows[b]], spin[held, 1, rows[b]]
                    re, im = re * c - im * s, re * s + im * c
                    spin[slot, 0, rows[b]] = re
                    if finish is None:
                        spin[slot, 1, rows[b]] = im
                    else:
                        spin[slot, 1, rows[b]], mixed[finish, rows[b]] = im - re, re + im

    def turn(slot):
        for row in range(125):
            re, im = state[0, row], state[1, row]
            c, s = spin[slot, 0, row], spin[slot, 1, row]
            state[0, row] = re * c - im * s
            state[1, row] = re * s + im * c

    def mix(axis, choose, finish):
        used = [
            [(b, choose(a, b)) for b in range(5) if MIX[0][a, b] != 0.0 or MIX[1][a, b] != 0.0]
            for a in range(5)
        ]
        for part in range(2):
            for o in range(5):
                for k in range(5):
                    rows = place(axis, o, k)
                    values = [state[part, r] for r in rows]
                    for a in range(5):
                        total = None
                        for b, coefficient in used[a]:
                            term = values[b] * coefficient
                            total = term if total is None else total + term
                        state[part, rows[a]] = finish(total)

    column = lax.broadcasted_iota(jnp.int32, (8, half), 1) + bits[0] * half
    centers = initial_centers(column)

    axis, quarter = advance()
    children = shifted(centers, axis, (1.0 - 2.0 * bits[1].astype(jnp.float32)) * quarter)
    low0, width0 = parent_low(0), 1.0 / size[0]
    low1, width1 = parent_low(1), 1.0 / size[1]
    xc = side_points(low1 + jnp.where(flag[2], width1, 0.0), width1)
    for t in range(2):
        x = [low0 + width0 * (t + 0.5)]
        old, new = radicands(centers, x, xc), radicands(children, x, xc)
        for j in range(5):
            for k, (c, s) in enumerate(pair_rotors(old(0, j), new(0, j), quarter, -sign[0])):
                row = (j * 2 + t) * 3 + k
                first_spin[0, row], first_spin[1, row] = c, s
    merged[0] += 1
    centers = children

    def pair_geometry(level_axis, centers):
        axis, quarter = advance()
        children = shifted(centers, axis, sign[1] * quarter)
        spans = []
        for k in range(2):
            low, width = box(k)
            if k == level_axis:
                low = parent_low(k) + jnp.where(flag[2], width, 0.0)
            spans.append(side_points(low, width))
        merged[level_axis] += 1
        return (centers, children, spans[0], spans[1], quarter), axis

    geometry, axis = pair_geometry(plan[1][0], centers)
    prepare_pairs(*geometry)
    later = []
    for k, level in enumerate(middle):
        side = 2.0 * bits[GATHERED + k].astype(jnp.float32) - 1.0
        centers = shifted(geometry[0], axis, side * geometry[4])
        geometry, axis = pair_geometry(level[0], centers)
        later.append(geometry)
    spot = [1, 2, 0]
    centers = geometry[1]
    upper = [bits[len(plan) - scattered + k] for k in range(scattered - 1)]
    turned = [1.0, 1.0]
    order = [list(range(5)) for _ in range(2)]
    for (axis, _), bit in zip(final, upper):
        turned[axis] = 2.0 * bit.astype(jnp.float32) - 1.0
        order[axis] = [4 - n + bit * (2 * n - 4) for n in range(5)]
    for k, level in enumerate(final):
        axis, quarter = advance()
        low0, width0 = box(0)
        low1, width1 = box(1)
        xi = side_points(low0, width0, turned[0])
        xc = side_points(low1, width1, turned[1])
        if k < scattered - 1:
            children = shifted(centers, axis, sign[spot[k + 1]] * quarter)
            prepare(1 + k, centers, children, xi, xc, quarter)
            centers = children
        else:
            for side in range(2):
                children = shifted(centers, axis, (2.0 * side - 1.0) * quarter)
                prepare(1 + k + side, centers, children, xi, xc, quarter)
        merged[level[0]] += 1
    for k in reversed(range(scattered - 1)):
        for last in range(2):
            fold(scattered + last, final[k][0], 1 + k, last if k == 0 else None)

    across = lagrange((np.arange(cx) + 0.5) / cx - 0.5)
    sums = [[None, None], [None, None], [None, None]]

    def gather_sums(row, re, im):
        whole = re + im
        row = (order[0][row // 25] * 5 + order[1][row // 5 % 5]) * 5 + row % 5
        for last in range(2):
            slot = scattered + last
            terms = whole * spin[slot, 0, row], re * spin[slot, 1, row], im * mixed[last, row]
            for which, term in enumerate(terms):
                held = sums[which][last]
                sums[which][last] = term if held is None else held + term

    def keep_state(row, re, im):
        state[0, row], state[1, row] = re, im

    emit = keep_state if middle else gather_sums
    used = [
        [
            (b, jnp.where(flag[2], MIX[1][a, b], MIX[0][a, b]).astype(jnp.float32))
            for b in range(5)
            if MIX[0][a, b] != 0.0 or MIX[1][a, b] != 0.0
        ]
        for a in range(5)
    ]
    even = [0.5 * (MIX[0][i, 2] + MIX[1][i, 2]) for i in range(3)]
    odd = [0.5 * (MIX[0][i, 2] - MIX[1][i, 2]) for i in range(3)]

    def second_level(pair, i, before):
        lo, hi = PAIRS[pair]
        turned = []
        for j in range(5):
            re, im = before[0][j], before[1][j]
            row = (i * 5 + j) * 3 + pair
            c, s = spin[0, 0, row], spin[0, 1, row]
            turned.append((re * c - im * s, re * s + im * c))
        for a in range(5):
            both = []
            for part in range(2):
                total = None
                for b, coefficient in used[a]:
                    term = turned[b][part] * coefficient
                    total = term if total is None else total + term
                both.append(total + pltpu.roll(total, 4, 0))
            row = (i * 5 + a) * 5
            if lo == hi:
                emit(row + lo, *both)
            else:
                emit(row + lo, *[jnp.where(flag[0], pltpu.roll(x, 1, 0), x) for x in both])
                emit(row + hi, *[jnp.where(flag[0], x, pltpu.roll(x, 7, 0)) for x in both])

    for pair, (lo, hi) in enumerate(PAIRS):
        wait_all(leaf_in.at[pl.ds(0, len(near) * pieces[pair][1]), :], gather_recv[pair])
        turned = []
        for t in range(2):
            across_sums = []
            for part in range(2):
                values = []
                for c in range(cx):
                    row = 2 * t * pitch + 2 * c + part
                    lines = []
                    for q in range(2):
                        first, second = [
                            jnp.broadcast_to(leaf_in[pl.ds(q * pitch + row + ORDER.index(k) * rows, 1), :], (8, half))
                            for k in (lo, hi)
                        ]
                        lines.append(first if lo == hi else jnp.where(flag[0], second, first))
                    values.append(jnp.where(flag[2], lines[1], lines[0]))
                totals = []
                for j in range(5):
                    total = values[0] * across[j, 0]
                    for c in range(1, cx):
                        total = total + values[c] * across[j, c]
                    totals.append(total)
                across_sums.append(totals)
            both = []
            for j in range(5):
                re, im = across_sums[0][j], across_sums[1][j]
                row = (j * 2 + t) * 3 + pair
                c, s = first_spin[0, row], first_spin[1, row]
                both.append((re * c - im * s, re * s + im * c))
            turned.append(both)
        plus = [[turned[0][j][p] + turned[1][j][p] for j in range(5)] for p in range(2)]
        minus = [[turned[0][j][p] - turned[1][j][p] for j in range(5)] for p in range(2)]
        for i in range(2):
            es = [[x * even[i] for x in line] for line in plus]
            os = [[x * odd[i] for x in line] for line in minus]
            second_level(pair, i, [[e + o for e, o in zip(*ls)] for ls in zip(es, os)])
            second_level(pair, 4 - i, [[e - o for e, o in zip(*ls)] for ls in zip(es, os)])
        second_level(pair, 2, [[x * even[2] for x in line] for line in plus])

    def joined(level_axis):
        turn(0)
        mix(
            level_axis,
            lambda a, b: jnp.where(flag[2], MIX[1][a, b], MIX[0][a, b]).astype(jnp.float32),
            lambda x: x + pltpu.roll(x, 4, 0),
        )

    for k, level in enumerate(middle):
        bit = bits[GATHERED + k]

        def pack(r, carry):
            mine = pl.ds(bit * 2, 1)
            theirs = pl.ds((1 - bit) * 2, 1)
            for part in range(2):
                line = pl.ds(part * 125 + r, 1)
                swap_out[k, line, :] = state[part, r, theirs, :]
                swap_in[2 * k + 1, line, :] = state[part, r, mine, :]
            return carry

        lax.fori_loop(0, 125, pack, 0)
        copy = pltpu.make_async_remote_copy(
            src_ref=swap_out.at[k],
            dst_ref=swap_in.at[2 * k],
            send_sem=swap_send.at[k],
            recv_sem=swap_recv.at[k],
            device_id=other([level]),
            device_id_type=MESH,
        )
        copy.start()
        prepare(0, *later[k])
        copy.wait()
        own_high = (sub >> 2) == bit

        def unpack(r, carry):
            for part in range(2):
                line = pl.ds(part * 125 + r, 1)
                near_line = jnp.broadcast_to(swap_in[2 * k + 1, line, :], (8, half))
                far_line = jnp.broadcast_to(swap_in[2 * k, line, :], (8, half))
                state[part, r] = jnp.where(own_high, near_line, far_line)
            return carry

        lax.fori_loop(0, 125, unpack, 0)
        joined(level[0])

    if middle:
        for row in range(125):
            gather_sums(row, state[0, row], state[1, row])
    for part in range(2):
        for side in range(2):
            first, second, third = [line[side] for line in sums]
            total = first - third if part == 0 else first + second
            part_out[pl.ds(part * 2 + side, 8, stride=8), :] = total

    def place_of(flips):
        total = 0
        for k, level in enumerate(final):
            bit = bits[len(plan) - scattered + k] ^ (1 if level in flips else 0)
            total = total + bit * (1 << spot[k])
        return pl.multiple_of(total * 8, 8)

    for k, flips in enumerate(far):
        copy = pltpu.make_async_remote_copy(
            src_ref=part_out.at[pl.ds(place_of(flips), 8), :],
            dst_ref=part_in.at[k],
            send_sem=scatter_send,
            recv_sem=scatter_recv,
            device_id=other(flips),
            device_id_type=MESH,
        )
        copy.start()
    wait_all(leaf_in.at[pl.ds(0, len(near) * pitch), :], gather_send)
    wait_all(part_in, scatter_recv)
    total = part_in[0]
    for k in range(1, len(far)):
        total = total + part_in[k]
    wait_all(part_in, scatter_send)
    for part in range(2):
        for side in range(2):
            line = part * 2 + side
            out_ref[part : part + 1, side * half : (side + 1) * half] = total[line : line + 1, :]


def shards(samples):
    counts = (lax.axis_size("inline"), lax.axis_size("xline"))
    plan = roster(*counts)
    scattered = SCATTERED
    middle = len(plan) - GATHERED - scattered
    size = samples.shape[2]
    fits = samples.shape[1] == 1 and size == 8 * LANES and NF == 2 * LANES
    fits = fits and middle >= 0 and plan[:2] == [(0, 0), (1, 0)]
    if not fits or plan[-3][0] == plan[-2][0]:
        raise ValueError("unsupported mesh")
    half = COLS // 2
    samples = samples.reshape(2, size // LANES, LANES)
    pitch = 5 * samples.shape[1]
    swaps = [
        pltpu.VMEM((middle, 256, half), jnp.float32),
        pltpu.VMEM((2 * middle, 256, half), jnp.float32),
        pltpu.SemaphoreType.DMA((middle,)),
        pltpu.SemaphoreType.DMA((middle,)),
    ]
    norm = 1.0 / math.sqrt(size * counts[0] * counts[1])
    values = pl.pallas_call(
        functools.partial(kernel, counts, scattered),
        out_shape=jax.ShapeDtypeStruct((2, COLS), jnp.float32),
        in_specs=[pl.BlockSpec(memory_space=pltpu.HBM)],
        out_specs=pl.BlockSpec(memory_space=pltpu.VMEM),
        scratch_shapes=[
            pltpu.VMEM(samples.shape, jnp.float32),
            pltpu.SemaphoreType.DMA,
            pltpu.VMEM((2, 125, 8, half), jnp.float32),
            pltpu.VMEM((2, 30, 8, half), jnp.float32),
            pltpu.VMEM((scattered + 2, 2, 125, 8, half), jnp.float32),
            pltpu.VMEM((2, 125, 8, half), jnp.float32),
            pltpu.VMEM((2 * pitch, half), jnp.float32),
            pltpu.VMEM((4 * pitch, half), jnp.float32),
            pltpu.VMEM((64, half), jnp.float32),
            pltpu.VMEM((1 << scattered, 8, half), jnp.float32),
            *[pltpu.SemaphoreType.DMA] * 6,
            *(swaps if middle else []),
        ],
        compiler_params=pltpu.CompilerParams(
            collective_id=0, has_side_effects=True, vmem_limit_bytes=20 << 20
        ),
    )(pltpu.with_memory_space_constraint(samples, pltpu.HBM))
    return values * norm


def solution(mesh):
    return jax.shard_map(
        shards,
        mesh=mesh,
        in_specs=(P(None, "inline", "xline"),),
        out_specs=P(None, ("inline", "xline")),
        check_vma=False,
    )
```

```python
import functools
import math

import jax
import jax.numpy as jnp
import numpy as np
from jax import lax
from jax.experimental import pallas as pl
from jax.experimental.pallas import tpu as pltpu
from jax.sharding import PartitionSpec as P

NF = 256
COLS = 256
KAPPA = 40.0
LANES = 128
GATHERED = 2
SCATTERED = 3
MESH = pl.DeviceIdType.MESH
PAIRS = [(0, 4), (1, 3), (2, 2)]
ORDER = [0, 4, 1, 3, 2]

NODES = np.array([0.5, 0.5 * math.sqrt(0.5), 0.0, -0.5 * math.sqrt(0.5), -0.5])


def lagrange(points):
    points = np.asarray(points, np.float64)
    rows = []
    for k in range(5):
        factor = np.ones_like(points)
        for j in range(5):
            if j != k:
                factor = factor * (points - NODES[j]) / (NODES[k] - NODES[j])
        rows.append(factor)
    table = np.stack(rows)
    return np.where(np.abs(table) < 1e-13, 0.0, table)


MIX = [lagrange((t - 0.5) / 2 + NODES / 2) for t in range(2)]


def roster(inline_count, xline_count):
    inline_bits = inline_count.bit_length() - 1
    xline_bits = xline_count.bit_length() - 1
    plan = []
    for level in range(max(inline_bits, xline_bits)):
        if level < inline_bits:
            plan.append((0, level))
        if level < xline_bits:
            plan.append((1, level))
    return plan


def split_counts():
    depth = (COLS - 1).bit_length()
    return depth, [len([j for j in range(depth) if j % 3 == axis]) for axis in range(3)]


def initial_centers(column):
    depth, _ = split_counts()
    coords = []
    for axis in range(3):
        splits = [j for j in range(depth) if j % 3 == axis]
        coord = jnp.full(column.shape, 0.5 * 0.5 ** len(splits), jnp.float32)
        for rank, j in enumerate(splits):
            digit = (column >> (depth - 1 - j)) & 1
            coord = coord + digit.astype(jnp.float32) * 0.5 ** (rank + 1)
        coords.append(coord)
    return coords


def poly(square, terms):
    total = jnp.full(square.shape, terms[-1], jnp.float32)
    for term in reversed(terms[:-1]):
        total = total * square + term
    return total


def series(limit):
    both = []
    for odd in (1, 0):
        terms = []
        while not terms or limit ** (2 * len(terms) + odd) / math.factorial(2 * len(terms) + odd) > 1e-7:
            terms.append((-1.0) ** len(terms) / math.factorial(2 * len(terms) + odd))
        both.append(terms)
    return both


def root_of(square):
    return square * lax.rsqrt(square)


def parts_of(value):
    high = value.astype(jnp.bfloat16)
    return high, (value - high.astype(jnp.float32)).astype(jnp.bfloat16)


def product(left, right):
    return jnp.dot(left, right, preferred_element_type=jnp.float32)


def small_sincos(angle, limit):
    sine, cosine = series(limit)
    square = angle * angle
    return angle * poly(square, sine), poly(square, cosine)


def turn_sincos(turns):
    half = (turns - jnp.round(turns)) * math.pi
    s, c = small_sincos(half, math.pi / 2)
    return 2.0 * s * c, 1.0 - 2.0 * s * s


def base_rotors(before, after, reach):
    gap = root_of(after) - root_of(before)
    cs, cc = small_sincos(gap * (0.5 * KAPPA), 0.5 * KAPPA * reach)
    bs, bc = small_sincos(gap * (NODES[1] * KAPPA), NODES[1] * KAPPA * reach)
    twice = cs + cs
    return (cc, cs), (bc, bs), (1.0 - twice * cs, twice * cc)


def rotors(before, after, reach):
    (cc, cs), (bc, bs), (a_c, a_s) = base_rotors(before, after, reach)
    p, q, u, v = a_c * bc, a_s * bs, a_s * bc, a_c * bs
    return [
        (a_c * cc - a_s * cs, a_s * cc + a_c * cs),
        (p - q, u + v),
        (a_c, a_s),
        (p + q, u - v),
        (cc, cs),
    ]


def pair_rotors(before, after, reach, sign):
    (cc, cs), (bc, bs), (a_c, a_s) = base_rotors(before, after, reach)
    cs, bs = cs * sign, bs * sign
    return [
        (a_c * cc - a_s * cs, a_s * cc + a_c * cs),
        (a_c * bc - a_s * bs, a_s * bc + a_c * bs),
        (a_c, a_s),
    ]


def side_points(low, width, turned=1.0):
    return [low + width * (z * turned + 0.5) for z in NODES]


def radicands(centers, xi, xc):
    anchor = 0.5 + centers[0]
    first = [anchor * anchor + centers[1] * (x * x) for x in xi]
    second = [centers[2] * (x * x) for x in xc]
    return lambda i, j: first[i] + second[j]


def shifted(centers, axis, amount):
    return [c + amount if k == axis else c for k, c in enumerate(centers)]


def leaf_sums(samples_ref, arrive, store, done, column, inline_pos, xline_pos, inline_count, xline_count):
    rows = samples_ref.shape[1]
    halves = NF // LANES
    cx = rows // halves
    fine = LANES // cx
    turn = KAPPA / (2 * math.pi)
    centers = initial_centers(column)
    anchor = 0.5 + centers[0]
    x0 = (inline_pos + 0.5) / inline_count
    roots = []
    for c in range(cx):
        x1 = (xline_pos + (c + 0.5) / cx) / xline_count
        root = root_of(anchor * anchor + centers[1] * (x0 * x0) + centers[2] * (x1 * x1))
        roots.append(root * turn)
    step = lax.broadcasted_iota(jnp.int32, (fine, COLS), 0).astype(jnp.float32) * (1.0 / NF)
    near = [turn_sincos(step * root) for root in roots]
    near = [jnp.concatenate([table[part] for table in near], axis=0) for part in range(2)]
    row = lax.broadcasted_iota(jnp.int32, (rows, COLS), 0)
    root = jnp.broadcast_to(roots[0], (rows, COLS))
    for c in range(1, cx):
        root = jnp.where(row // halves == c, roots[c], root)
    far = []
    for d in range(cx):
        start = row % halves * LANES + (row // halves + cx - d) % cx * fine
        far.append(turn_sincos(root * (0.5 + (start.astype(jnp.float32) + 0.5) / NF)))
    row = lax.broadcasted_iota(jnp.int32, (rows, LANES), 0)
    lane = lax.broadcasted_iota(jnp.int32, (rows, LANES), 1)
    mask = lane // fine == row // halves
    basis = []
    for d in range(cx):
        spot = row % halves * LANES + (row // halves + cx - d) % cx * fine + lane % fine
        z = (spot.astype(jnp.float32) + 0.5) / NF - 0.5
        line = []
        for k in range(5):
            factor = None
            for j in range(5):
                if j != k:
                    term = (z - NODES[j]) * (1.0 / (NODES[k] - NODES[j]))
                    factor = term if factor is None else factor * term
            line.append(jnp.where(mask, factor, 0.0))
        basis.append(line)
    odd = row % 2 == 1
    width = COLS // 2
    tables = []
    for side in range(2):
        lanes = slice(side * width, (side + 1) * width)
        high, low = parts_of(jnp.concatenate([near[1][:, lanes], near[0][:, lanes]], axis=1))
        tables.append((jnp.concatenate([high, high], axis=0), low))
    arrive()
    moved = [
        [samples_ref[part] if d == 0 else pltpu.roll(samples_ref[part], d * fine, 1) for d in range(cx)]
        for part in range(2)
    ]
    left = [moved[part][d] * basis[d][k] for k in ORDER for part in range(2) for d in range(cx)]
    high, low = parts_of(jnp.concatenate(left, axis=0))
    both = jnp.concatenate([high, low], axis=1)
    cut = 4 * cx * rows
    for side in range(2):
        lanes = slice(side * width, (side + 1) * width)
        made = [
            product(both[part], tables[side][0]) + product(high[part], tables[side][1])
            for part in (slice(0, cut), slice(cut, None))
        ]
        for spot in range(5):
            sums = [None, None]
            for d in range(cx):
                start = (spot * 2 * cx + d) * rows
                half = made[start >= cut]
                start = start - cut if start >= cut else start
                re = half[start : start + rows]
                im = half[start + cx * rows : start + (cx + 1) * rows]
                r, i = re[:, :width] - im[:, width:], re[:, width:] + im[:, :width]
                hs, hc = far[d][0][:, lanes], far[d][1][:, lanes]
                for part, term in enumerate((r * hc - i * hs, i * hc + r * hs)):
                    sums[part] = term if sums[part] is None else sums[part] + term
            re, im = sums
            pair = jnp.where(odd, im + pltpu.roll(im, 1, 0), re + pltpu.roll(re, rows - 1, 0))
            store(side, spot, pair)
        done(side)


def wait_all(ref, sem):
    pltpu.make_async_copy(ref, ref, sem).wait()


def kernel(
    counts,
    scattered,
    samples_hbm,
    out_ref,
    samples_ref,
    fetch_sem,
    state,
    first_spin,
    spin,
    mixed,
    leaf_out,
    leaf_in,
    part_out,
    part_in,
    send_sem,
    gather_recv_0,
    gather_recv_1,
    gather_recv_2,
    scatter_recv,
    swap_out=None,
    swap_in=None,
    swap_send=None,
    swap_recv=None,
):
    gather_recv = (gather_recv_0, gather_recv_1, gather_recv_2)
    fetch = pltpu.make_async_copy(samples_hbm, samples_ref, fetch_sem)
    fetch.start()
    rows = samples_ref.shape[1]
    cx = rows * LANES // NF
    pitch = 5 * rows
    index = (lax.axis_index("inline"), lax.axis_index("xline"))
    plan = roster(*counts)
    middle = plan[GATHERED : len(plan) - scattered]
    final = plan[len(plan) - scattered :]
    bits = [(index[axis] >> place) & 1 for axis, place in plan]
    size = [c * 1.0 for c in counts]

    def other(flips):
        target = list(index)
        for axis, place in flips:
            target[axis] = target[axis] ^ (1 << place)
        return tuple(target)

    def subsets(levels):
        return [
            [level for k, level in enumerate(levels) if pattern >> k & 1]
            for pattern in range(1, 1 << len(levels))
        ]

    near = sorted(subsets(plan[:GATHERED]), key=lambda flips: plan[0] not in flips)
    far = [[plan[1]] + flips for flips in [[]] + subsets(final)][::-1]
    calls = near + [f for f in far if f not in near] + [[level] for level in middle]
    partners = [other(f) for f in calls]
    barrier = pltpu.get_barrier_semaphore()
    for partner in partners:
        pl.semaphore_signal(barrier, inc=1, device_id=partner, device_id_type=MESH)

    half = COLS // 2
    own_slot = bits[0] * 2 + bits[1]
    own_row = own_slot * pitch

    def keep(side, spot, value):
        row = side * pitch + spot * rows
        leaf_out[row : row + rows, :] = value

    def send(side):
        if side == 0:
            pl.semaphore_wait(barrier, len(partners))
            lax.fori_loop(0, 1 + jnp.minimum(index[0], 0), first_copies, 0)
        else:
            start_copies(1)

    def first_copies(_, carry):
        start_copies(0)
        return carry

    def start_copies(side):
        for (start, length), sem in zip(pieces, gather_recv):
            for flips in near:
                if (plan[0] in flips) == (side == 0):
                    pltpu.make_async_remote_copy(
                        src_ref=leaf_out.at[pl.ds(side * pitch + start, length), :],
                        dst_ref=leaf_in.at[pl.ds(pl.multiple_of(own_row + start, 8), length), :],
                        send_sem=send_sem,
                        recv_sem=sem,
                        device_id=other(flips),
                        device_id_type=MESH,
                    ).start()

    pieces = [(0, 2 * rows), (2 * rows, 2 * rows), (4 * rows, rows)]
    lane = lax.broadcasted_iota(jnp.int32, (1, COLS), 1)
    column = lane % half + half * jnp.where(lane < half, 1 - bits[0], bits[0])
    position = [i.astype(jnp.float32) for i in index]
    leaf_sums(samples_ref, fetch.wait, keep, send, column, position[0], position[1], size[0], size[1])
    leaf_in[pl.ds(pl.multiple_of(own_row, 8), pitch), :] = leaf_out[pl.ds(pitch, pitch), :]

    sub = lax.broadcasted_iota(jnp.int32, (8, half), 0)
    flag = [((sub >> k) & 1) == 1 for k in range(3)]
    sign = [jnp.where(f, 1.0, -1.0) for f in flag]
    depth, splits = split_counts()
    merged = [0, 0]

    def advance():
        nonlocal depth
        axis = depth % 3
        quarter = 0.25 * 0.5 ** splits[axis]
        splits[axis] += 1
        depth += 1
        return axis, quarter

    def box(axis):
        width = 2.0 ** merged[axis] / size[axis]
        low = ((index[axis] >> merged[axis]) << merged[axis]).astype(jnp.float32) / size[axis]
        return low, width

    def parent_low(axis):
        up = merged[axis] + 1
        return ((index[axis] >> up) << up).astype(jnp.float32) / size[axis]

    def prepare(slot, centers, children, xi, xc, reach):
        old, new = radicands(centers, xi, xc), radicands(children, xi, xc)
        for i in range(5):
            for j in range(5):
                for k, (c, s) in enumerate(rotors(old(i, j), new(i, j), reach)):
                    row = (i * 5 + j) * 5 + k
                    spin[slot, 0, row], spin[slot, 1, row] = c, s

    def prepare_pairs(centers, children, xi, xc, reach):
        old, new = radicands(centers, xi, xc), radicands(children, xi, xc)
        for i in range(5):
            for j in range(5):
                for k, (c, s) in enumerate(pair_rotors(old(i, j), new(i, j), reach, -sign[0])):
                    row = (i * 5 + j) * 3 + k
                    spin[0, 0, row], spin[0, 1, row] = c, s

    def place(axis, o, k):
        return [((a * 5 + o) if axis == 0 else (o * 5 + a)) * 5 + k for a in range(5)]

    def fold(slot, axis, held, finish):
        for o in range(5):
            for k in range(5):
                rows = place(axis, o, k)
                after = [[spin[slot, part, r] for r in rows] for part in range(2)]
                for b in range(5):
                    both = []
                    for part in range(2):
                        total = None
                        for a in range(5):
                            if MIX[1][a, b] != 0.0:
                                term = after[part][a]
                                if MIX[1][a, b] != 1.0:
                                    term = term * MIX[1][a, b]
                                total = term if total is None else total + term
                        both.append(total)
                    re, im = both
                    c, s = spin[held, 0, rows[b]], spin[held, 1, rows[b]]
                    re, im = re * c - im * s, re * s + im * c
                    spin[slot, 0, rows[b]] = re
                    if finish is None:
                        spin[slot, 1, rows[b]] = im
                    else:
                        spin[slot, 1, rows[b]], mixed[finish, rows[b]] = im - re, re + im

    def turn(slot):
        for row in range(125):
            re, im = state[0, row], state[1, row]
            c, s = spin[slot, 0, row], spin[slot, 1, row]
            state[0, row] = re * c - im * s
            state[1, row] = re * s + im * c

    def mix(axis, choose, finish):
        used = [
            [(b, choose(a, b)) for b in range(5) if MIX[0][a, b] != 0.0 or MIX[1][a, b] != 0.0]
            for a in range(5)
        ]
        for part in range(2):
            for o in range(5):
                for k in range(5):
                    rows = place(axis, o, k)
                    values = [state[part, r] for r in rows]
                    for a in range(5):
                        total = None
                        for b, coefficient in used[a]:
                            term = values[b] * coefficient
                            total = term if total is None else total + term
                        state[part, rows[a]] = finish(total)

    column = lax.broadcasted_iota(jnp.int32, (8, half), 1) + bits[0] * half
    centers = initial_centers(column)

    axis, quarter = advance()
    children = shifted(centers, axis, (1.0 - 2.0 * bits[1].astype(jnp.float32)) * quarter)
    low0, width0 = parent_low(0), 1.0 / size[0]
    low1, width1 = parent_low(1), 1.0 / size[1]
    xc = side_points(low1 + jnp.where(flag[2], width1, 0.0), width1)
    for t in range(2):
        x = [low0 + width0 * (t + 0.5)]
        old, new = radicands(centers, x, xc), radicands(children, x, xc)
        for j in range(5):
            for k, (c, s) in enumerate(pair_rotors(old(0, j), new(0, j), quarter, -sign[0])):
                row = (j * 2 + t) * 3 + k
                first_spin[0, row], first_spin[1, row] = c, s
    merged[0] += 1
    centers = children

    def pair_geometry(level_axis, centers):
        axis, quarter = advance()
        children = shifted(centers, axis, sign[1] * quarter)
        spans = []
        for k in range(2):
            low, width = box(k)
            if k == level_axis:
                low = parent_low(k) + jnp.where(flag[2], width, 0.0)
            spans.append(side_points(low, width))
        merged[level_axis] += 1
        return (centers, children, spans[0], spans[1], quarter), axis

    geometry, axis = pair_geometry(plan[1][0], centers)
    prepare_pairs(*geometry)
    later = []
    for k, level in enumerate(middle):
        side = 2.0 * bits[GATHERED + k].astype(jnp.float32) - 1.0
        centers = shifted(geometry[0], axis, side * geometry[4])
        geometry, axis = pair_geometry(level[0], centers)
        later.append(geometry)
    spot = [1, 2, 0]
    centers = geometry[1]
    upper = [bits[len(plan) - scattered + k] for k in range(scattered - 1)]
    turned = [1.0, 1.0]
    order = [list(range(5)) for _ in range(2)]
    for (axis, _), bit in zip(final, upper):
        turned[axis] = 2.0 * bit.astype(jnp.float32) - 1.0
        order[axis] = [4 - n + bit * (2 * n - 4) for n in range(5)]
    for k, level in enumerate(final):
        axis, quarter = advance()
        low0, width0 = box(0)
        low1, width1 = box(1)
        xi = side_points(low0, width0, turned[0])
        xc = side_points(low1, width1, turned[1])
        if k < scattered - 1:
            children = shifted(centers, axis, sign[spot[k + 1]] * quarter)
            prepare(1 + k, centers, children, xi, xc, quarter)
            centers = children
        else:
            for side in range(2):
                children = shifted(centers, axis, (2.0 * side - 1.0) * quarter)
                prepare(1 + k + side, centers, children, xi, xc, quarter)
        merged[level[0]] += 1
    for k in reversed(range(scattered - 1)):
        for last in range(2):
            fold(scattered + last, final[k][0], 1 + k, last if k == 0 else None)

    across = lagrange((np.arange(cx) + 0.5) / cx - 0.5)
    sums = [[None, None], [None, None], [None, None]]

    def gather_sums(row, re, im):
        whole = re + im
        row = (order[0][row // 25] * 5 + order[1][row // 5 % 5]) * 5 + row % 5
        for last in range(2):
            slot = scattered + last
            terms = whole * spin[slot, 0, row], re * spin[slot, 1, row], im * mixed[last, row]
            for which, term in enumerate(terms):
                held = sums[which][last]
                sums[which][last] = term if held is None else held + term

    def keep_state(row, re, im):
        state[0, row], state[1, row] = re, im

    emit = keep_state if middle else gather_sums
    used = [
        [
            (b, jnp.where(flag[2], MIX[1][a, b], MIX[0][a, b]).astype(jnp.float32))
            for b in range(5)
            if MIX[0][a, b] != 0.0 or MIX[1][a, b] != 0.0
        ]
        for a in range(5)
    ]
    even = [0.5 * (MIX[0][i, 2] + MIX[1][i, 2]) for i in range(3)]
    odd = [0.5 * (MIX[0][i, 2] - MIX[1][i, 2]) for i in range(3)]

    def second_level(pair, i, before):
        lo, hi = PAIRS[pair]
        turned = []
        for j in range(5):
            re, im = before[0][j], before[1][j]
            row = (i * 5 + j) * 3 + pair
            c, s = spin[0, 0, row], spin[0, 1, row]
            turned.append((re * c - im * s, re * s + im * c))
        for a in range(5):
            both = []
            for part in range(2):
                total = None
                for b, coefficient in used[a]:
                    term = turned[b][part] * coefficient
                    total = term if total is None else total + term
                both.append(total + pltpu.roll(total, 4, 0))
            row = (i * 5 + a) * 5
            if lo == hi:
                emit(row + lo, *both)
            else:
                emit(row + lo, *[jnp.where(flag[0], pltpu.roll(x, 1, 0), x) for x in both])
                emit(row + hi, *[jnp.where(flag[0], x, pltpu.roll(x, 7, 0)) for x in both])

    for pair, (lo, hi) in enumerate(PAIRS):
        wait_all(leaf_in.at[pl.ds(0, len(near) * pieces[pair][1]), :], gather_recv[pair])
        turned = []
        for t in range(2):
            across_sums = []
            for part in range(2):
                values = []
                for c in range(cx):
                    row = 2 * t * pitch + 2 * c + part
                    lines = []
                    for q in range(2):
                        first, second = [
                            jnp.broadcast_to(leaf_in[pl.ds(q * pitch + row + ORDER.index(k) * rows, 1), :], (8, half))
                            for k in (lo, hi)
                        ]
                        lines.append(first if lo == hi else jnp.where(flag[0], second, first))
                    values.append(jnp.where(flag[2], lines[1], lines[0]))
                totals = []
                for j in range(5):
                    total = values[0] * across[j, 0]
                    for c in range(1, cx):
                        total = total + values[c] * across[j, c]
                    totals.append(total)
                across_sums.append(totals)
            both = []
            for j in range(5):
                re, im = across_sums[0][j], across_sums[1][j]
                row = (j * 2 + t) * 3 + pair
                c, s = first_spin[0, row], first_spin[1, row]
                both.append((re * c - im * s, re * s + im * c))
            turned.append(both)
        plus = [[turned[0][j][p] + turned[1][j][p] for j in range(5)] for p in range(2)]
        minus = [[turned[0][j][p] - turned[1][j][p] for j in range(5)] for p in range(2)]
        for i in range(2):
            es = [[x * even[i] for x in line] for line in plus]
            os = [[x * odd[i] for x in line] for line in minus]
            second_level(pair, i, [[e + o for e, o in zip(*ls)] for ls in zip(es, os)])
            second_level(pair, 4 - i, [[e - o for e, o in zip(*ls)] for ls in zip(es, os)])
        second_level(pair, 2, [[x * even[2] for x in line] for line in plus])

    def joined(level_axis):
        turn(0)
        mix(
            level_axis,
            lambda a, b: jnp.where(flag[2], MIX[1][a, b], MIX[0][a, b]).astype(jnp.float32),
            lambda x: x + pltpu.roll(x, 4, 0),
        )

    for k, level in enumerate(middle):
        bit = bits[GATHERED + k]

        def pack(r, carry):
            mine = pl.ds(bit * 2, 1)
            theirs = pl.ds((1 - bit) * 2, 1)
            for part in range(2):
                line = pl.ds(part * 125 + r, 1)
                swap_out[k, line, :] = state[part, r, theirs, :]
                swap_in[2 * k + 1, line, :] = state[part, r, mine, :]
            return carry

        lax.fori_loop(0, 125, pack, 0)
        copy = pltpu.make_async_remote_copy(
            src_ref=swap_out.at[k],
            dst_ref=swap_in.at[2 * k],
            send_sem=swap_send.at[k],
            recv_sem=swap_recv.at[k],
            device_id=other([level]),
            device_id_type=MESH,
        )
        copy.start()
        prepare(0, *later[k])
        copy.wait()
        own_high = (sub >> 2) == bit

        def unpack(r, carry):
            for part in range(2):
                line = pl.ds(part * 125 + r, 1)
                near_line = jnp.broadcast_to(swap_in[2 * k + 1, line, :], (8, half))
                far_line = jnp.broadcast_to(swap_in[2 * k, line, :], (8, half))
                state[part, r] = jnp.where(own_high, near_line, far_line)
            return carry

        lax.fori_loop(0, 125, unpack, 0)
        joined(level[0])

    if middle:
        for row in range(125):
            gather_sums(row, state[0, row], state[1, row])
    for part in range(2):
        for side in range(2):
            first, second, third = [line[side] for line in sums]
            total = first - third if part == 0 else first + second
            part_out[pl.ds(part * 2 + side, 8, stride=8), :] = total

    def place_of(flips):
        total = 0
        for k, level in enumerate(final):
            bit = bits[len(plan) - scattered + k] ^ (1 if level in flips else 0)
            total = total + bit * (1 << spot[k])
        return pl.multiple_of(total * 8, 8)

    for k, flips in enumerate(far):
        copy = pltpu.make_async_remote_copy(
            src_ref=part_out.at[pl.ds(place_of(flips), 4), :],
            dst_ref=part_in.at[k],
            send_sem=send_sem,
            recv_sem=scatter_recv,
            device_id=other(flips),
            device_id_type=MESH,
        )
        copy.start()
    wait_all(part_in, scatter_recv)
    total = part_in[0]
    for k in range(1, len(far)):
        total = total + part_in[k]
    wait_all(leaf_in.at[pl.ds(0, len(near) * pitch + 4 * len(far)), :], send_sem)
    for part in range(2):
        for side in range(2):
            line = part * 2 + side
            out_ref[part : part + 1, side * half : (side + 1) * half] = total[line : line + 1, :]


def shards(samples):
    counts = (lax.axis_size("inline"), lax.axis_size("xline"))
    plan = roster(*counts)
    scattered = SCATTERED
    middle = len(plan) - GATHERED - scattered
    size = samples.shape[2]
    fits = samples.shape[1] == 1 and size == 8 * LANES and NF == 2 * LANES
    fits = fits and middle >= 0 and plan[:2] == [(0, 0), (1, 0)]
    if not fits or plan[-3][0] == plan[-2][0]:
        raise ValueError("unsupported mesh")
    half = COLS // 2
    samples = samples.reshape(2, size // LANES, LANES)
    pitch = 5 * samples.shape[1]
    swaps = [
        pltpu.VMEM((middle, 256, half), jnp.float32),
        pltpu.VMEM((2 * middle, 256, half), jnp.float32),
        pltpu.SemaphoreType.DMA((middle,)),
        pltpu.SemaphoreType.DMA((middle,)),
    ]
    norm = 1.0 / math.sqrt(size * counts[0] * counts[1])
    values = pl.pallas_call(
        functools.partial(kernel, counts, scattered),
        out_shape=jax.ShapeDtypeStruct((2, COLS), jnp.float32),
        in_specs=[pl.BlockSpec(memory_space=pltpu.HBM)],
        out_specs=pl.BlockSpec(memory_space=pltpu.VMEM),
        scratch_shapes=[
            pltpu.VMEM(samples.shape, jnp.float32),
            pltpu.SemaphoreType.DMA,
            pltpu.VMEM((2, 125, 8, half), jnp.float32),
            pltpu.VMEM((2, 30, 8, half), jnp.float32),
            pltpu.VMEM((scattered + 2, 2, 125, 8, half), jnp.float32),
            pltpu.VMEM((2, 125, 8, half), jnp.float32),
            pltpu.VMEM((2 * pitch, half), jnp.float32),
            pltpu.VMEM((4 * pitch, half), jnp.float32),
            pltpu.VMEM((64, half), jnp.float32),
            pltpu.VMEM((1 << scattered, 4, half), jnp.float32),
            *[pltpu.SemaphoreType.DMA] * 5,
            *(swaps if middle else []),
        ],
        compiler_params=pltpu.CompilerParams(
            collective_id=0, has_side_effects=True, vmem_limit_bytes=20 << 20
        ),
    )(pltpu.with_memory_space_constraint(samples, pltpu.HBM))
    return values * norm


def solution(mesh):
    return jax.shard_map(
        shards,
        mesh=mesh,
        in_specs=(P(None, "inline", "xline"),),
        out_specs=P(None, ("inline", "xline")),
        check_vma=False,
    )
```

```python
import functools
import math

import jax
import jax.numpy as jnp
import numpy as np
from jax import lax
from jax.experimental import pallas as pl
from jax.experimental.pallas import tpu as pltpu
from jax.sharding import PartitionSpec as P

NF = 256
COLS = 256
KAPPA = 40.0
LANES = 128
GATHERED = 2
SCATTERED = 3
MESH = pl.DeviceIdType.MESH
PAIRS = [(0, 4), (1, 3), (2, 2)]
ORDER = [0, 4, 1, 3, 2]

NODES = np.array([0.5, 0.5 * math.sqrt(0.5), 0.0, -0.5 * math.sqrt(0.5), -0.5])


def lagrange(points):
    points = np.asarray(points, np.float64)
    rows = []
    for k in range(5):
        factor = np.ones_like(points)
        for j in range(5):
            if j != k:
                factor = factor * (points - NODES[j]) / (NODES[k] - NODES[j])
        rows.append(factor)
    table = np.stack(rows)
    return np.where(np.abs(table) < 1e-13, 0.0, table)


MIX = [lagrange((t - 0.5) / 2 + NODES / 2) for t in range(2)]


def roster(inline_count, xline_count):
    inline_bits = inline_count.bit_length() - 1
    xline_bits = xline_count.bit_length() - 1
    plan = []
    for level in range(max(inline_bits, xline_bits)):
        if level < inline_bits:
            plan.append((0, level))
        if level < xline_bits:
            plan.append((1, level))
    return plan


def split_counts():
    depth = (COLS - 1).bit_length()
    return depth, [len([j for j in range(depth) if j % 3 == axis]) for axis in range(3)]


def initial_centers(column):
    depth, _ = split_counts()
    coords = []
    for axis in range(3):
        splits = [j for j in range(depth) if j % 3 == axis]
        coord = jnp.full(column.shape, 0.5 * 0.5 ** len(splits), jnp.float32)
        for rank, j in enumerate(splits):
            digit = (column >> (depth - 1 - j)) & 1
            coord = coord + digit.astype(jnp.float32) * 0.5 ** (rank + 1)
        coords.append(coord)
    return coords


def poly(square, terms):
    total = jnp.full(square.shape, terms[-1], jnp.float32)
    for term in reversed(terms[:-1]):
        total = total * square + term
    return total


def series(limit):
    both = []
    for odd in (1, 0):
        terms = []
        while not terms or limit ** (2 * len(terms) + odd) / math.factorial(2 * len(terms) + odd) > 1e-7:
            terms.append((-1.0) ** len(terms) / math.factorial(2 * len(terms) + odd))
        both.append(terms)
    return both


def root_of(square):
    return square * lax.rsqrt(square)


def parts_of(value):
    high = value.astype(jnp.bfloat16)
    return high, (value - high.astype(jnp.float32)).astype(jnp.bfloat16)


def product(left, right):
    return jnp.dot(left, right, preferred_element_type=jnp.float32)


def small_sincos(angle, limit):
    sine, cosine = series(limit)
    square = angle * angle
    return angle * poly(square, sine), poly(square, cosine)


def turn_sincos(turns):
    half = (turns - jnp.round(turns)) * math.pi
    s, c = small_sincos(half, math.pi / 2)
    return 2.0 * s * c, 1.0 - 2.0 * s * s


def base_rotors(before, after, reach):
    gap = root_of(after) - root_of(before)
    cs, cc = small_sincos(gap * (0.5 * KAPPA), 0.5 * KAPPA * reach)
    bs, bc = small_sincos(gap * (NODES[1] * KAPPA), NODES[1] * KAPPA * reach)
    twice = cs + cs
    return (cc, cs), (bc, bs), (1.0 - twice * cs, twice * cc)


def rotors(before, after, reach):
    (cc, cs), (bc, bs), (a_c, a_s) = base_rotors(before, after, reach)
    p, q, u, v = a_c * bc, a_s * bs, a_s * bc, a_c * bs
    return [
        (a_c * cc - a_s * cs, a_s * cc + a_c * cs),
        (p - q, u + v),
        (a_c, a_s),
        (p + q, u - v),
        (cc, cs),
    ]


def pair_rotors(before, after, reach, sign):
    (cc, cs), (bc, bs), (a_c, a_s) = base_rotors(before, after, reach)
    cs, bs = cs * sign, bs * sign
    return [
        (a_c * cc - a_s * cs, a_s * cc + a_c * cs),
        (a_c * bc - a_s * bs, a_s * bc + a_c * bs),
        (a_c, a_s),
    ]


def side_points(low, width, turned=1.0):
    return [low + width * (z * turned + 0.5) for z in NODES]


def radicands(centers, xi, xc):
    anchor = 0.5 + centers[0]
    first = [anchor * anchor + centers[1] * (x * x) for x in xi]
    second = [centers[2] * (x * x) for x in xc]
    return lambda i, j: first[i] + second[j]


def shifted(centers, axis, amount):
    return [c + amount if k == axis else c for k, c in enumerate(centers)]


def leaf_sums(samples_ref, arrive, store, done, column, inline_pos, xline_pos, inline_count, xline_count):
    rows = samples_ref.shape[1]
    halves = NF // LANES
    cx = rows // halves
    fine = LANES // cx
    turn = KAPPA / (2 * math.pi)
    centers = initial_centers(column)
    anchor = 0.5 + centers[0]
    x0 = (inline_pos + 0.5) / inline_count
    roots = []
    for c in range(cx):
        x1 = (xline_pos + (c + 0.5) / cx) / xline_count
        root = root_of(anchor * anchor + centers[1] * (x0 * x0) + centers[2] * (x1 * x1))
        roots.append(root * turn)
    step = lax.broadcasted_iota(jnp.int32, (fine, COLS), 0).astype(jnp.float32) * (1.0 / NF)
    near = [turn_sincos(step * root) for root in roots]
    near = [jnp.concatenate([table[part] for table in near], axis=0) for part in range(2)]
    row = lax.broadcasted_iota(jnp.int32, (rows, COLS), 0)
    root = jnp.broadcast_to(roots[0], (rows, COLS))
    for c in range(1, cx):
        root = jnp.where(row // halves == c, roots[c], root)
    far = []
    for d in range(cx):
        start = row % halves * LANES + (row // halves + cx - d) % cx * fine
        far.append(turn_sincos(root * (0.5 + (start.astype(jnp.float32) + 0.5) / NF)))
    row = lax.broadcasted_iota(jnp.int32, (rows, LANES), 0)
    lane = lax.broadcasted_iota(jnp.int32, (rows, LANES), 1)
    mask = lane // fine == row // halves
    basis = []
    for d in range(cx):
        spot = row % halves * LANES + (row // halves + cx - d) % cx * fine + lane % fine
        z = (spot.astype(jnp.float32) + 0.5) / NF - 0.5
        line = []
        for k in range(5):
            factor = None
            for j in range(5):
                if j != k:
                    term = (z - NODES[j]) * (1.0 / (NODES[k] - NODES[j]))
                    factor = term if factor is None else factor * term
            line.append(jnp.where(mask, factor, 0.0))
        basis.append(line)
    odd = row % 2 == 1
    width = COLS // 2
    tables = []
    for side in range(2):
        lanes = slice(side * width, (side + 1) * width)
        high, low = parts_of(jnp.concatenate([near[1][:, lanes], near[0][:, lanes]], axis=1))
        tables.append((jnp.concatenate([high, high], axis=0), low))
    arrive()
    moved = [
        [samples_ref[part] if d == 0 else pltpu.roll(samples_ref[part], d * fine, 1) for d in range(cx)]
        for part in range(2)
    ]
    left = [moved[part][d] * basis[d][k] for k in ORDER for part in range(2) for d in range(cx)]
    high, low = parts_of(jnp.concatenate(left, axis=0))
    both = jnp.concatenate([high, low], axis=1)
    cut = 4 * cx * rows
    for side in range(2):
        lanes = slice(side * width, (side + 1) * width)
        made = [
            product(both[part], tables[side][0]) + product(high[part], tables[side][1])
            for part in (slice(0, cut), slice(cut, None))
        ]
        for spot in range(5):
            sums = [None, None]
            for d in range(cx):
                start = (spot * 2 * cx + d) * rows
                half = made[start >= cut]
                start = start - cut if start >= cut else start
                re = half[start : start + rows]
                im = half[start + cx * rows : start + (cx + 1) * rows]
                r, i = re[:, :width] - im[:, width:], re[:, width:] + im[:, :width]
                hs, hc = far[d][0][:, lanes], far[d][1][:, lanes]
                for part, term in enumerate((r * hc - i * hs, i * hc + r * hs)):
                    sums[part] = term if sums[part] is None else sums[part] + term
            re, im = sums
            pair = jnp.where(odd, im + pltpu.roll(im, 1, 0), re + pltpu.roll(re, rows - 1, 0))
            store(side, spot, pair)
        done(side)


def wait_all(ref, sem):
    pltpu.make_async_copy(ref, ref, sem).wait()


def kernel(
    counts,
    scattered,
    samples_hbm,
    out_ref,
    samples_ref,
    fetch_sem,
    state,
    first_spin,
    own_first,
    spin,
    mixed,
    leaf_out,
    leaf_in,
    part_out,
    part_in,
    send_sem,
    gather_recv_0,
    gather_recv_1,
    gather_recv_2,
    core_recv,
    scatter_recv,
    swap_out=None,
    swap_in=None,
    swap_send=None,
    swap_recv=None,
):
    gather_recv = (gather_recv_0, gather_recv_1, gather_recv_2)
    fetch = pltpu.make_async_copy(samples_hbm, samples_ref, fetch_sem)
    fetch.start()
    rows = samples_ref.shape[1]
    cx = rows * LANES // NF
    pitch = 5 * rows
    index = (lax.axis_index("inline"), lax.axis_index("xline"))
    plan = roster(*counts)
    middle = plan[GATHERED : len(plan) - scattered]
    final = plan[len(plan) - scattered :]
    bits = [(index[axis] >> place) & 1 for axis, place in plan]
    size = [c * 1.0 for c in counts]

    def other(flips):
        target = list(index)
        for axis, place in flips:
            target[axis] = target[axis] ^ (1 << place)
        return tuple(target)

    def subsets(levels):
        return [
            [level for k, level in enumerate(levels) if pattern >> k & 1]
            for pattern in range(1, 1 << len(levels))
        ]

    near = sorted(subsets(plan[:GATHERED]), key=lambda flips: plan[0] not in flips)
    far = [[plan[1]] + flips for flips in [[]] + subsets(final)][::-1]
    calls = near + [f for f in far if f not in near] + [[level] for level in middle]
    partners = [other(f) for f in calls]
    barrier = pltpu.get_barrier_semaphore()
    for partner in partners:
        pl.semaphore_signal(barrier, inc=1, device_id=partner, device_id_type=MESH)

    half = COLS // 2

    def keep(side, spot, value):
        row = side * pitch + spot * rows
        leaf_out[row : row + rows, :] = value

    def send(side):
        if side == 0:
            pl.semaphore_wait(barrier, len(partners))
            lax.fori_loop(0, 1 + jnp.minimum(index[0], 0), first_copies, 0)
        else:
            start_copies(1)

    def first_copies(_, carry):
        start_copies(0)
        return carry

    def start_copies(side):
        whole = [((0, pitch), core_recv)]
        for (start, length), sem in zip(pieces, gather_recv) if side == 0 else whole:
            for flips in near:
                if (plan[0] in flips) == (side == 0):
                    pltpu.make_async_remote_copy(
                        src_ref=leaf_out.at[pl.ds(side * pitch + start, length), :],
                        dst_ref=leaf_in.at[
                            bits[0], pl.ds(pl.multiple_of(bits[1] * pitch + start, 8), length), :
                        ],
                        send_sem=send_sem,
                        recv_sem=sem,
                        device_id=other(flips),
                        device_id_type=MESH,
                    ).start()

    pieces = [(0, 2 * rows), (2 * rows, 2 * rows), (4 * rows, rows)]
    lane = lax.broadcasted_iota(jnp.int32, (1, COLS), 1)
    column = lane % half + half * jnp.where(lane < half, 1 - bits[0], bits[0])
    position = [i.astype(jnp.float32) for i in index]
    leaf_sums(samples_ref, fetch.wait, keep, send, column, position[0], position[1], size[0], size[1])
    own_row = pl.multiple_of(bits[1] * pitch, 8)
    leaf_in[bits[0], pl.ds(own_row, pitch), :] = leaf_out[pl.ds(pitch, pitch), :]

    sub = lax.broadcasted_iota(jnp.int32, (8, half), 0)
    flag = [((sub >> k) & 1) == 1 for k in range(3)]
    sign = [jnp.where(f, 1.0, -1.0) for f in flag]
    depth, splits = split_counts()
    merged = [0, 0]

    def advance():
        nonlocal depth
        axis = depth % 3
        quarter = 0.25 * 0.5 ** splits[axis]
        splits[axis] += 1
        depth += 1
        return axis, quarter

    def box(axis):
        width = 2.0 ** merged[axis] / size[axis]
        low = ((index[axis] >> merged[axis]) << merged[axis]).astype(jnp.float32) / size[axis]
        return low, width

    def parent_low(axis):
        up = merged[axis] + 1
        return ((index[axis] >> up) << up).astype(jnp.float32) / size[axis]

    def prepare(slot, centers, children, xi, xc, reach):
        old, new = radicands(centers, xi, xc), radicands(children, xi, xc)
        for i in range(5):
            for j in range(5):
                for k, (c, s) in enumerate(rotors(old(i, j), new(i, j), reach)):
                    row = (i * 5 + j) * 5 + k
                    spin[slot, 0, row], spin[slot, 1, row] = c, s

    def prepare_pairs(centers, children, xi, xc, reach):
        old, new = radicands(centers, xi, xc), radicands(children, xi, xc)
        for i in range(5):
            for j in range(5):
                for k, (c, s) in enumerate(pair_rotors(old(i, j), new(i, j), reach, -sign[0])):
                    row = (i * 5 + j) * 3 + k
                    spin[0, 0, row], spin[0, 1, row] = c, s

    def place(axis, o, k):
        return [((a * 5 + o) if axis == 0 else (o * 5 + a)) * 5 + k for a in range(5)]

    def fold(slot, axis, held, finish):
        for o in range(5):
            for k in range(5):
                rows = place(axis, o, k)
                after = [[spin[slot, part, r] for r in rows] for part in range(2)]
                for b in range(5):
                    both = []
                    for part in range(2):
                        total = None
                        for a in range(5):
                            if MIX[1][a, b] != 0.0:
                                term = after[part][a]
                                if MIX[1][a, b] != 1.0:
                                    term = term * MIX[1][a, b]
                                total = term if total is None else total + term
                        both.append(total)
                    re, im = both
                    c, s = spin[held, 0, rows[b]], spin[held, 1, rows[b]]
                    re, im = re * c - im * s, re * s + im * c
                    spin[slot, 0, rows[b]] = re
                    if finish is None:
                        spin[slot, 1, rows[b]] = im
                    else:
                        spin[slot, 1, rows[b]], mixed[finish, rows[b]] = im - re, re + im

    def turn(slot):
        for row in range(125):
            re, im = state[0, row], state[1, row]
            c, s = spin[slot, 0, row], spin[slot, 1, row]
            state[0, row] = re * c - im * s
            state[1, row] = re * s + im * c

    def mix(axis, choose, finish):
        used = [
            [(b, choose(a, b)) for b in range(5) if MIX[0][a, b] != 0.0 or MIX[1][a, b] != 0.0]
            for a in range(5)
        ]
        for part in range(2):
            for o in range(5):
                for k in range(5):
                    rows = place(axis, o, k)
                    values = [state[part, r] for r in rows]
                    for a in range(5):
                        total = None
                        for b, coefficient in used[a]:
                            term = values[b] * coefficient
                            total = term if total is None else total + term
                        state[part, rows[a]] = finish(total)

    column = lax.broadcasted_iota(jnp.int32, (8, half), 1) + bits[0] * half
    centers = initial_centers(column)

    axis, quarter = advance()
    children = shifted(centers, axis, (1.0 - 2.0 * bits[1].astype(jnp.float32)) * quarter)
    low0, width0 = parent_low(0), 1.0 / size[0]
    low1, width1 = parent_low(1), 1.0 / size[1]
    xc = side_points(low1 + jnp.where(flag[2], width1, 0.0), width1)
    for t in range(2):
        x = [low0 + width0 * (t + 0.5)]
        old, new = radicands(centers, x, xc), radicands(children, x, xc)
        for j in range(5):
            for k, (c, s) in enumerate(pair_rotors(old(0, j), new(0, j), quarter, -sign[0])):
                row = j * 3 + k
                first_spin[t, 0, row], first_spin[t, 1, row] = c, s
    merged[0] += 1
    centers = children

    def pair_geometry(level_axis, centers):
        axis, quarter = advance()
        children = shifted(centers, axis, sign[1] * quarter)
        spans = []
        for k in range(2):
            low, width = box(k)
            if k == level_axis:
                low = parent_low(k) + jnp.where(flag[2], width, 0.0)
            spans.append(side_points(low, width))
        merged[level_axis] += 1
        return (centers, children, spans[0], spans[1], quarter), axis

    geometry, axis = pair_geometry(plan[1][0], centers)
    prepare_pairs(*geometry)
    later = []
    for k, level in enumerate(middle):
        side = 2.0 * bits[GATHERED + k].astype(jnp.float32) - 1.0
        centers = shifted(geometry[0], axis, side * geometry[4])
        geometry, axis = pair_geometry(level[0], centers)
        later.append(geometry)
    spot = [1, 2, 0]
    centers = geometry[1]
    upper = [bits[len(plan) - scattered + k] for k in range(scattered - 1)]
    turned = [1.0, 1.0]
    order = [list(range(5)) for _ in range(2)]
    for (axis, _), bit in zip(final, upper):
        turned[axis] = 2.0 * bit.astype(jnp.float32) - 1.0
        order[axis] = [4 - n + bit * (2 * n - 4) for n in range(5)]
    for k, level in enumerate(final):
        axis, quarter = advance()
        low0, width0 = box(0)
        low1, width1 = box(1)
        xi = side_points(low0, width0, turned[0])
        xc = side_points(low1, width1, turned[1])
        if k < scattered - 1:
            children = shifted(centers, axis, sign[spot[k + 1]] * quarter)
            prepare(1 + k, centers, children, xi, xc, quarter)
            centers = children
        else:
            for side in range(2):
                children = shifted(centers, axis, (2.0 * side - 1.0) * quarter)
                prepare(1 + k + side, centers, children, xi, xc, quarter)
        merged[level[0]] += 1
    for k in reversed(range(scattered - 1)):
        for last in range(2):
            fold(scattered + last, final[k][0], 1 + k, last if k == 0 else None)

    across = lagrange((np.arange(cx) + 0.5) / cx - 0.5)
    sums = [[None, None], [None, None], [None, None]]

    def gather_sums(row, re, im):
        whole = re + im
        row = (order[0][row // 25] * 5 + order[1][row // 5 % 5]) * 5 + row % 5
        for last in range(2):
            slot = scattered + last
            terms = whole * spin[slot, 0, row], re * spin[slot, 1, row], im * mixed[last, row]
            for which, term in enumerate(terms):
                held = sums[which][last]
                sums[which][last] = term if held is None else held + term

    def keep_state(row, re, im):
        state[0, row], state[1, row] = re, im

    emit = keep_state if middle else gather_sums
    used = [
        [
            (b, jnp.where(flag[2], MIX[1][a, b], MIX[0][a, b]).astype(jnp.float32))
            for b in range(5)
            if MIX[0][a, b] != 0.0 or MIX[1][a, b] != 0.0
        ]
        for a in range(5)
    ]
    even = [0.5 * (MIX[0][i, 2] + MIX[1][i, 2]) for i in range(3)]
    odd = [0.5 * (MIX[0][i, 2] - MIX[1][i, 2]) for i in range(3)]

    def second_level(pair, i, before):
        lo, hi = PAIRS[pair]
        turned = []
        for j in range(5):
            re, im = before[0][j], before[1][j]
            row = (i * 5 + j) * 3 + pair
            c, s = spin[0, 0, row], spin[0, 1, row]
            turned.append((re * c - im * s, re * s + im * c))
        for a in range(5):
            both = []
            for part in range(2):
                total = None
                for b, coefficient in used[a]:
                    term = turned[b][part] * coefficient
                    total = term if total is None else total + term
                both.append(total + pltpu.roll(total, 4, 0))
            row = (i * 5 + a) * 5
            if lo == hi:
                emit(row + lo, *both)
            else:
                emit(row + lo, *[jnp.where(flag[0], pltpu.roll(x, 1, 0), x) for x in both])
                emit(row + hi, *[jnp.where(flag[0], x, pltpu.roll(x, 7, 0)) for x in both])

    def first_level(pair, t):
        lo, hi = PAIRS[pair]
        across_sums = []
        for part in range(2):
            values = []
            for c in range(cx):
                lines = []
                for q in range(2):
                    row = q * pitch + 2 * c + part
                    first, second = [
                        jnp.broadcast_to(
                            leaf_in[t, pl.ds(row + ORDER.index(k) * rows, 1), :], (8, half)
                        )
                        for k in (lo, hi)
                    ]
                    lines.append(first if lo == hi else jnp.where(flag[0], second, first))
                values.append(jnp.where(flag[2], lines[1], lines[0]))
            totals = []
            for j in range(5):
                total = values[0] * across[j, 0]
                for c in range(1, cx):
                    total = total + values[c] * across[j, c]
                totals.append(total)
            across_sums.append(totals)
        both = []
        for j in range(5):
            re, im = across_sums[0][j], across_sums[1][j]
            row = j * 3 + pair
            c, s = first_spin[t, 0, row], first_spin[t, 1, row]
            both.append((re * c - im * s, re * s + im * c))
        return both

    wait_all(leaf_in.at[0, pl.ds(0, pitch), :], core_recv)
    for pair in range(len(PAIRS)):
        for j, both in enumerate(first_level(pair, bits[0])):
            for part in range(2):
                own_first[part, pair * 5 + j] = both[part]
    facing = 1.0 - 2.0 * bits[0].astype(jnp.float32)
    odd = [facing * x for x in odd]
    for pair, (lo, hi) in enumerate(PAIRS):
        wait_all(leaf_in.at[0, pl.ds(0, 2 * pieces[pair][1]), :], gather_recv[pair])
        theirs = first_level(pair, 1 - bits[0])
        plus, minus = [], []
        for part in range(2):
            mine = [own_first[part, pair * 5 + j] for j in range(5)]
            plus.append([mine[j] + theirs[j][part] for j in range(5)])
            minus.append([mine[j] - theirs[j][part] for j in range(5)])
        for i in range(2):
            es = [[x * even[i] for x in line] for line in plus]
            os = [[x * odd[i] for x in line] for line in minus]
            second_level(pair, i, [[e + o for e, o in zip(*ls)] for ls in zip(es, os)])
            second_level(pair, 4 - i, [[e - o for e, o in zip(*ls)] for ls in zip(es, os)])
        second_level(pair, 2, [[x * even[2] for x in line] for line in plus])

    def joined(level_axis):
        turn(0)
        mix(
            level_axis,
            lambda a, b: jnp.where(flag[2], MIX[1][a, b], MIX[0][a, b]).astype(jnp.float32),
            lambda x: x + pltpu.roll(x, 4, 0),
        )

    for k, level in enumerate(middle):
        bit = bits[GATHERED + k]

        def pack(r, carry):
            mine = pl.ds(bit * 2, 1)
            theirs = pl.ds((1 - bit) * 2, 1)
            for part in range(2):
                line = pl.ds(part * 125 + r, 1)
                swap_out[k, line, :] = state[part, r, theirs, :]
                swap_in[2 * k + 1, line, :] = state[part, r, mine, :]
            return carry

        lax.fori_loop(0, 125, pack, 0)
        copy = pltpu.make_async_remote_copy(
            src_ref=swap_out.at[k],
            dst_ref=swap_in.at[2 * k],
            send_sem=swap_send.at[k],
            recv_sem=swap_recv.at[k],
            device_id=other([level]),
            device_id_type=MESH,
        )
        copy.start()
        prepare(0, *later[k])
        copy.wait()
        own_high = (sub >> 2) == bit

        def unpack(r, carry):
            for part in range(2):
                line = pl.ds(part * 125 + r, 1)
                near_line = jnp.broadcast_to(swap_in[2 * k + 1, line, :], (8, half))
                far_line = jnp.broadcast_to(swap_in[2 * k, line, :], (8, half))
                state[part, r] = jnp.where(own_high, near_line, far_line)
            return carry

        lax.fori_loop(0, 125, unpack, 0)
        joined(level[0])

    if middle:
        for row in range(125):
            gather_sums(row, state[0, row], state[1, row])
    for part in range(2):
        for side in range(2):
            first, second, third = [line[side] for line in sums]
            total = first - third if part == 0 else first + second
            part_out[pl.ds(part * 2 + side, 8, stride=8), :] = total

    def place_of(flips):
        total = 0
        for k, level in enumerate(final):
            bit = bits[len(plan) - scattered + k] ^ (1 if level in flips else 0)
            total = total + bit * (1 << spot[k])
        return pl.multiple_of(total * 8, 8)

    for k, flips in enumerate(far):
        copy = pltpu.make_async_remote_copy(
            src_ref=part_out.at[pl.ds(place_of(flips), 4), :],
            dst_ref=part_in.at[k],
            send_sem=send_sem,
            recv_sem=scatter_recv,
            device_id=other(flips),
            device_id_type=MESH,
        )
        copy.start()
    wait_all(part_in, scatter_recv)
    sent = spin.at[0, 0, pl.ds(0, (len(near) * pitch + 4 * len(far)) // 8)]
    total = part_in[0]
    for k in range(1, len(far)):
        total = total + part_in[k]
    wait_all(sent, send_sem)
    for part in range(2):
        for side in range(2):
            line = part * 2 + side
            out_ref[part : part + 1, side * half : (side + 1) * half] = total[line : line + 1, :]


def shards(samples):
    counts = (lax.axis_size("inline"), lax.axis_size("xline"))
    plan = roster(*counts)
    scattered = SCATTERED
    middle = len(plan) - GATHERED - scattered
    size = samples.shape[2]
    fits = samples.shape[1] == 1 and size == 8 * LANES and NF == 2 * LANES
    fits = fits and middle >= 0 and plan[:2] == [(0, 0), (1, 0)]
    if not fits or plan[-3][0] == plan[-2][0]:
        raise ValueError("unsupported mesh")
    half = COLS // 2
    samples = samples.reshape(2, size // LANES, LANES)
    pitch = 5 * samples.shape[1]
    swaps = [
        pltpu.VMEM((middle, 256, half), jnp.float32),
        pltpu.VMEM((2 * middle, 256, half), jnp.float32),
        pltpu.SemaphoreType.DMA((middle,)),
        pltpu.SemaphoreType.DMA((middle,)),
    ]
    norm = 1.0 / math.sqrt(size * counts[0] * counts[1])
    values = pl.pallas_call(
        functools.partial(kernel, counts, scattered),
        out_shape=jax.ShapeDtypeStruct((2, COLS), jnp.float32),
        in_specs=[pl.BlockSpec(memory_space=pltpu.HBM)],
        out_specs=pl.BlockSpec(memory_space=pltpu.VMEM),
        scratch_shapes=[
            pltpu.VMEM(samples.shape, jnp.float32),
            pltpu.SemaphoreType.DMA,
            pltpu.VMEM((2, 125, 8, half), jnp.float32),
            pltpu.VMEM((2, 2, 15, 8, half), jnp.float32),
            pltpu.VMEM((2, 15, 8, half), jnp.float32),
            pltpu.VMEM((scattered + 2, 2, 125, 8, half), jnp.float32),
            pltpu.VMEM((2, 125, 8, half), jnp.float32),
            pltpu.VMEM((2 * pitch, half), jnp.float32),
            pltpu.VMEM((2, 2 * pitch, half), jnp.float32),
            pltpu.VMEM((64, half), jnp.float32),
            pltpu.VMEM((1 << scattered, 4, half), jnp.float32),
            *[pltpu.SemaphoreType.DMA] * 6,
            *(swaps if middle else []),
        ],
        compiler_params=pltpu.CompilerParams(
            collective_id=0, has_side_effects=True, vmem_limit_bytes=20 << 20
        ),
    )(pltpu.with_memory_space_constraint(samples, pltpu.HBM))
    return values * norm


def solution(mesh):
    return jax.shard_map(
        shards,
        mesh=mesh,
        in_specs=(P(None, "inline", "xline"),),
        out_specs=P(None, ("inline", "xline")),
        check_vma=False,
    )
```

```python
import functools
import math

import jax
import jax.numpy as jnp
import numpy as np
from jax import lax
from jax.experimental import pallas as pl
from jax.experimental.pallas import tpu as pltpu
from jax.sharding import PartitionSpec as P

NF = 256
COLS = 256
KAPPA = 40.0
LANES = 128
GATHERED = 2
SCATTERED = 3
MESH = pl.DeviceIdType.MESH
PAIRS = [(0, 4), (1, 3), (2, 2)]
ORDER = [0, 4, 1, 3, 2]

NODES = np.array([0.5, 0.5 * math.sqrt(0.5), 0.0, -0.5 * math.sqrt(0.5), -0.5])


def lagrange(points):
    points = np.asarray(points, np.float64)
    rows = []
    for k in range(5):
        factor = np.ones_like(points)
        for j in range(5):
            if j != k:
                factor = factor * (points - NODES[j]) / (NODES[k] - NODES[j])
        rows.append(factor)
    table = np.stack(rows)
    return np.where(np.abs(table) < 1e-13, 0.0, table)


MIX = [lagrange((t - 0.5) / 2 + NODES / 2) for t in range(2)]


def roster(inline_count, xline_count):
    inline_bits = inline_count.bit_length() - 1
    xline_bits = xline_count.bit_length() - 1
    plan = []
    for level in range(max(inline_bits, xline_bits)):
        if level < inline_bits:
            plan.append((0, level))
        if level < xline_bits:
            plan.append((1, level))
    return plan


def split_counts():
    depth = (COLS - 1).bit_length()
    return depth, [len([j for j in range(depth) if j % 3 == axis]) for axis in range(3)]


def initial_centers(column):
    depth, _ = split_counts()
    coords = []
    for axis in range(3):
        splits = [j for j in range(depth) if j % 3 == axis]
        coord = jnp.full(column.shape, 0.5 * 0.5 ** len(splits), jnp.float32)
        for rank, j in enumerate(splits):
            digit = (column >> (depth - 1 - j)) & 1
            coord = coord + digit.astype(jnp.float32) * 0.5 ** (rank + 1)
        coords.append(coord)
    return coords


def poly(square, terms):
    total = jnp.full(square.shape, terms[-1], jnp.float32)
    for term in reversed(terms[:-1]):
        total = total * square + term
    return total


def series(limit):
    both = []
    for odd in (1, 0):
        terms = []
        while not terms or limit ** (2 * len(terms) + odd) / math.factorial(2 * len(terms) + odd) > 1e-7:
            terms.append((-1.0) ** len(terms) / math.factorial(2 * len(terms) + odd))
        both.append(terms)
    return both


def root_of(square):
    return square * lax.rsqrt(square)


def parts_of(value):
    high = value.astype(jnp.bfloat16)
    return high, (value - high.astype(jnp.float32)).astype(jnp.bfloat16)


def product(left, right):
    return jnp.dot(left, right, preferred_element_type=jnp.float32)


def small_sincos(angle, limit):
    sine, cosine = series(limit)
    square = angle * angle
    return angle * poly(square, sine), poly(square, cosine)


def turn_sincos(turns):
    half = (turns - jnp.round(turns)) * math.pi
    s, c = small_sincos(half, math.pi / 2)
    return 2.0 * s * c, 1.0 - 2.0 * s * s


def base_rotors(before, after, reach):
    gap = root_of(after) - root_of(before)
    cs, cc = small_sincos(gap * (0.5 * KAPPA), 0.5 * KAPPA * reach)
    bs, bc = small_sincos(gap * (NODES[1] * KAPPA), NODES[1] * KAPPA * reach)
    twice = cs + cs
    return (cc, cs), (bc, bs), (1.0 - twice * cs, twice * cc)


def rotors(before, after, reach):
    (cc, cs), (bc, bs), (a_c, a_s) = base_rotors(before, after, reach)
    p, q, u, v = a_c * bc, a_s * bs, a_s * bc, a_c * bs
    return [
        (a_c * cc - a_s * cs, a_s * cc + a_c * cs),
        (p - q, u + v),
        (a_c, a_s),
        (p + q, u - v),
        (cc, cs),
    ]


def pair_rotors(before, after, reach, sign):
    (cc, cs), (bc, bs), (a_c, a_s) = base_rotors(before, after, reach)
    cs, bs = cs * sign, bs * sign
    return [
        (a_c * cc - a_s * cs, a_s * cc + a_c * cs),
        (a_c * bc - a_s * bs, a_s * bc + a_c * bs),
        (a_c, a_s),
    ]


def side_points(low, width, turned=1.0):
    return [low + width * (z * turned + 0.5) for z in NODES]


def radicands(centers, xi, xc):
    anchor = 0.5 + centers[0]
    first = [anchor * anchor + centers[1] * (x * x) for x in xi]
    second = [centers[2] * (x * x) for x in xc]
    return lambda i, j: first[i] + second[j]


def shifted(centers, axis, amount):
    return [c + amount if k == axis else c for k, c in enumerate(centers)]


def leaf_sums(samples_ref, arrive, store, done, column, inline_pos, xline_pos, inline_count, xline_count):
    rows = samples_ref.shape[1]
    halves = NF // LANES
    cx = rows // halves
    fine = LANES // cx
    turn = KAPPA / (2 * math.pi)
    centers = initial_centers(column)
    anchor = 0.5 + centers[0]
    x0 = (inline_pos + 0.5) / inline_count
    roots = []
    for c in range(cx):
        x1 = (xline_pos + (c + 0.5) / cx) / xline_count
        root = root_of(anchor * anchor + centers[1] * (x0 * x0) + centers[2] * (x1 * x1))
        roots.append(root * turn)
    step = lax.broadcasted_iota(jnp.int32, (fine, COLS), 0).astype(jnp.float32) * (1.0 / NF)
    near = [turn_sincos(step * root) for root in roots]
    near = [jnp.concatenate([table[part] for table in near], axis=0) for part in range(2)]
    row = lax.broadcasted_iota(jnp.int32, (rows, COLS), 0)
    root = jnp.broadcast_to(roots[0], (rows, COLS))
    for c in range(1, cx):
        root = jnp.where(row // halves == c, roots[c], root)
    far = []
    for d in range(cx):
        start = row % halves * LANES + (row // halves + cx - d) % cx * fine
        far.append(turn_sincos(root * (0.5 + (start.astype(jnp.float32) + 0.5) / NF)))
    row = lax.broadcasted_iota(jnp.int32, (rows, LANES), 0)
    lane = lax.broadcasted_iota(jnp.int32, (rows, LANES), 1)
    mask = lane // fine == row // halves
    basis = []
    for d in range(cx):
        spot = row % halves * LANES + (row // halves + cx - d) % cx * fine + lane % fine
        z = (spot.astype(jnp.float32) + 0.5) / NF - 0.5
        line = []
        for k in range(5):
            factor = None
            for j in range(5):
                if j != k:
                    term = (z - NODES[j]) * (1.0 / (NODES[k] - NODES[j]))
                    factor = term if factor is None else factor * term
            line.append(jnp.where(mask, factor, 0.0))
        basis.append(line)
    odd = row % 2 == 1
    width = COLS // 2
    tables = []
    for side in range(2):
        lanes = slice(side * width, (side + 1) * width)
        high, low = parts_of(jnp.concatenate([near[1][:, lanes], near[0][:, lanes]], axis=1))
        tables.append((jnp.concatenate([high, high], axis=0), low))
    arrive()
    moved = [
        [samples_ref[part] if d == 0 else pltpu.roll(samples_ref[part], d * fine, 1) for d in range(cx)]
        for part in range(2)
    ]
    left = [moved[part][d] * basis[d][k] for k in ORDER for part in range(2) for d in range(cx)]
    high, low = parts_of(jnp.concatenate(left, axis=0))
    both = jnp.concatenate([high, low], axis=1)
    for side in range(2):
        lanes = slice(side * width, (side + 1) * width)
        made = product(both, tables[side][0]), product(high, tables[side][1])
        for spot in range(5):
            sums = [None, None]
            for d in range(cx):
                start = (spot * 2 * cx + d) * rows
                r, i = [], []
                for half in made:
                    re = half[start : start + rows]
                    im = half[start + cx * rows : start + (cx + 1) * rows]
                    r.append(re[:, :width] - im[:, width:])
                    i.append(re[:, width:] + im[:, :width])
                r, i = r[0] + r[1], i[0] + i[1]
                hs, hc = far[d][0][:, lanes], far[d][1][:, lanes]
                for part, term in enumerate((r * hc - i * hs, i * hc + r * hs)):
                    sums[part] = term if sums[part] is None else sums[part] + term
            re, im = sums
            pair = jnp.where(odd, im + pltpu.roll(im, 1, 0), re + pltpu.roll(re, rows - 1, 0))
            store(side, spot, pair)
        done(side)


def wait_all(ref, sem):
    pltpu.make_async_copy(ref, ref, sem).wait()


def kernel(
    counts,
    scattered,
    samples_hbm,
    out_ref,
    samples_ref,
    fetch_sem,
    state,
    first_spin,
    own_first,
    spin,
    mixed,
    leaf_out,
    leaf_in,
    part_out,
    part_in,
    gather_recv_0,
    gather_recv_1,
    gather_recv_2,
    core_recv,
    scatter_recv,
    swap_out=None,
    swap_in=None,
    swap_send=None,
    swap_recv=None,
):
    send_sem = fetch_sem
    gather_recv = (gather_recv_0, gather_recv_1, gather_recv_2)
    fetch = pltpu.make_async_copy(samples_hbm, samples_ref, fetch_sem)
    fetch.start()
    rows = samples_ref.shape[1]
    cx = rows * LANES // NF
    pitch = 5 * rows
    index = (lax.axis_index("inline"), lax.axis_index("xline"))
    plan = roster(*counts)
    middle = plan[GATHERED : len(plan) - scattered]
    final = plan[len(plan) - scattered :]
    bits = [(index[axis] >> place) & 1 for axis, place in plan]
    size = [c * 1.0 for c in counts]

    def other(flips):
        target = list(index)
        for axis, place in flips:
            target[axis] = target[axis] ^ (1 << place)
        return tuple(target)

    def subsets(levels):
        return [
            [level for k, level in enumerate(levels) if pattern >> k & 1]
            for pattern in range(1, 1 << len(levels))
        ]

    near = sorted(subsets(plan[:GATHERED]), key=lambda flips: plan[0] not in flips)
    far = [[plan[1]] + flips for flips in [[]] + subsets(final)][::-1]
    calls = near + [f for f in far if f not in near] + [[level] for level in middle]
    partners = [other(f) for f in calls]
    barrier = pltpu.get_barrier_semaphore()
    for partner in partners:
        pl.semaphore_signal(barrier, inc=1, device_id=partner, device_id_type=MESH)

    half = COLS // 2

    def keep(side, spot, value):
        row = side * pitch + spot * rows
        leaf_out[row : row + rows, :] = value

    def send(side):
        if side == 0:
            pl.semaphore_wait(barrier, len(partners))
            lax.fori_loop(0, 1 + jnp.minimum(index[0], 0), first_copies, 0)
        else:
            start_copies(1)

    def first_copies(_, carry):
        start_copies(0)
        return carry

    def start_copies(side):
        whole = [((0, pitch), core_recv)]
        for (start, length), sem in zip(pieces, gather_recv) if side == 0 else whole:
            for flips in near:
                if (plan[0] in flips) == (side == 0):
                    pltpu.make_async_remote_copy(
                        src_ref=leaf_out.at[pl.ds(side * pitch + start, length), :],
                        dst_ref=leaf_in.at[
                            bits[0], pl.ds(pl.multiple_of(bits[1] * pitch + start, 8), length), :
                        ],
                        send_sem=send_sem,
                        recv_sem=sem,
                        device_id=other(flips),
                        device_id_type=MESH,
                    ).start()

    pieces = [(0, 2 * rows), (2 * rows, 2 * rows), (4 * rows, rows)]
    lane = lax.broadcasted_iota(jnp.int32, (1, COLS), 1)
    column = lane % half + half * jnp.where(lane < half, 1 - bits[0], bits[0])
    position = [i.astype(jnp.float32) for i in index]
    leaf_sums(samples_ref, fetch.wait, keep, send, column, position[0], position[1], size[0], size[1])
    own_row = pl.multiple_of(bits[1] * pitch, 8)
    leaf_in[bits[0], pl.ds(own_row, pitch), :] = leaf_out[pl.ds(pitch, pitch), :]

    sub = lax.broadcasted_iota(jnp.int32, (8, half), 0)
    flag = [((sub >> k) & 1) == 1 for k in range(3)]
    sign = [jnp.where(f, 1.0, -1.0) for f in flag]
    depth, splits = split_counts()
    merged = [0, 0]

    def advance():
        nonlocal depth
        axis = depth % 3
        quarter = 0.25 * 0.5 ** splits[axis]
        splits[axis] += 1
        depth += 1
        return axis, quarter

    def box(axis):
        width = 2.0 ** merged[axis] / size[axis]
        low = ((index[axis] >> merged[axis]) << merged[axis]).astype(jnp.float32) / size[axis]
        return low, width

    def parent_low(axis):
        up = merged[axis] + 1
        return ((index[axis] >> up) << up).astype(jnp.float32) / size[axis]

    def prepare(slot, centers, children, xi, xc, reach):
        old, new = radicands(centers, xi, xc), radicands(children, xi, xc)
        for i in range(5):
            for j in range(5):
                for k, (c, s) in enumerate(rotors(old(i, j), new(i, j), reach)):
                    row = (i * 5 + j) * 5 + k
                    spin[slot, 0, row], spin[slot, 1, row] = c, s

    def prepare_pairs(centers, children, xi, xc, reach):
        old, new = radicands(centers, xi, xc), radicands(children, xi, xc)
        for i in range(5):
            for j in range(5):
                for k, (c, s) in enumerate(pair_rotors(old(i, j), new(i, j), reach, -sign[0])):
                    row = (i * 5 + j) * 3 + k
                    spin[0, 0, row], spin[0, 1, row] = c, s

    def place(axis, o, k):
        return [((a * 5 + o) if axis == 0 else (o * 5 + a)) * 5 + k for a in range(5)]

    def fold(slot, axis, held, finish):
        for o in range(5):
            for k in range(5):
                rows = place(axis, o, k)
                after = [[spin[slot, part, r] for r in rows] for part in range(2)]
                for b in range(5):
                    both = []
                    for part in range(2):
                        total = None
                        for a in range(5):
                            if MIX[1][a, b] != 0.0:
                                term = after[part][a]
                                if MIX[1][a, b] != 1.0:
                                    term = term * MIX[1][a, b]
                                total = term if total is None else total + term
                        both.append(total)
                    re, im = both
                    c, s = spin[held, 0, rows[b]], spin[held, 1, rows[b]]
                    re, im = re * c - im * s, re * s + im * c
                    spin[slot, 0, rows[b]] = re
                    if finish is None:
                        spin[slot, 1, rows[b]] = im
                    else:
                        spin[slot, 1, rows[b]], mixed[finish, rows[b]] = im - re, re + im

    def turn(slot):
        for row in range(125):
            re, im = state[0, row], state[1, row]
            c, s = spin[slot, 0, row], spin[slot, 1, row]
            state[0, row] = re * c - im * s
            state[1, row] = re * s + im * c

    def mix(axis, choose, finish):
        used = [
            [(b, choose(a, b)) for b in range(5) if MIX[0][a, b] != 0.0 or MIX[1][a, b] != 0.0]
            for a in range(5)
        ]
        for part in range(2):
            for o in range(5):
                for k in range(5):
                    rows = place(axis, o, k)
                    values = [state[part, r] for r in rows]
                    for a in range(5):
                        total = None
                        for b, coefficient in used[a]:
                            term = values[b] * coefficient
                            total = term if total is None else total + term
                        state[part, rows[a]] = finish(total)

    column = lax.broadcasted_iota(jnp.int32, (8, half), 1) + bits[0] * half
    centers = initial_centers(column)

    axis, quarter = advance()
    children = shifted(centers, axis, (1.0 - 2.0 * bits[1].astype(jnp.float32)) * quarter)
    low0, width0 = parent_low(0), 1.0 / size[0]
    low1, width1 = parent_low(1), 1.0 / size[1]
    xc = side_points(low1 + jnp.where(flag[2], width1, 0.0), width1)
    for t in range(2):
        x = [low0 + width0 * (t + 0.5)]
        old, new = radicands(centers, x, xc), radicands(children, x, xc)
        for j in range(5):
            for k, (c, s) in enumerate(pair_rotors(old(0, j), new(0, j), quarter, -sign[0])):
                row = j * 3 + k
                first_spin[t, 0, row], first_spin[t, 1, row] = c, s
    merged[0] += 1
    centers = children

    def pair_geometry(level_axis, centers):
        axis, quarter = advance()
        children = shifted(centers, axis, sign[1] * quarter)
        spans = []
        for k in range(2):
            low, width = box(k)
            if k == level_axis:
                low = parent_low(k) + jnp.where(flag[2], width, 0.0)
            spans.append(side_points(low, width))
        merged[level_axis] += 1
        return (centers, children, spans[0], spans[1], quarter), axis

    geometry, axis = pair_geometry(plan[1][0], centers)
    prepare_pairs(*geometry)
    later = []
    for k, level in enumerate(middle):
        side = 2.0 * bits[GATHERED + k].astype(jnp.float32) - 1.0
        centers = shifted(geometry[0], axis, side * geometry[4])
        geometry, axis = pair_geometry(level[0], centers)
        later.append(geometry)
    spot = [1, 2, 0]
    centers = geometry[1]
    upper = [bits[len(plan) - scattered + k] for k in range(scattered - 1)]
    turned = [1.0, 1.0]
    order = [list(range(5)) for _ in range(2)]
    for (axis, _), bit in zip(final, upper):
        turned[axis] = 2.0 * bit.astype(jnp.float32) - 1.0
        order[axis] = [4 - n + bit * (2 * n - 4) for n in range(5)]
    for k, level in enumerate(final):
        axis, quarter = advance()
        low0, width0 = box(0)
        low1, width1 = box(1)
        xi = side_points(low0, width0, turned[0])
        xc = side_points(low1, width1, turned[1])
        if k < scattered - 1:
            children = shifted(centers, axis, sign[spot[k + 1]] * quarter)
            prepare(1 + k, centers, children, xi, xc, quarter)
            centers = children
        else:
            for side in range(2):
                children = shifted(centers, axis, (2.0 * side - 1.0) * quarter)
                prepare(1 + k + side, centers, children, xi, xc, quarter)
        merged[level[0]] += 1
    for k in reversed(range(scattered - 1)):
        for last in range(2):
            fold(scattered + last, final[k][0], 1 + k, last if k == 0 else None)

    across = lagrange((np.arange(cx) + 0.5) / cx - 0.5)
    sums = [[None, None], [None, None], [None, None]]

    def gather_sums(row, re, im):
        whole = re + im
        row = (order[0][row // 25] * 5 + order[1][row // 5 % 5]) * 5 + row % 5
        for last in range(2):
            slot = scattered + last
            terms = whole * spin[slot, 0, row], re * spin[slot, 1, row], im * mixed[last, row]
            for which, term in enumerate(terms):
                held = sums[which][last]
                sums[which][last] = term if held is None else held + term

    def keep_state(row, re, im):
        state[0, row], state[1, row] = re, im

    emit = keep_state if middle else gather_sums
    used = [
        [
            (b, jnp.where(flag[2], MIX[1][a, b], MIX[0][a, b]).astype(jnp.float32))
            for b in range(5)
            if MIX[0][a, b] != 0.0 or MIX[1][a, b] != 0.0
        ]
        for a in range(5)
    ]
    even = [0.5 * (MIX[0][i, 2] + MIX[1][i, 2]) for i in range(3)]
    odd = [0.5 * (MIX[0][i, 2] - MIX[1][i, 2]) for i in range(3)]

    def second_level(pair, i, before):
        lo, hi = PAIRS[pair]
        turned = []
        for j in range(5):
            re, im = before[0][j], before[1][j]
            row = (i * 5 + j) * 3 + pair
            c, s = spin[0, 0, row], spin[0, 1, row]
            turned.append((re * c - im * s, re * s + im * c))
        for a in range(5):
            both = []
            for part in range(2):
                total = None
                for b, coefficient in used[a]:
                    term = turned[b][part] * coefficient
                    total = term if total is None else total + term
                both.append(total + pltpu.roll(total, 4, 0))
            row = (i * 5 + a) * 5
            if lo == hi:
                emit(row + lo, *both)
            else:
                emit(row + lo, *[jnp.where(flag[0], pltpu.roll(x, 1, 0), x) for x in both])
                emit(row + hi, *[jnp.where(flag[0], x, pltpu.roll(x, 7, 0)) for x in both])

    def first_level(pair, t):
        lo, hi = PAIRS[pair]
        across_sums = []
        for part in range(2):
            values = []
            for c in range(cx):
                lines = []
                for q in range(2):
                    row = q * pitch + 2 * c + part
                    first, second = [
                        jnp.broadcast_to(
                            leaf_in[t, pl.ds(row + ORDER.index(k) * rows, 1), :], (8, half)
                        )
                        for k in (lo, hi)
                    ]
                    lines.append(first if lo == hi else jnp.where(flag[0], second, first))
                values.append(jnp.where(flag[2], lines[1], lines[0]))
            totals = []
            for j in range(5):
                total = values[0] * across[j, 0]
                for c in range(1, cx):
                    total = total + values[c] * across[j, c]
                totals.append(total)
            across_sums.append(totals)
        both = []
        for j in range(5):
            re, im = across_sums[0][j], across_sums[1][j]
            row = j * 3 + pair
            c, s = first_spin[t, 0, row], first_spin[t, 1, row]
            both.append((re * c - im * s, re * s + im * c))
        return both

    wait_all(leaf_in.at[0, pl.ds(0, pitch), :], core_recv)
    for pair in range(len(PAIRS)):
        for j, both in enumerate(first_level(pair, bits[0])):
            for part in range(2):
                own_first[part, pair * 5 + j] = both[part]
    facing = 1.0 - 2.0 * bits[0].astype(jnp.float32)
    odd = [facing * x for x in odd]
    for pair, (lo, hi) in enumerate(PAIRS):
        wait_all(leaf_in.at[0, pl.ds(0, 2 * pieces[pair][1]), :], gather_recv[pair])
        theirs = first_level(pair, 1 - bits[0])
        plus, minus = [], []
        for part in range(2):
            mine = [own_first[part, pair * 5 + j] for j in range(5)]
            plus.append([mine[j] + theirs[j][part] for j in range(5)])
            minus.append([mine[j] - theirs[j][part] for j in range(5)])
        for i in range(2):
            es = [[x * even[i] for x in line] for line in plus]
            os = [[x * odd[i] for x in line] for line in minus]
            second_level(pair, i, [[e + o for e, o in zip(*ls)] for ls in zip(es, os)])
            second_level(pair, 4 - i, [[e - o for e, o in zip(*ls)] for ls in zip(es, os)])
        second_level(pair, 2, [[x * even[2] for x in line] for line in plus])

    def joined(level_axis):
        turn(0)
        mix(
            level_axis,
            lambda a, b: jnp.where(flag[2], MIX[1][a, b], MIX[0][a, b]).astype(jnp.float32),
            lambda x: x + pltpu.roll(x, 4, 0),
        )

    for k, level in enumerate(middle):
        bit = bits[GATHERED + k]

        def pack(r, carry):
            mine = pl.ds(bit * 2, 1)
            theirs = pl.ds((1 - bit) * 2, 1)
            for part in range(2):
                line = pl.ds(part * 125 + r, 1)
                swap_out[k, line, :] = state[part, r, theirs, :]
                swap_in[2 * k + 1, line, :] = state[part, r, mine, :]
            return carry

        lax.fori_loop(0, 125, pack, 0)
        copy = pltpu.make_async_remote_copy(
            src_ref=swap_out.at[k],
            dst_ref=swap_in.at[2 * k],
            send_sem=swap_send.at[k],
            recv_sem=swap_recv.at[k],
            device_id=other([level]),
            device_id_type=MESH,
        )
        copy.start()
        prepare(0, *later[k])
        copy.wait()
        own_high = (sub >> 2) == bit

        def unpack(r, carry):
            for part in range(2):
                line = pl.ds(part * 125 + r, 1)
                near_line = jnp.broadcast_to(swap_in[2 * k + 1, line, :], (8, half))
                far_line = jnp.broadcast_to(swap_in[2 * k, line, :], (8, half))
                state[part, r] = jnp.where(own_high, near_line, far_line)
            return carry

        lax.fori_loop(0, 125, unpack, 0)
        joined(level[0])

    if middle:
        for row in range(125):
            gather_sums(row, state[0, row], state[1, row])
    for part in range(2):
        for side in range(2):
            first, second, third = [line[side] for line in sums]
            total = first - third if part == 0 else first + second
            part_out[pl.ds(part * 2 + side, 8, stride=8), :] = total

    def place_of(flips):
        total = 0
        for k, level in enumerate(final):
            bit = bits[len(plan) - scattered + k] ^ (1 if level in flips else 0)
            total = total + bit * (1 << spot[k])
        return pl.multiple_of(total * 8, 8)

    for k, flips in enumerate(far):
        copy = pltpu.make_async_remote_copy(
            src_ref=part_out.at[pl.ds(place_of(flips), 4), :],
            dst_ref=part_in.at[k],
            send_sem=send_sem,
            recv_sem=scatter_recv,
            device_id=other(flips),
            device_id_type=MESH,
        )
        copy.start()
    wait_all(part_in, scatter_recv)
    sent = spin.at[0, 0, pl.ds(0, (len(near) * pitch + 4 * len(far)) // 8)]
    total = part_in[0]
    for k in range(1, len(far)):
        total = total + part_in[k]
    wait_all(sent, send_sem)
    for part in range(2):
        for side in range(2):
            line = part * 2 + side
            out_ref[part : part + 1, side * half : (side + 1) * half] = total[line : line + 1, :]


def shards(samples):
    counts = (lax.axis_size("inline"), lax.axis_size("xline"))
    plan = roster(*counts)
    scattered = SCATTERED
    middle = len(plan) - GATHERED - scattered
    size = samples.shape[2]
    fits = samples.shape[1] == 1 and size == 8 * LANES and NF == 2 * LANES
    fits = fits and middle >= 0 and plan[:2] == [(0, 0), (1, 0)]
    if not fits or plan[-3][0] == plan[-2][0]:
        raise ValueError("unsupported mesh")
    half = COLS // 2
    samples = samples.reshape(2, size // LANES, LANES)
    pitch = 5 * samples.shape[1]
    swaps = [
        pltpu.VMEM((middle, 256, half), jnp.float32),
        pltpu.VMEM((2 * middle, 256, half), jnp.float32),
        pltpu.SemaphoreType.DMA((middle,)),
        pltpu.SemaphoreType.DMA((middle,)),
    ]
    norm = 1.0 / math.sqrt(size * counts[0] * counts[1])
    values = pl.pallas_call(
        functools.partial(kernel, counts, scattered),
        out_shape=jax.ShapeDtypeStruct((2, COLS), jnp.float32),
        in_specs=[pl.BlockSpec(memory_space=pltpu.HBM)],
        out_specs=pl.BlockSpec(memory_space=pltpu.VMEM),
        scratch_shapes=[
            pltpu.VMEM(samples.shape, jnp.float32),
            pltpu.SemaphoreType.DMA,
            pltpu.VMEM((2, 125, 8, half), jnp.float32),
            pltpu.VMEM((2, 2, 15, 8, half), jnp.float32),
            pltpu.VMEM((2, 15, 8, half), jnp.float32),
            pltpu.VMEM((scattered + 2, 2, 125, 8, half), jnp.float32),
            pltpu.VMEM((2, 125, 8, half), jnp.float32),
            pltpu.VMEM((2 * pitch, half), jnp.float32),
            pltpu.VMEM((2, 2 * pitch, half), jnp.float32),
            pltpu.VMEM((64, half), jnp.float32),
            pltpu.VMEM((1 << scattered, 4, half), jnp.float32),
            *[pltpu.SemaphoreType.DMA] * 5,
            *(swaps if middle else []),
        ],
        compiler_params=pltpu.CompilerParams(
            collective_id=0, has_side_effects=True, vmem_limit_bytes=20 << 20
        ),
    )(pltpu.with_memory_space_constraint(samples, pltpu.HBM))
    return values * norm


def solution(mesh):
    return jax.shard_map(
        shards,
        mesh=mesh,
        in_specs=(P(None, "inline", "xline"),),
        out_specs=P(None, ("inline", "xline")),
        check_vma=False,
    )
```

```python
import functools
import math

import jax
import jax.numpy as jnp
import numpy as np
from jax import lax
from jax.experimental import pallas as pl
from jax.experimental.pallas import tpu as pltpu
from jax.sharding import PartitionSpec as P

NF = 256
COLS = 256
KAPPA = 40.0
LANES = 128
GATHERED = 2
SCATTERED = 3
MESH = pl.DeviceIdType.MESH
PAIRS = [(0, 4), (1, 3), (2, 2)]
ORDER = [0, 4, 1, 3, 2]

NODES = np.array([0.5, 0.5 * math.sqrt(0.5), 0.0, -0.5 * math.sqrt(0.5), -0.5])


def lagrange(points):
    points = np.asarray(points, np.float64)
    rows = []
    for k in range(5):
        factor = np.ones_like(points)
        for j in range(5):
            if j != k:
                factor = factor * (points - NODES[j]) / (NODES[k] - NODES[j])
        rows.append(factor)
    table = np.stack(rows)
    return np.where(np.abs(table) < 1e-13, 0.0, table)


MIX = [lagrange((t - 0.5) / 2 + NODES / 2) for t in range(2)]


def roster(inline_count, xline_count):
    inline_bits = inline_count.bit_length() - 1
    xline_bits = xline_count.bit_length() - 1
    plan = []
    for level in range(max(inline_bits, xline_bits)):
        if level < inline_bits:
            plan.append((0, level))
        if level < xline_bits:
            plan.append((1, level))
    return plan


def split_counts():
    depth = (COLS - 1).bit_length()
    return depth, [len([j for j in range(depth) if j % 3 == axis]) for axis in range(3)]


def initial_centers(column):
    depth, _ = split_counts()
    coords = []
    for axis in range(3):
        splits = [j for j in range(depth) if j % 3 == axis]
        coord = jnp.full(column.shape, 0.5 * 0.5 ** len(splits), jnp.float32)
        for rank, j in enumerate(splits):
            digit = (column >> (depth - 1 - j)) & 1
            coord = coord + digit.astype(jnp.float32) * 0.5 ** (rank + 1)
        coords.append(coord)
    return coords


def poly(square, terms):
    total = jnp.full(square.shape, terms[-1], jnp.float32)
    for term in reversed(terms[:-1]):
        total = total * square + term
    return total


def series(limit):
    both = []
    for odd in (1, 0):
        terms = []
        while not terms or limit ** (2 * len(terms) + odd) / math.factorial(2 * len(terms) + odd) > 1e-7:
            terms.append((-1.0) ** len(terms) / math.factorial(2 * len(terms) + odd))
        both.append(terms)
    return both


def root_of(square):
    return square * lax.rsqrt(square)


def parts_of(value):
    high = value.astype(jnp.bfloat16)
    return high, (value - high.astype(jnp.float32)).astype(jnp.bfloat16)


def product(left, right):
    return jnp.dot(left, right, preferred_element_type=jnp.float32)


def small_sincos(angle, limit):
    sine, cosine = series(limit)
    square = angle * angle
    return angle * poly(square, sine), poly(square, cosine)


def turn_sincos(turns):
    half = (turns - jnp.round(turns)) * math.pi
    s, c = small_sincos(half, math.pi / 2)
    return 2.0 * s * c, 1.0 - 2.0 * s * s


def base_rotors(before, after, reach):
    gap = root_of(after) - root_of(before)
    cs, cc = small_sincos(gap * (0.5 * KAPPA), 0.5 * KAPPA * reach)
    bs, bc = small_sincos(gap * (NODES[1] * KAPPA), NODES[1] * KAPPA * reach)
    twice = cs + cs
    return (cc, cs), (bc, bs), (1.0 - twice * cs, twice * cc)


def rotors(before, after, reach):
    (cc, cs), (bc, bs), (a_c, a_s) = base_rotors(before, after, reach)
    p, q, u, v = a_c * bc, a_s * bs, a_s * bc, a_c * bs
    return [
        (a_c * cc - a_s * cs, a_s * cc + a_c * cs),
        (p - q, u + v),
        (a_c, a_s),
        (p + q, u - v),
        (cc, cs),
    ]


def pair_rotors(before, after, reach, sign):
    (cc, cs), (bc, bs), (a_c, a_s) = base_rotors(before, after, reach)
    cs, bs = cs * sign, bs * sign
    return [
        (a_c * cc - a_s * cs, a_s * cc + a_c * cs),
        (a_c * bc - a_s * bs, a_s * bc + a_c * bs),
        (a_c, a_s),
    ]


def side_points(low, width, turned=1.0):
    return [low + width * (z * turned + 0.5) for z in NODES]


def radicands(centers, xi, xc):
    anchor = 0.5 + centers[0]
    first = [anchor * anchor + centers[1] * (x * x) for x in xi]
    second = [centers[2] * (x * x) for x in xc]
    return lambda i, j: first[i] + second[j]


def shifted(centers, axis, amount):
    return [c + amount if k == axis else c for k, c in enumerate(centers)]


def leaf_sums(samples_ref, arrive, store, done, column, inline_pos, xline_pos, inline_count, xline_count):
    rows = samples_ref.shape[1]
    halves = NF // LANES
    cx = rows // halves
    fine = LANES // cx
    turn = KAPPA / (2 * math.pi)
    centers = initial_centers(column)
    anchor = 0.5 + centers[0]
    x0 = (inline_pos + 0.5) / inline_count
    roots = []
    for c in range(cx):
        x1 = (xline_pos + (c + 0.5) / cx) / xline_count
        root = root_of(anchor * anchor + centers[1] * (x0 * x0) + centers[2] * (x1 * x1))
        roots.append(root * turn)
    step = lax.broadcasted_iota(jnp.int32, (fine, COLS), 0).astype(jnp.float32) * (1.0 / NF)
    near = [turn_sincos(step * root) for root in roots]
    near = [jnp.concatenate([table[part] for table in near], axis=0) for part in range(2)]
    row = lax.broadcasted_iota(jnp.int32, (rows, COLS), 0)
    root = jnp.broadcast_to(roots[0], (rows, COLS))
    for c in range(1, cx):
        root = jnp.where(row // halves == c, roots[c], root)
    far = []
    for d in range(cx):
        start = row % halves * LANES + (row // halves + cx - d) % cx * fine
        far.append(turn_sincos(root * (0.5 + (start.astype(jnp.float32) + 0.5) / NF)))
    row = lax.broadcasted_iota(jnp.int32, (rows, LANES), 0)
    lane = lax.broadcasted_iota(jnp.int32, (rows, LANES), 1)
    mask = lane // fine == row // halves
    basis = []
    for d in range(cx):
        spot = row % halves * LANES + (row // halves + cx - d) % cx * fine + lane % fine
        z = (spot.astype(jnp.float32) + 0.5) / NF - 0.5
        line = []
        for k in range(5):
            factor = None
            for j in range(5):
                if j != k:
                    term = (z - NODES[j]) * (1.0 / (NODES[k] - NODES[j]))
                    factor = term if factor is None else factor * term
            line.append(jnp.where(mask, factor, 0.0))
        basis.append(line)
    odd = row % 2 == 1
    width = COLS // 2
    tables = []
    for side in range(2):
        lanes = slice(side * width, (side + 1) * width)
        high, low = parts_of(jnp.concatenate([near[1][:, lanes], near[0][:, lanes]], axis=1))
        tables.append((jnp.concatenate([high, high], axis=0), low))
    arrive()
    moved = [
        [samples_ref[part] if d == 0 else pltpu.roll(samples_ref[part], d * fine, 1) for d in range(cx)]
        for part in range(2)
    ]
    left = [moved[part][d] * basis[d][k] for k in ORDER for part in range(2) for d in range(cx)]
    high, low = parts_of(jnp.concatenate(left, axis=0))
    both = jnp.concatenate([high, low], axis=1)
    for side in range(2):
        lanes = slice(side * width, (side + 1) * width)
        made = product(both, tables[side][0]), product(high, tables[side][1])
        for spot in range(5):
            sums = [None, None]
            for d in range(cx):
                start = (spot * 2 * cx + d) * rows
                r, i = [], []
                for half in made:
                    re = half[start : start + rows]
                    im = half[start + cx * rows : start + (cx + 1) * rows]
                    r.append(re[:, :width] - im[:, width:])
                    i.append(re[:, width:] + im[:, :width])
                r, i = r[0] + r[1], i[0] + i[1]
                hs, hc = far[d][0][:, lanes], far[d][1][:, lanes]
                for part, term in enumerate((r * hc - i * hs, i * hc + r * hs)):
                    sums[part] = term if sums[part] is None else sums[part] + term
            re, im = sums
            pair = jnp.where(odd, im + pltpu.roll(im, 1, 0), re + pltpu.roll(re, rows - 1, 0))
            store(side, spot, pair)
        done(side)


def wait_all(ref, sem):
    pltpu.make_async_copy(ref, ref, sem).wait()


def kernel(
    counts,
    scattered,
    samples_hbm,
    out_ref,
    samples_ref,
    fetch_sem,
    state,
    first_spin,
    own_first,
    spin,
    mixed,
    leaf_out,
    leaf_in,
    part_out,
    part_in,
    gather_recv_0,
    gather_recv_1,
    gather_recv_2,
    core_recv,
    scatter_recv,
    swap_out=None,
    swap_in=None,
    swap_send=None,
    swap_recv=None,
):
    send_sem = fetch_sem
    gather_recv = (gather_recv_0, gather_recv_1, gather_recv_2)
    fetch = pltpu.make_async_copy(samples_hbm, samples_ref, fetch_sem)
    fetch.start()
    rows = samples_ref.shape[1]
    cx = rows * LANES // NF
    pitch = 5 * rows
    index = (lax.axis_index("inline"), lax.axis_index("xline"))
    plan = roster(*counts)
    middle = plan[GATHERED : len(plan) - scattered]
    final = plan[len(plan) - scattered :]
    bits = [(index[axis] >> place) & 1 for axis, place in plan]
    size = [c * 1.0 for c in counts]

    def other(flips):
        target = list(index)
        for axis, place in flips:
            target[axis] = target[axis] ^ (1 << place)
        return tuple(target)

    def subsets(levels):
        return [
            [level for k, level in enumerate(levels) if pattern >> k & 1]
            for pattern in range(1, 1 << len(levels))
        ]

    near = sorted(subsets(plan[:GATHERED]), key=lambda flips: plan[0] not in flips)
    far = [[plan[1]] + flips for flips in [[]] + subsets(final)][::-1]
    calls = near + [f for f in far if f not in near] + [[level] for level in middle]
    partners = [other(f) for f in calls]
    barrier = pltpu.get_barrier_semaphore()
    for partner in partners:
        pl.semaphore_signal(barrier, inc=1, device_id=partner, device_id_type=MESH)

    half = COLS // 2

    def keep(side, spot, value):
        row = side * pitch + spot * rows
        leaf_out[row : row + rows, :] = value

    def send(side):
        if side == 0:
            pl.semaphore_wait(barrier, len(partners))
            lax.fori_loop(0, 1 + jnp.minimum(index[0], 0), first_copies, 0)
        else:
            start_copies(1)

    def first_copies(_, carry):
        start_copies(0)
        return carry

    def start_copies(side):
        whole = [((0, pitch), core_recv)]
        for (start, length), sem in zip(pieces, gather_recv) if side == 0 else whole:
            for flips in near:
                if (plan[0] in flips) == (side == 0):
                    pltpu.make_async_remote_copy(
                        src_ref=leaf_out.at[pl.ds(side * pitch + start, length), :],
                        dst_ref=leaf_in.at[
                            bits[0], pl.ds(pl.multiple_of(bits[1] * pitch + start, 8), length), :
                        ],
                        send_sem=send_sem,
                        recv_sem=sem,
                        device_id=other(flips),
                        device_id_type=MESH,
                    ).start()

    pieces = [(0, 2 * rows), (2 * rows, 2 * rows), (4 * rows, rows)]
    lane = lax.broadcasted_iota(jnp.int32, (1, COLS), 1)
    column = lane % half + half * jnp.where(lane < half, 1 - bits[0], bits[0])
    position = [i.astype(jnp.float32) for i in index]
    leaf_sums(samples_ref, fetch.wait, keep, send, column, position[0], position[1], size[0], size[1])
    own_row = pl.multiple_of(bits[1] * pitch, 8)
    leaf_in[bits[0], pl.ds(own_row, pitch), :] = leaf_out[pl.ds(pitch, pitch), :]

    sub = lax.broadcasted_iota(jnp.int32, (8, half), 0)
    flag = [((sub >> k) & 1) == 1 for k in range(3)]
    sign = [jnp.where(f, 1.0, -1.0) for f in flag]
    depth, splits = split_counts()
    merged = [0, 0]

    def advance():
        nonlocal depth
        axis = depth % 3
        quarter = 0.25 * 0.5 ** splits[axis]
        splits[axis] += 1
        depth += 1
        return axis, quarter

    def box(axis):
        width = 2.0 ** merged[axis] / size[axis]
        low = ((index[axis] >> merged[axis]) << merged[axis]).astype(jnp.float32) / size[axis]
        return low, width

    def parent_low(axis):
        up = merged[axis] + 1
        return ((index[axis] >> up) << up).astype(jnp.float32) / size[axis]

    def prepare(slot, centers, children, xi, xc, reach):
        old, new = radicands(centers, xi, xc), radicands(children, xi, xc)
        for i in range(5):
            for j in range(5):
                for k, (c, s) in enumerate(rotors(old(i, j), new(i, j), reach)):
                    row = (i * 5 + j) * 5 + k
                    spin[slot, 0, row], spin[slot, 1, row] = c, s

    def prepare_pairs(centers, children, xi, xc, reach):
        old, new = radicands(centers, xi, xc), radicands(children, xi, xc)
        for i in range(5):
            for j in range(5):
                for k, (c, s) in enumerate(pair_rotors(old(i, j), new(i, j), reach, -sign[0])):
                    row = (i * 5 + j) * 3 + k
                    spin[0, 0, row], spin[0, 1, row] = c, s

    def place(axis, o, k):
        return [((a * 5 + o) if axis == 0 else (o * 5 + a)) * 5 + k for a in range(5)]

    def fold(slot, axis, held, finish):
        for o in range(5):
            for k in range(5):
                rows = place(axis, o, k)
                after = [[spin[slot, part, r] for r in rows] for part in range(2)]
                for b in range(5):
                    both = []
                    for part in range(2):
                        total = None
                        for a in range(5):
                            if MIX[1][a, b] != 0.0:
                                term = after[part][a]
                                if MIX[1][a, b] != 1.0:
                                    term = term * MIX[1][a, b]
                                total = term if total is None else total + term
                        both.append(total)
                    re, im = both
                    c, s = spin[held, 0, rows[b]], spin[held, 1, rows[b]]
                    re, im = re * c - im * s, re * s + im * c
                    spin[slot, 0, rows[b]] = re
                    if finish is None:
                        spin[slot, 1, rows[b]] = im
                    else:
                        spin[slot, 1, rows[b]], mixed[finish, rows[b]] = im - re, re + im

    def turn(slot):
        for row in range(125):
            re, im = state[0, row], state[1, row]
            c, s = spin[slot, 0, row], spin[slot, 1, row]
            state[0, row] = re * c - im * s
            state[1, row] = re * s + im * c

    def mix(axis, choose, finish):
        used = [
            [(b, choose(a, b)) for b in range(5) if MIX[0][a, b] != 0.0 or MIX[1][a, b] != 0.0]
            for a in range(5)
        ]
        for part in range(2):
            for o in range(5):
                for k in range(5):
                    rows = place(axis, o, k)
                    values = [state[part, r] for r in rows]
                    for a in range(5):
                        total = None
                        for b, coefficient in used[a]:
                            term = values[b] * coefficient
                            total = term if total is None else total + term
                        state[part, rows[a]] = finish(total)

    column = lax.broadcasted_iota(jnp.int32, (8, half), 1) + bits[0] * half
    centers = initial_centers(column)

    axis, quarter = advance()
    children = shifted(centers, axis, (1.0 - 2.0 * bits[1].astype(jnp.float32)) * quarter)
    low0, width0 = parent_low(0), 1.0 / size[0]
    low1, width1 = parent_low(1), 1.0 / size[1]
    xc = side_points(low1 + jnp.where(flag[2], width1, 0.0), width1)
    for t in range(2):
        x = [low0 + width0 * (t + 0.5)]
        old, new = radicands(centers, x, xc), radicands(children, x, xc)
        for j in range(5):
            for k, (c, s) in enumerate(pair_rotors(old(0, j), new(0, j), quarter, -sign[0])):
                row = j * 3 + k
                first_spin[t, 0, row], first_spin[t, 1, row] = c, s
    merged[0] += 1
    centers = children

    def pair_geometry(level_axis, centers):
        axis, quarter = advance()
        children = shifted(centers, axis, sign[1] * quarter)
        spans = []
        for k in range(2):
            low, width = box(k)
            if k == level_axis:
                low = parent_low(k) + jnp.where(flag[2], width, 0.0)
            spans.append(side_points(low, width))
        merged[level_axis] += 1
        return (centers, children, spans[0], spans[1], quarter), axis

    geometry, axis = pair_geometry(plan[1][0], centers)
    prepare_pairs(*geometry)
    later = []
    for k, level in enumerate(middle):
        side = 2.0 * bits[GATHERED + k].astype(jnp.float32) - 1.0
        centers = shifted(geometry[0], axis, side * geometry[4])
        geometry, axis = pair_geometry(level[0], centers)
        later.append(geometry)
    spot = [1, 2, 0]
    centers = geometry[1]
    upper = [bits[len(plan) - scattered + k] for k in range(scattered - 1)]
    turned = [1.0, 1.0]
    order = [list(range(5)) for _ in range(2)]
    for (axis, _), bit in zip(final, upper):
        turned[axis] = 2.0 * bit.astype(jnp.float32) - 1.0
        order[axis] = [4 - n + bit * (2 * n - 4) for n in range(5)]
    for k, level in enumerate(final):
        axis, quarter = advance()
        low0, width0 = box(0)
        low1, width1 = box(1)
        xi = side_points(low0, width0, turned[0])
        xc = side_points(low1, width1, turned[1])
        if k < scattered - 1:
            children = shifted(centers, axis, sign[spot[k + 1]] * quarter)
            prepare(1 + k, centers, children, xi, xc, quarter)
            centers = children
        else:
            for side in range(2):
                children = shifted(centers, axis, (2.0 * side - 1.0) * quarter)
                prepare(1 + k + side, centers, children, xi, xc, quarter)
        merged[level[0]] += 1
    for k in reversed(range(scattered - 1)):
        for last in range(2):
            fold(scattered + last, final[k][0], 1 + k, last if k == 0 else None)

    across = lagrange((np.arange(cx) + 0.5) / cx - 0.5)
    sums = [[None, None], [None, None], [None, None]]

    def gather_sums(row, re, im):
        whole = re + im
        row = (order[0][row // 25] * 5 + order[1][row // 5 % 5]) * 5 + row % 5
        for last in range(2):
            slot = scattered + last
            terms = whole * spin[slot, 0, row], re * spin[slot, 1, row], im * mixed[last, row]
            for which, term in enumerate(terms):
                held = sums[which][last]
                sums[which][last] = term if held is None else held + term

    def keep_state(row, re, im):
        state[0, row], state[1, row] = re, im

    emit = keep_state if middle else gather_sums
    used = [
        [
            (b, jnp.where(flag[2], MIX[1][a, b], MIX[0][a, b]).astype(jnp.float32))
            for b in range(5)
            if MIX[0][a, b] != 0.0 or MIX[1][a, b] != 0.0
        ]
        for a in range(5)
    ]
    even = [0.5 * (MIX[0][i, 2] + MIX[1][i, 2]) for i in range(3)]
    odd = [0.5 * (MIX[0][i, 2] - MIX[1][i, 2]) for i in range(3)]

    def second_level(pair, i, before):
        lo, hi = PAIRS[pair]
        turned = []
        for j in range(5):
            re, im = before[0][j], before[1][j]
            row = (i * 5 + j) * 3 + pair
            c, s = spin[0, 0, row], spin[0, 1, row]
            turned.append((re * c - im * s, re * s + im * c))
        for a in range(5):
            both = []
            for part in range(2):
                total = None
                for b, coefficient in used[a]:
                    term = turned[b][part] * coefficient
                    total = term if total is None else total + term
                both.append(total + pltpu.roll(total, 4, 0))
            row = (i * 5 + a) * 5
            if lo == hi:
                emit(row + lo, *both)
            else:
                emit(row + lo, *[jnp.where(flag[0], pltpu.roll(x, 1, 0), x) for x in both])
                emit(row + hi, *[jnp.where(flag[0], x, pltpu.roll(x, 7, 0)) for x in both])

    def first_level(pair, t):
        lo, hi = PAIRS[pair]
        across_sums = []
        for part in range(2):
            values = []
            for c in range(cx):
                lines = []
                for q in range(2):
                    row = q * pitch + 2 * c + part
                    first, second = [
                        jnp.broadcast_to(
                            leaf_in[t, pl.ds(row + ORDER.index(k) * rows, 1), :], (8, half)
                        )
                        for k in (lo, hi)
                    ]
                    lines.append(first if lo == hi else jnp.where(flag[0], second, first))
                values.append(jnp.where(flag[2], lines[1], lines[0]))
            totals = []
            for j in range(5):
                total = values[0] * across[j, 0]
                for c in range(1, cx):
                    total = total + values[c] * across[j, c]
                totals.append(total)
            across_sums.append(totals)
        both = []
        for j in range(5):
            re, im = across_sums[0][j], across_sums[1][j]
            row = j * 3 + pair
            c, s = first_spin[t, 0, row], first_spin[t, 1, row]
            both.append((re * c - im * s, re * s + im * c))
        return both

    wait_all(leaf_in.at[0, pl.ds(0, pitch), :], core_recv)
    for pair in range(len(PAIRS)):
        for j, both in enumerate(first_level(pair, bits[0])):
            for part in range(2):
                own_first[part, pair * 5 + j] = both[part]
    facing = 1.0 - 2.0 * bits[0].astype(jnp.float32)
    odd = [facing * x for x in odd]
    for pair, (lo, hi) in enumerate(PAIRS):
        wait_all(leaf_in.at[0, pl.ds(0, 2 * pieces[pair][1]), :], gather_recv[pair])
        theirs = first_level(pair, 1 - bits[0])
        plus, minus = [], []
        for part in range(2):
            mine = [own_first[part, pair * 5 + j] for j in range(5)]
            plus.append([mine[j] + theirs[j][part] for j in range(5)])
            minus.append([mine[j] - theirs[j][part] for j in range(5)])
        for i in range(2):
            es = [[x * even[i] for x in line] for line in plus]
            os = [[x * odd[i] for x in line] for line in minus]
            second_level(pair, i, [[e + o for e, o in zip(*ls)] for ls in zip(es, os)])
            second_level(pair, 4 - i, [[e - o for e, o in zip(*ls)] for ls in zip(es, os)])
        second_level(pair, 2, [[x * even[2] for x in line] for line in plus])

    def joined(level_axis):
        turn(0)
        mix(
            level_axis,
            lambda a, b: jnp.where(flag[2], MIX[1][a, b], MIX[0][a, b]).astype(jnp.float32),
            lambda x: x + pltpu.roll(x, 4, 0),
        )

    for k, level in enumerate(middle):
        bit = bits[GATHERED + k]

        def pack(r, carry):
            mine = pl.ds(bit * 2, 1)
            theirs = pl.ds((1 - bit) * 2, 1)
            for part in range(2):
                line = pl.ds(part * 125 + r, 1)
                swap_out[k, line, :] = state[part, r, theirs, :]
                swap_in[2 * k + 1, line, :] = state[part, r, mine, :]
            return carry

        lax.fori_loop(0, 125, pack, 0)
        copy = pltpu.make_async_remote_copy(
            src_ref=swap_out.at[k],
            dst_ref=swap_in.at[2 * k],
            send_sem=swap_send.at[k],
            recv_sem=swap_recv.at[k],
            device_id=other([level]),
            device_id_type=MESH,
        )
        copy.start()
        prepare(0, *later[k])
        copy.wait()
        own_high = (sub >> 2) == bit

        def unpack(r, carry):
            for part in range(2):
                line = pl.ds(part * 125 + r, 1)
                near_line = jnp.broadcast_to(swap_in[2 * k + 1, line, :], (8, half))
                far_line = jnp.broadcast_to(swap_in[2 * k, line, :], (8, half))
                state[part, r] = jnp.where(own_high, near_line, far_line)
            return carry

        lax.fori_loop(0, 125, unpack, 0)
        joined(level[0])

    if middle:
        for row in range(125):
            gather_sums(row, state[0, row], state[1, row])
    for part in range(2):
        for side in range(2):
            first, second, third = [line[side] for line in sums]
            total = first - third if part == 0 else first + second
            part_out[pl.ds(side * 2 + part, 8, stride=8), :] = total

    def place_of(flips):
        total = 0
        for k, level in enumerate(final):
            bit = bits[len(plan) - scattered + k] ^ (1 if level in flips else 0)
            total = total + bit * (1 << spot[k])
        return pl.multiple_of(total * 8, 8)

    for k, flips in enumerate(far):
        copy = pltpu.make_async_remote_copy(
            src_ref=part_out.at[pl.ds(place_of(flips), 4), :],
            dst_ref=part_in.at[k],
            send_sem=send_sem,
            recv_sem=scatter_recv,
            device_id=other(flips),
            device_id_type=MESH,
        )
        copy.start()
    wait_all(part_in, scatter_recv)
    sent = spin.at[0, 0, pl.ds(0, (len(near) * pitch + 4 * len(far)) // 8)]
    total = part_in[0]
    for k in range(1, len(far)):
        total = total + part_in[k]
    wait_all(sent, send_sem)
    out_ref[...] = total


def shards(samples):
    counts = (lax.axis_size("inline"), lax.axis_size("xline"))
    plan = roster(*counts)
    scattered = SCATTERED
    middle = len(plan) - GATHERED - scattered
    size = samples.shape[2]
    fits = samples.shape[1] == 1 and size == 8 * LANES and NF == 2 * LANES
    fits = fits and middle >= 0 and plan[:2] == [(0, 0), (1, 0)]
    if not fits or plan[-3][0] == plan[-2][0]:
        raise ValueError("unsupported mesh")
    half = COLS // 2
    samples = samples.reshape(2, size // LANES, LANES)
    pitch = 5 * samples.shape[1]
    swaps = [
        pltpu.VMEM((middle, 256, half), jnp.float32),
        pltpu.VMEM((2 * middle, 256, half), jnp.float32),
        pltpu.SemaphoreType.DMA((middle,)),
        pltpu.SemaphoreType.DMA((middle,)),
    ]
    norm = 1.0 / math.sqrt(size * counts[0] * counts[1])
    values = pl.pallas_call(
        functools.partial(kernel, counts, scattered),
        out_shape=jax.ShapeDtypeStruct((4, half), jnp.float32),
        in_specs=[pl.BlockSpec(memory_space=pltpu.HBM)],
        out_specs=pl.BlockSpec(memory_space=pltpu.VMEM),
        scratch_shapes=[
            pltpu.VMEM(samples.shape, jnp.float32),
            pltpu.SemaphoreType.DMA,
            pltpu.VMEM((2, 125, 8, half), jnp.float32),
            pltpu.VMEM((2, 2, 15, 8, half), jnp.float32),
            pltpu.VMEM((2, 15, 8, half), jnp.float32),
            pltpu.VMEM((scattered + 2, 2, 125, 8, half), jnp.float32),
            pltpu.VMEM((2, 125, 8, half), jnp.float32),
            pltpu.VMEM((2 * pitch, half), jnp.float32),
            pltpu.VMEM((2, 2 * pitch, half), jnp.float32),
            pltpu.VMEM((64, half), jnp.float32),
            pltpu.VMEM((1 << scattered, 4, half), jnp.float32),
            *[pltpu.SemaphoreType.DMA] * 5,
            *(swaps if middle else []),
        ],
        compiler_params=pltpu.CompilerParams(
            collective_id=0, has_side_effects=True, vmem_limit_bytes=20 << 20
        ),
    )(pltpu.with_memory_space_constraint(samples, pltpu.HBM))
    return (values * norm).reshape(2, 2, half).transpose(1, 0, 2).reshape(2, COLS)


def solution(mesh):
    return jax.shard_map(
        shards,
        mesh=mesh,
        in_specs=(P(None, "inline", "xline"),),
        out_specs=P(None, ("inline", "xline")),
        check_vma=False,
    )
```

```python
import functools
import math

import jax
import jax.numpy as jnp
import numpy as np
from jax import lax
from jax.experimental import pallas as pl
from jax.experimental.pallas import tpu as pltpu
from jax.sharding import PartitionSpec as P

NF = 256
COLS = 256
KAPPA = 40.0
LANES = 128
GATHERED = 2
SCATTERED = 3
MESH = pl.DeviceIdType.MESH
PAIRS = [(0, 4), (1, 3), (2, 2)]
ORDER = [0, 4, 1, 3, 2]

NODES = np.array([0.5, 0.5 * math.sqrt(0.5), 0.0, -0.5 * math.sqrt(0.5), -0.5])


def lagrange(points):
    points = np.asarray(points, np.float64)
    rows = []
    for k in range(5):
        factor = np.ones_like(points)
        for j in range(5):
            if j != k:
                factor = factor * (points - NODES[j]) / (NODES[k] - NODES[j])
        rows.append(factor)
    table = np.stack(rows)
    return np.where(np.abs(table) < 1e-13, 0.0, table)


MIX = [lagrange((t - 0.5) / 2 + NODES / 2) for t in range(2)]


def roster(inline_count, xline_count):
    inline_bits = inline_count.bit_length() - 1
    xline_bits = xline_count.bit_length() - 1
    plan = []
    for level in range(max(inline_bits, xline_bits)):
        if level < inline_bits:
            plan.append((0, level))
        if level < xline_bits:
            plan.append((1, level))
    return plan


def split_counts():
    depth = (COLS - 1).bit_length()
    return depth, [len([j for j in range(depth) if j % 3 == axis]) for axis in range(3)]


def initial_centers(column):
    depth, _ = split_counts()
    coords = []
    for axis in range(3):
        splits = [j for j in range(depth) if j % 3 == axis]
        coord = jnp.full(column.shape, 0.5 * 0.5 ** len(splits), jnp.float32)
        for rank, j in enumerate(splits):
            digit = (column >> (depth - 1 - j)) & 1
            coord = coord + digit.astype(jnp.float32) * 0.5 ** (rank + 1)
        coords.append(coord)
    return coords


def poly(square, terms):
    total = jnp.full(square.shape, terms[-1], jnp.float32)
    for term in reversed(terms[:-1]):
        total = total * square + term
    return total


def series(limit):
    both = []
    for odd in (1, 0):
        terms = []
        while not terms or limit ** (2 * len(terms) + odd) / math.factorial(2 * len(terms) + odd) > 1e-7:
            terms.append((-1.0) ** len(terms) / math.factorial(2 * len(terms) + odd))
        both.append(terms)
    return both


def root_of(square):
    return square * lax.rsqrt(square)


def parts_of(value):
    high = value.astype(jnp.bfloat16)
    return high, (value - high.astype(jnp.float32)).astype(jnp.bfloat16)


def product(left, right):
    return jnp.dot(left, right, preferred_element_type=jnp.float32)


def small_sincos(angle, limit):
    sine, cosine = series(limit)
    square = angle * angle
    return angle * poly(square, sine), poly(square, cosine)


def turn_sincos(turns):
    half = (turns - jnp.round(turns)) * math.pi
    s, c = small_sincos(half, math.pi / 2)
    return 2.0 * s * c, 1.0 - 2.0 * s * s


def base_rotors(before, after, reach):
    gap = root_of(after) - root_of(before)
    cs, cc = small_sincos(gap * (0.5 * KAPPA), 0.5 * KAPPA * reach)
    bs, bc = small_sincos(gap * (NODES[1] * KAPPA), NODES[1] * KAPPA * reach)
    twice = cs + cs
    return (cc, cs), (bc, bs), (1.0 - twice * cs, twice * cc)


def rotors(before, after, reach):
    (cc, cs), (bc, bs), (a_c, a_s) = base_rotors(before, after, reach)
    p, q, u, v = a_c * bc, a_s * bs, a_s * bc, a_c * bs
    return [
        (a_c * cc - a_s * cs, a_s * cc + a_c * cs),
        (p - q, u + v),
        (a_c, a_s),
        (p + q, u - v),
        (cc, cs),
    ]


def pair_rotors(before, after, reach, sign):
    (cc, cs), (bc, bs), (a_c, a_s) = base_rotors(before, after, reach)
    cs, bs = cs * sign, bs * sign
    return [
        (a_c * cc - a_s * cs, a_s * cc + a_c * cs),
        (a_c * bc - a_s * bs, a_s * bc + a_c * bs),
        (a_c, a_s),
    ]


def side_points(low, width, turned=1.0):
    return [low + width * (z * turned + 0.5) for z in NODES]


def radicands(centers, xi, xc):
    anchor = 0.5 + centers[0]
    first = [anchor * anchor + centers[1] * (x * x) for x in xi]
    second = [centers[2] * (x * x) for x in xc]
    return lambda i, j: first[i] + second[j]


def shifted(centers, axis, amount):
    return [c + amount if k == axis else c for k, c in enumerate(centers)]


def leaf_sums(samples_ref, arrive, store, done, column, inline_pos, xline_pos, inline_count, xline_count):
    rows = samples_ref.shape[1]
    halves = NF // LANES
    cx = rows // halves
    fine = LANES // cx
    turn = KAPPA / (2 * math.pi)
    centers = initial_centers(column)
    anchor = 0.5 + centers[0]
    x0 = (inline_pos + 0.5) / inline_count
    roots = []
    for c in range(cx):
        x1 = (xline_pos + (c + 0.5) / cx) / xline_count
        root = root_of(anchor * anchor + centers[1] * (x0 * x0) + centers[2] * (x1 * x1))
        roots.append(root * turn)
    step = lax.broadcasted_iota(jnp.int32, (fine, COLS), 0).astype(jnp.float32) * (1.0 / NF)
    near = [turn_sincos(step * root) for root in roots]
    near = [jnp.concatenate([table[part] for table in near], axis=0) for part in range(2)]
    row = lax.broadcasted_iota(jnp.int32, (rows, COLS), 0)
    root = jnp.broadcast_to(roots[0], (rows, COLS))
    for c in range(1, cx):
        root = jnp.where(row // halves == c, roots[c], root)
    far = []
    for d in range(cx):
        start = row % halves * LANES + (row // halves + cx - d) % cx * fine
        far.append(turn_sincos(root * (0.5 + (start.astype(jnp.float32) + 0.5) / NF)))
    row = lax.broadcasted_iota(jnp.int32, (rows, LANES), 0)
    lane = lax.broadcasted_iota(jnp.int32, (rows, LANES), 1)
    mask = lane // fine == row // halves
    basis = []
    for d in range(cx):
        spot = row % halves * LANES + (row // halves + cx - d) % cx * fine + lane % fine
        z = (spot.astype(jnp.float32) + 0.5) / NF - 0.5
        line = []
        for k in range(5):
            factor = None
            for j in range(5):
                if j != k:
                    term = (z - NODES[j]) * (1.0 / (NODES[k] - NODES[j]))
                    factor = term if factor is None else factor * term
            line.append(jnp.where(mask, factor, 0.0))
        basis.append(line)
    odd = row % 2 == 1
    width = COLS // 2
    tables = []
    for side in range(2):
        lanes = slice(side * width, (side + 1) * width)
        high, low = parts_of(jnp.concatenate([near[1][:, lanes], near[0][:, lanes]], axis=1))
        tables.append((jnp.concatenate([high, high], axis=0), low))
    arrive()
    moved = [
        [samples_ref[part] if d == 0 else pltpu.roll(samples_ref[part], d * fine, 1) for d in range(cx)]
        for part in range(2)
    ]
    left = [moved[part][d] * basis[d][k] for k in ORDER for part in range(2) for d in range(cx)]
    high, low = parts_of(jnp.concatenate(left, axis=0))
    both = jnp.concatenate([high, low], axis=1)
    for side in range(2):
        lanes = slice(side * width, (side + 1) * width)
        made = product(both, tables[side][0]), product(high, tables[side][1])
        for spot in range(5):
            sums = [None, None]
            for d in range(cx):
                start = (spot * 2 * cx + d) * rows
                r, i = [], []
                for half in made:
                    re = half[start : start + rows]
                    im = half[start + cx * rows : start + (cx + 1) * rows]
                    r.append(re[:, :width] - im[:, width:])
                    i.append(re[:, width:] + im[:, :width])
                r, i = r[0] + r[1], i[0] + i[1]
                hs, hc = far[d][0][:, lanes], far[d][1][:, lanes]
                for part, term in enumerate((r * hc - i * hs, i * hc + r * hs)):
                    sums[part] = term if sums[part] is None else sums[part] + term
            re, im = sums
            pair = jnp.where(odd, im + pltpu.roll(im, 1, 0), re + pltpu.roll(re, rows - 1, 0))
            store(side, spot, pair)
        done(side)


def wait_all(ref, sem):
    pltpu.make_async_copy(ref, ref, sem).wait()


def kernel(
    counts,
    scattered,
    samples_hbm,
    out_ref,
    samples_ref,
    fetch_sem,
    state,
    first_spin,
    own_first,
    spin,
    mixed,
    leaf_out,
    leaf_in,
    part_out,
    part_in,
    gather_recv_0,
    gather_recv_1,
    core_recv,
    scatter_recv,
    swap_out=None,
    swap_in=None,
    swap_send=None,
    swap_recv=None,
):
    send_sem = fetch_sem
    gather_recv = (gather_recv_0, gather_recv_1)
    fetch = pltpu.make_async_copy(samples_hbm, samples_ref, fetch_sem)
    fetch.start()
    rows = samples_ref.shape[1]
    cx = rows * LANES // NF
    pitch = 5 * rows
    index = (lax.axis_index("inline"), lax.axis_index("xline"))
    plan = roster(*counts)
    middle = plan[GATHERED : len(plan) - scattered]
    final = plan[len(plan) - scattered :]
    bits = [(index[axis] >> place) & 1 for axis, place in plan]
    size = [c * 1.0 for c in counts]

    def other(flips):
        target = list(index)
        for axis, place in flips:
            target[axis] = target[axis] ^ (1 << place)
        return tuple(target)

    def subsets(levels):
        return [
            [level for k, level in enumerate(levels) if pattern >> k & 1]
            for pattern in range(1, 1 << len(levels))
        ]

    near = sorted(subsets(plan[:GATHERED]), key=lambda flips: plan[0] not in flips)
    far = [[plan[1]] + flips for flips in [[]] + subsets(final)][::-1]
    calls = near + [f for f in far if f not in near] + [[level] for level in middle]
    partners = [other(f) for f in calls]
    barrier = pltpu.get_barrier_semaphore()
    for partner in partners:
        pl.semaphore_signal(barrier, inc=1, device_id=partner, device_id_type=MESH)

    half = COLS // 2

    def keep(side, spot, value):
        row = side * pitch + spot * rows
        leaf_out[row : row + rows, :] = value

    def send(side):
        if side == 0:
            pl.semaphore_wait(barrier, len(partners))
            lax.fori_loop(0, 1 + jnp.minimum(index[0], 0), first_copies, 0)
        else:
            start_copies(1)

    def first_copies(_, carry):
        start_copies(0)
        return carry

    def start_copies(side):
        whole = [((0, pitch), core_recv)]
        for (start, length), sem in zip(pieces, gather_recv) if side == 0 else whole:
            for flips in near:
                if (plan[0] in flips) == (side == 0):
                    pltpu.make_async_remote_copy(
                        src_ref=leaf_out.at[pl.ds(side * pitch + start, length), :],
                        dst_ref=leaf_in.at[
                            bits[0], pl.ds(pl.multiple_of(bits[1] * pitch + start, 8), length), :
                        ],
                        send_sem=send_sem,
                        recv_sem=sem,
                        device_id=other(flips),
                        device_id_type=MESH,
                    ).start()

    pieces = [(0, 2 * rows), (2 * rows, 3 * rows)]
    lane = lax.broadcasted_iota(jnp.int32, (1, COLS), 1)
    column = lane % half + half * jnp.where(lane < half, 1 - bits[0], bits[0])
    position = [i.astype(jnp.float32) for i in index]
    leaf_sums(samples_ref, fetch.wait, keep, send, column, position[0], position[1], size[0], size[1])
    own_row = pl.multiple_of(bits[1] * pitch, 8)
    leaf_in[bits[0], pl.ds(own_row, pitch), :] = leaf_out[pl.ds(pitch, pitch), :]

    sub = lax.broadcasted_iota(jnp.int32, (8, half), 0)
    flag = [((sub >> k) & 1) == 1 for k in range(3)]
    sign = [jnp.where(f, 1.0, -1.0) for f in flag]
    depth, splits = split_counts()
    merged = [0, 0]

    def advance():
        nonlocal depth
        axis = depth % 3
        quarter = 0.25 * 0.5 ** splits[axis]
        splits[axis] += 1
        depth += 1
        return axis, quarter

    def box(axis):
        width = 2.0 ** merged[axis] / size[axis]
        low = ((index[axis] >> merged[axis]) << merged[axis]).astype(jnp.float32) / size[axis]
        return low, width

    def parent_low(axis):
        up = merged[axis] + 1
        return ((index[axis] >> up) << up).astype(jnp.float32) / size[axis]

    def prepare(slot, centers, children, xi, xc, reach):
        old, new = radicands(centers, xi, xc), radicands(children, xi, xc)
        for i in range(5):
            for j in range(5):
                for k, (c, s) in enumerate(rotors(old(i, j), new(i, j), reach)):
                    row = (i * 5 + j) * 5 + k
                    spin[slot, 0, row], spin[slot, 1, row] = c, s

    def prepare_pairs(centers, children, xi, xc, reach):
        old, new = radicands(centers, xi, xc), radicands(children, xi, xc)
        for i in range(5):
            for j in range(5):
                for k, (c, s) in enumerate(pair_rotors(old(i, j), new(i, j), reach, -sign[0])):
                    row = (i * 5 + j) * 3 + k
                    spin[0, 0, row], spin[0, 1, row] = c, s

    def place(axis, o, k):
        return [((a * 5 + o) if axis == 0 else (o * 5 + a)) * 5 + k for a in range(5)]

    def fold(slot, axis, held, finish):
        for o in range(5):
            for k in range(5):
                rows = place(axis, o, k)
                after = [[spin[slot, part, r] for r in rows] for part in range(2)]
                for b in range(5):
                    both = []
                    for part in range(2):
                        total = None
                        for a in range(5):
                            if MIX[1][a, b] != 0.0:
                                term = after[part][a]
                                if MIX[1][a, b] != 1.0:
                                    term = term * MIX[1][a, b]
                                total = term if total is None else total + term
                        both.append(total)
                    re, im = both
                    c, s = spin[held, 0, rows[b]], spin[held, 1, rows[b]]
                    re, im = re * c - im * s, re * s + im * c
                    spin[slot, 0, rows[b]] = re
                    if finish is None:
                        spin[slot, 1, rows[b]] = im
                    else:
                        spin[slot, 1, rows[b]], mixed[finish, rows[b]] = im - re, re + im

    def turn(slot):
        for row in range(125):
            re, im = state[0, row], state[1, row]
            c, s = spin[slot, 0, row], spin[slot, 1, row]
            state[0, row] = re * c - im * s
            state[1, row] = re * s + im * c

    def mix(axis, choose, finish):
        used = [
            [(b, choose(a, b)) for b in range(5) if MIX[0][a, b] != 0.0 or MIX[1][a, b] != 0.0]
            for a in range(5)
        ]
        for part in range(2):
            for o in range(5):
                for k in range(5):
                    rows = place(axis, o, k)
                    values = [state[part, r] for r in rows]
                    for a in range(5):
                        total = None
                        for b, coefficient in used[a]:
                            term = values[b] * coefficient
                            total = term if total is None else total + term
                        state[part, rows[a]] = finish(total)

    column = lax.broadcasted_iota(jnp.int32, (8, half), 1) + bits[0] * half
    centers = initial_centers(column)

    axis, quarter = advance()
    children = shifted(centers, axis, (1.0 - 2.0 * bits[1].astype(jnp.float32)) * quarter)
    low0, width0 = parent_low(0), 1.0 / size[0]
    low1, width1 = parent_low(1), 1.0 / size[1]
    xc = side_points(low1 + jnp.where(flag[2], width1, 0.0), width1)
    for t in range(2):
        x = [low0 + width0 * (t + 0.5)]
        old, new = radicands(centers, x, xc), radicands(children, x, xc)
        for j in range(5):
            for k, (c, s) in enumerate(pair_rotors(old(0, j), new(0, j), quarter, -sign[0])):
                row = j * 3 + k
                first_spin[t, 0, row], first_spin[t, 1, row] = c, s
    merged[0] += 1
    centers = children

    def pair_geometry(level_axis, centers):
        axis, quarter = advance()
        children = shifted(centers, axis, sign[1] * quarter)
        spans = []
        for k in range(2):
            low, width = box(k)
            if k == level_axis:
                low = parent_low(k) + jnp.where(flag[2], width, 0.0)
            spans.append(side_points(low, width))
        merged[level_axis] += 1
        return (centers, children, spans[0], spans[1], quarter), axis

    geometry, axis = pair_geometry(plan[1][0], centers)
    prepare_pairs(*geometry)
    later = []
    for k, level in enumerate(middle):
        side = 2.0 * bits[GATHERED + k].astype(jnp.float32) - 1.0
        centers = shifted(geometry[0], axis, side * geometry[4])
        geometry, axis = pair_geometry(level[0], centers)
        later.append(geometry)
    spot = [1, 2, 0]
    centers = geometry[1]
    upper = [bits[len(plan) - scattered + k] for k in range(scattered - 1)]
    turned = [1.0, 1.0]
    order = [list(range(5)) for _ in range(2)]
    for (axis, _), bit in zip(final, upper):
        turned[axis] = 2.0 * bit.astype(jnp.float32) - 1.0
        order[axis] = [4 - n + bit * (2 * n - 4) for n in range(5)]
    for k, level in enumerate(final):
        axis, quarter = advance()
        low0, width0 = box(0)
        low1, width1 = box(1)
        xi = side_points(low0, width0, turned[0])
        xc = side_points(low1, width1, turned[1])
        if k < scattered - 1:
            children = shifted(centers, axis, sign[spot[k + 1]] * quarter)
            prepare(1 + k, centers, children, xi, xc, quarter)
            centers = children
        else:
            for side in range(2):
                children = shifted(centers, axis, (2.0 * side - 1.0) * quarter)
                prepare(1 + k + side, centers, children, xi, xc, quarter)
        merged[level[0]] += 1
    for k in reversed(range(scattered - 1)):
        for last in range(2):
            fold(scattered + last, final[k][0], 1 + k, last if k == 0 else None)

    across = lagrange((np.arange(cx) + 0.5) / cx - 0.5)
    sums = [[None, None], [None, None], [None, None]]

    def gather_sums(row, re, im):
        whole = re + im
        row = (order[0][row // 25] * 5 + order[1][row // 5 % 5]) * 5 + row % 5
        for last in range(2):
            slot = scattered + last
            terms = whole * spin[slot, 0, row], re * spin[slot, 1, row], im * mixed[last, row]
            for which, term in enumerate(terms):
                held = sums[which][last]
                sums[which][last] = term if held is None else held + term

    def keep_state(row, re, im):
        state[0, row], state[1, row] = re, im

    emit = keep_state if middle else gather_sums
    used = [
        [
            (b, jnp.where(flag[2], MIX[1][a, b], MIX[0][a, b]).astype(jnp.float32))
            for b in range(5)
            if MIX[0][a, b] != 0.0 or MIX[1][a, b] != 0.0
        ]
        for a in range(5)
    ]
    even = [0.5 * (MIX[0][i, 2] + MIX[1][i, 2]) for i in range(3)]
    odd = [0.5 * (MIX[0][i, 2] - MIX[1][i, 2]) for i in range(3)]

    def second_level(pair, i, before):
        lo, hi = PAIRS[pair]
        turned = []
        for j in range(5):
            re, im = before[0][j], before[1][j]
            row = (i * 5 + j) * 3 + pair
            c, s = spin[0, 0, row], spin[0, 1, row]
            turned.append((re * c - im * s, re * s + im * c))
        for a in range(5):
            both = []
            for part in range(2):
                total = None
                for b, coefficient in used[a]:
                    term = turned[b][part] * coefficient
                    total = term if total is None else total + term
                both.append(total + pltpu.roll(total, 4, 0))
            row = (i * 5 + a) * 5
            if lo == hi:
                emit(row + lo, *both)
            else:
                emit(row + lo, *[jnp.where(flag[0], pltpu.roll(x, 1, 0), x) for x in both])
                emit(row + hi, *[jnp.where(flag[0], x, pltpu.roll(x, 7, 0)) for x in both])

    def first_level(pair, t):
        lo, hi = PAIRS[pair]
        across_sums = []
        for part in range(2):
            values = []
            for c in range(cx):
                lines = []
                for q in range(2):
                    row = q * pitch + 2 * c + part
                    first, second = [
                        jnp.broadcast_to(
                            leaf_in[t, pl.ds(row + ORDER.index(k) * rows, 1), :], (8, half)
                        )
                        for k in (lo, hi)
                    ]
                    lines.append(first if lo == hi else jnp.where(flag[0], second, first))
                values.append(jnp.where(flag[2], lines[1], lines[0]))
            totals = []
            for j in range(5):
                total = values[0] * across[j, 0]
                for c in range(1, cx):
                    total = total + values[c] * across[j, c]
                totals.append(total)
            across_sums.append(totals)
        both = []
        for j in range(5):
            re, im = across_sums[0][j], across_sums[1][j]
            row = j * 3 + pair
            c, s = first_spin[t, 0, row], first_spin[t, 1, row]
            both.append((re * c - im * s, re * s + im * c))
        return both

    wait_all(leaf_in.at[0, pl.ds(0, pitch), :], core_recv)
    for pair in range(len(PAIRS)):
        for j, both in enumerate(first_level(pair, bits[0])):
            for part in range(2):
                own_first[part, pair * 5 + j] = both[part]
    facing = 1.0 - 2.0 * bits[0].astype(jnp.float32)
    odd = [facing * x for x in odd]
    for pair, (lo, hi) in enumerate(PAIRS):
        if pair < len(pieces):
            wait_all(leaf_in.at[0, pl.ds(0, 2 * pieces[pair][1]), :], gather_recv[pair])
        theirs = first_level(pair, 1 - bits[0])
        plus, minus = [], []
        for part in range(2):
            mine = [own_first[part, pair * 5 + j] for j in range(5)]
            plus.append([mine[j] + theirs[j][part] for j in range(5)])
            minus.append([mine[j] - theirs[j][part] for j in range(5)])
        for i in range(2):
            es = [[x * even[i] for x in line] for line in plus]
            os = [[x * odd[i] for x in line] for line in minus]
            second_level(pair, i, [[e + o for e, o in zip(*ls)] for ls in zip(es, os)])
            second_level(pair, 4 - i, [[e - o for e, o in zip(*ls)] for ls in zip(es, os)])
        second_level(pair, 2, [[x * even[2] for x in line] for line in plus])

    def joined(level_axis):
        turn(0)
        mix(
            level_axis,
            lambda a, b: jnp.where(flag[2], MIX[1][a, b], MIX[0][a, b]).astype(jnp.float32),
            lambda x: x + pltpu.roll(x, 4, 0),
        )

    for k, level in enumerate(middle):
        bit = bits[GATHERED + k]

        def pack(r, carry):
            mine = pl.ds(bit * 2, 1)
            theirs = pl.ds((1 - bit) * 2, 1)
            for part in range(2):
                line = pl.ds(part * 125 + r, 1)
                swap_out[k, line, :] = state[part, r, theirs, :]
                swap_in[2 * k + 1, line, :] = state[part, r, mine, :]
            return carry

        lax.fori_loop(0, 125, pack, 0)
        copy = pltpu.make_async_remote_copy(
            src_ref=swap_out.at[k],
            dst_ref=swap_in.at[2 * k],
            send_sem=swap_send.at[k],
            recv_sem=swap_recv.at[k],
            device_id=other([level]),
            device_id_type=MESH,
        )
        copy.start()
        prepare(0, *later[k])
        copy.wait()
        own_high = (sub >> 2) == bit

        def unpack(r, carry):
            for part in range(2):
                line = pl.ds(part * 125 + r, 1)
                near_line = jnp.broadcast_to(swap_in[2 * k + 1, line, :], (8, half))
                far_line = jnp.broadcast_to(swap_in[2 * k, line, :], (8, half))
                state[part, r] = jnp.where(own_high, near_line, far_line)
            return carry

        lax.fori_loop(0, 125, unpack, 0)
        joined(level[0])

    if middle:
        for row in range(125):
            gather_sums(row, state[0, row], state[1, row])
    for part in range(2):
        for side in range(2):
            first, second, third = [line[side] for line in sums]
            total = first - third if part == 0 else first + second
            part_out[pl.ds(part * 2 + side, 8, stride=8), :] = total

    def place_of(flips):
        total = 0
        for k, level in enumerate(final):
            bit = bits[len(plan) - scattered + k] ^ (1 if level in flips else 0)
            total = total + bit * (1 << spot[k])
        return pl.multiple_of(total * 8, 8)

    for k, flips in enumerate(far):
        copy = pltpu.make_async_remote_copy(
            src_ref=part_out.at[pl.ds(place_of(flips), 4), :],
            dst_ref=part_in.at[k],
            send_sem=send_sem,
            recv_sem=scatter_recv,
            device_id=other(flips),
            device_id_type=MESH,
        )
        copy.start()
    wait_all(part_in, scatter_recv)
    sent = spin.at[0, 0, pl.ds(0, (len(near) * pitch + 4 * len(far)) // 8)]
    total = part_in[0]
    for k in range(1, len(far)):
        total = total + part_in[k]
    wait_all(sent, send_sem)
    for part in range(2):
        for side in range(2):
            line = part * 2 + side
            out_ref[part : part + 1, side * half : (side + 1) * half] = total[line : line + 1, :]


def shards(samples):
    counts = (lax.axis_size("inline"), lax.axis_size("xline"))
    plan = roster(*counts)
    scattered = SCATTERED
    middle = len(plan) - GATHERED - scattered
    size = samples.shape[2]
    fits = samples.shape[1] == 1 and size == 8 * LANES and NF == 2 * LANES
    fits = fits and middle >= 0 and plan[:2] == [(0, 0), (1, 0)]
    if not fits or plan[-3][0] == plan[-2][0]:
        raise ValueError("unsupported mesh")
    half = COLS // 2
    samples = samples.reshape(2, size // LANES, LANES)
    pitch = 5 * samples.shape[1]
    swaps = [
        pltpu.VMEM((middle, 256, half), jnp.float32),
        pltpu.VMEM((2 * middle, 256, half), jnp.float32),
        pltpu.SemaphoreType.DMA((middle,)),
        pltpu.SemaphoreType.DMA((middle,)),
    ]
    norm = 1.0 / math.sqrt(size * counts[0] * counts[1])
    values = pl.pallas_call(
        functools.partial(kernel, counts, scattered),
        out_shape=jax.ShapeDtypeStruct((2, COLS), jnp.float32),
        in_specs=[pl.BlockSpec(memory_space=pltpu.HBM)],
        out_specs=pl.BlockSpec(memory_space=pltpu.VMEM),
        scratch_shapes=[
            pltpu.VMEM(samples.shape, jnp.float32),
            pltpu.SemaphoreType.DMA,
            pltpu.VMEM((2, 125, 8, half), jnp.float32),
            pltpu.VMEM((2, 2, 15, 8, half), jnp.float32),
            pltpu.VMEM((2, 15, 8, half), jnp.float32),
            pltpu.VMEM((scattered + 2, 2, 125, 8, half), jnp.float32),
            pltpu.VMEM((2, 125, 8, half), jnp.float32),
            pltpu.VMEM((2 * pitch, half), jnp.float32),
            pltpu.VMEM((2, 2 * pitch, half), jnp.float32),
            pltpu.VMEM((64, half), jnp.float32),
            pltpu.VMEM((1 << scattered, 4, half), jnp.float32),
            *[pltpu.SemaphoreType.DMA] * 4,
            *(swaps if middle else []),
        ],
        compiler_params=pltpu.CompilerParams(
            collective_id=0, has_side_effects=True, vmem_limit_bytes=20 << 20
        ),
    )(pltpu.with_memory_space_constraint(samples, pltpu.HBM))
    return values * norm


def solution(mesh):
    return jax.shard_map(
        shards,
        mesh=mesh,
        in_specs=(P(None, "inline", "xline"),),
        out_specs=P(None, ("inline", "xline")),
        check_vma=False,
    )
```
